128 devices in a mesh: ctx: 32 (over y_lo, x, z), exp: 4 (over y_hi, core).
Axes of the slice: x: 4, y: 4 (y_hi: 2, y_lo: 2; y = y_hi * 2 + y_lo), z: 4, core: 2. Of those that a mesh axis runs over, the one named last changes fastest.
Arguments:
- hit_features: bfloat16 [16384, 1024], P('ctx'), may hold values from -6 to 6
- norm_attn: float32 [1024], replicated, may hold values from 0.1 to 1.9
- w_query: bfloat16 [1024, 1024], P(None, 'exp'), may hold values from -6 to 6
- w_key: bfloat16 [1024, 1024], P(None, 'exp'), may hold values from -0.1875 to 0.1875
- w_value: bfloat16 [1024, 1024], P(None, 'exp'), may hold values from -0.1875 to 0.1875
- w_out: bfloat16 [1024, 1024], P('exp'), may hold values from -0.1875 to 0.1875
- norm_ffn: float32 [1024], replicated, may hold values from 0.1 to 1.9
- w_router: bfloat16 [1024, 64], replicated, may hold values from -0.1875 to 0.1875
- w_gate: bfloat16 [64, 1024, 2048], P('ctx', None, 'exp'), may hold values from -0.1875 to 0.1875
- w_up: bfloat16 [64, 1024, 2048], P('ctx', None, 'exp'), may hold values from -0.1875 to 0.1875
- w_down: bfloat16 [64, 2048, 1024], P('ctx', 'exp'), may hold values from -0.125 to 0.125
- routes: int32 [16384, 2], P(('ctx', 'exp')), may hold values from 0 to 63, all different within a row; in each aligned block of 128 rows (0 to 127, 128 to 255, ...) at most 8 rows name the same one
Outputs:
- layer_out: bfloat16 [16384, 1024], P(('ctx', 'exp'))
The draws below stay inside these ranges and needn't reach their ends.
Inputs may be any that keep to these rules, and one draw needn't show every extreme that they name: `routes`: each row names 2 different experts; in each aligned block of 128 rows (the rows of one device) no expert is named by more than 8 rows, a bound that some block reaches.
All inputs are finite; a program needn't handle non-finite values.
Results may differ from the reference program's by a relative error of at most 0.013.
The reference program's roundings to bfloat16 on the way (of `normed`, `query_proj`, `key_proj`, `value_proj`, `exp_weights`, `attended`, `normed_ffn` and `hidden`) count: a program that leaves them out, or rounds other values in their place, can miss the bound.
Values may be sent and summed in bfloat16 or wider, within the bound.
A program may use at most 128 MiB of HBM per device.

```python
import math
import jax
import jax.numpy as jnp
import numpy as np
from jax import lax

D = 1024
HEADS = 16
HD = 64
FF = 2048
TOPK = 2
EXPERTS = 64
TOKENS = 16384
ROWS = 128
CAP = 8
N_CTX = 32
N_EXP = 4


def draw_w_query(key, part):
    base = jnp.clip(jax.random.normal(key, (D, HEADS * HD), jnp.float32), -4.0, 4.0) * (3.0 / math.sqrt(D))
    return base.astype(jnp.bfloat16)


def block_levels(own_key, dims, pieces, least, largest):
    gain, own = 1.0, jax.random.fold_in(own_key, 6)
    for dim, parts in pieces:
        steps = jnp.exp(jax.random.uniform(jax.random.fold_in(own, dim), (parts,), jnp.float32, least / len(pieces), largest / len(pieces)))
        gain = gain * jnp.repeat(steps, dims[dim] // parts).reshape([-1 if axis == dim else 1 for axis in range(len(dims))])
    return gain


def shared_out(key, own, number, rows, count, top, reach, slope):
    sequence = jax.random.permutation(key, count)
    crowded, ordinary = load_shares(count, rows * top, reach, slope, True), load_shares(count, rows * top, reach, slope, False)
    places = jnp.arange(count)

    def named(lengths, rotation):
        used = int((lengths > 0).sum())
        fixed = max(1, used // 4)
        passed = fixed + (places - fixed + rotation * (used - fixed)) % max(1, count - fixed)
        return jnp.zeros((count,), jnp.int32).at[sequence[jnp.where(places < fixed, places, passed)]].set(jnp.asarray(lengths, jnp.int32))

    lengths = jnp.where(number % 4 == 0, named(crowded, number // 4), named(ordinary, number - number // 4 - 1))
    mixed = jax.random.permutation(jax.random.fold_in(own, 3), count)
    donor, receiver = mixed[0:count // 2 * 2:2], mixed[1:count // 2 * 2:2]
    slack = jnp.minimum(lengths[donor] - 1, reach - lengths[receiver]) // 2
    slack = jnp.where((donor == sequence[0]) | (receiver == sequence[0]) | (lengths[receiver] == 0), 0, jnp.maximum(slack, 0))
    passed = jax.random.randint(jax.random.fold_in(own, 4), (count // 2,), 0, 1 << 20) % (slack + 1)
    lengths = lengths.at[donor].add(-passed).at[receiver].add(passed)
    items = jnp.searchsorted(jnp.cumsum(lengths), jnp.arange(rows * top), side="right").astype(jnp.int32)
    grid = items.reshape(top, rows).T
    grid = grid[jax.random.permutation(jax.random.fold_in(own, 1), rows)]
    rotation = jax.random.randint(jax.random.fold_in(own, 2), (rows, 1), 0, top)
    return jnp.take_along_axis(grid, (jnp.arange(top)[None, :] + rotation) % top, axis=1)


def load_shares(count, total, most, skew, full):
    portions = [(1 << 20) // math.isqrt(standing ** skew) + 1 for standing in range(1, count + 1)]
    largest = most if full else min(most, max(-(-total // count), total * portions[0] // sum(portions)))
    least = 1 if total - largest >= count - 1 else 0
    counts, spare = [largest] + [least] * (count - 1), total - largest - least * (count - 1)
    while spare > 0:
        movable = [i for i in range(1, count) if counts[i] < largest] or [i for i in range(1, count) if counts[i] < most]
        whole, remaining = sum([portions[i] for i in movable]), spare
        for i in movable:
            extra = min(most - counts[i], max(1, remaining * portions[i] // whole), spare)
            counts[i] = counts[i] + extra
            spare = spare - extra
    return np.array(counts)


def scatter_about(own_key, shape, spread, reach, split=(), kind=jnp.bfloat16):
    result = jax.random.normal(own_key, shape, jnp.float32) * spread
    if len(split) > 0:
        result = block_levels(own_key, shape, split, -0.22, 0.18) * result
    return jnp.clip(result, min=-reach, max=reach).astype(kind)


def setup_inputs(seed: int = 0) -> dict:
    splits = jax.random.split(jax.random.key(seed), 13)
    hit_features = scatter_about(splits[0], (TOKENS, D), 1.0, 6.0, ((0, 32),))
    norm_attn = jnp.clip(1.0 + 0.18 * jax.random.normal(splits[1], (D,), jnp.float32), 0.1, 1.9)
    w_query = draw_w_query(jax.random.fold_in(splits[12], 71), 0)
    w_key = scatter_about(splits[3], (D, HEADS * HD), D ** -0.5, 0.1875, ((1, 4),))
    w_value = scatter_about(splits[4], (D, HEADS * HD), D ** -0.5, 0.1875, ((1, 4),))
    w_out = scatter_about(splits[5], (HEADS * HD, D), (HEADS * HD) ** -0.5, 0.1875, ((0, 4),))
    norm_ffn = jnp.clip(1.0 + 0.18 * jax.random.normal(splits[6], (D,), jnp.float32), 0.1, 1.9)
    w_router = scatter_about(splits[7], (D, EXPERTS), D ** -0.5, 0.1875)
    w_gate = scatter_about(splits[8], (EXPERTS, D, FF), D ** -0.5, 0.1875, ((0, 32), (2, 4)))
    w_up = scatter_about(splits[9], (EXPERTS, D, FF), D ** -0.5, 0.1875, ((0, 32), (2, 4)))
    w_down = scatter_about(splits[10], (EXPERTS, FF, D), FF ** -0.5, 0.125, ((0, 32), (1, 4)))
    routes_keys = jax.random.split(jax.random.fold_in(splits[11], 1), TOKENS // ROWS)
    routes_turns = jax.random.permutation(jax.random.fold_in(splits[11], 3), TOKENS // ROWS)
    routes = jax.vmap(lambda own, number: shared_out(jax.random.fold_in(splits[11], 2), own, number, ROWS, EXPERTS, TOPK, CAP, 2))(routes_keys, routes_turns).reshape((TOKENS, TOPK))
    return dict(hit_features=hit_features, norm_attn=norm_attn, w_query=w_query, w_key=w_key, w_value=w_value, w_out=w_out, norm_ffn=norm_ffn, w_router=w_router, w_gate=w_gate, w_up=w_up, w_down=w_down, routes=routes)


def rms_norm(row_block, gain_vec):
    values = row_block.astype(jnp.float32)
    inv_rms = lax.rsqrt(lax.optimization_barrier(jnp.mean(values * values, axis=-1, keepdims=True)) + 1e-05)
    return (values * inv_rms * gain_vec.astype(jnp.float32)).astype(jnp.bfloat16)

def reference(hit_features, norm_attn, w_query, w_key, w_value, w_out, norm_ffn, w_router, w_gate, w_up, w_down, routes):
    normed = rms_norm(hit_features, norm_attn)
    query_proj = lax.optimization_barrier(jnp.dot(normed, w_query, preferred_element_type=jnp.float32).astype(jnp.bfloat16))
    key_proj = lax.optimization_barrier(jnp.dot(normed, w_key, preferred_element_type=jnp.float32).astype(jnp.bfloat16))
    value_proj = lax.optimization_barrier(jnp.dot(normed, w_value, preferred_element_type=jnp.float32).astype(jnp.bfloat16))
    key_float = key_proj.astype(jnp.float32).reshape(TOKENS, HEADS, HD)
    value_float = value_proj.astype(jnp.float32).reshape(TOKENS, HEADS, HD)
    query_three = query_proj.reshape(TOKENS, HEADS, HD)
    block_rows = math.gcd(TOKENS, 128)

    def one_block(start):
        query_block = lax.dynamic_slice_in_dim(query_three, start, block_rows, 0).astype(jnp.float32)
        scores = jnp.einsum('qhd,khd->hqk', query_block, key_float) * (1.0 / math.sqrt(HD))
        top_score = lax.optimization_barrier(jnp.max(scores, axis=-1, keepdims=True))
        exp_scores = jnp.exp(scores - top_score)
        denominator = lax.optimization_barrier(jnp.sum(exp_scores, axis=-1, keepdims=True))
        exp_weights = lax.optimization_barrier(exp_scores.astype(jnp.bfloat16)).astype(jnp.float32)
        weighted = jnp.einsum('hqk,khd->qhd', exp_weights, value_float)
        return (weighted / jnp.transpose(denominator, (1, 0, 2))).astype(jnp.bfloat16)
    starts = jnp.arange(TOKENS // block_rows, dtype=jnp.int32) * block_rows
    attended = lax.map(one_block, starts).reshape(TOKENS, HEADS * HD)
    residual = hit_features.astype(jnp.float32) + jnp.dot(attended, w_out, preferred_element_type=jnp.float32)
    normed_ffn = rms_norm(residual, norm_ffn)
    logits = jnp.dot(normed_ffn, w_router, preferred_element_type=jnp.float32)
    picks = routes[:, :, None] == jnp.arange(EXPERTS, dtype=jnp.int32)[None, None, :]
    chosen = lax.optimization_barrier(jnp.sum(jnp.where(picks, logits[:, None, :], jnp.zeros_like(logits[:, None, :])), axis=-1))
    gates = jax.nn.softmax(chosen, axis=-1)
    devices = N_CTX * N_EXP
    one_hot = picks.reshape(devices, ROWS * TOPK, EXPERTS).astype(jnp.int32)
    earlier = jnp.cumsum(one_hot, axis=1) - one_hot
    slots = lax.optimization_barrier(jnp.sum(earlier * one_hot, axis=-1))
    depth = devices * CAP
    position = slots + (jnp.arange(devices, dtype=jnp.int32) * CAP)[:, None]
    target = (routes.reshape(devices, ROWS * TOPK) * depth + position).reshape(-1).astype(jnp.int32)
    buffers = jnp.zeros((EXPERTS * depth, D), jnp.bfloat16).at[target].set(jnp.repeat(normed_ffn, TOPK, axis=0))
    stacked = buffers.reshape(EXPERTS, depth, D)

    def one_expert(operands):
        row_block, gate_mat, up_mat, down_mat = operands
        gate_act = jnp.dot(row_block, gate_mat, preferred_element_type=jnp.float32)
        up_act = jnp.dot(row_block, up_mat, preferred_element_type=jnp.float32)
        hidden = (jax.nn.silu(gate_act) * up_act).astype(jnp.bfloat16)
        return jnp.dot(hidden, down_mat, preferred_element_type=jnp.float32)
    outputs = lax.map(one_expert, (stacked, w_gate, w_up, w_down)).reshape(EXPERTS * depth, D)
    picked = jnp.take(outputs, target, axis=0).reshape(TOKENS, TOPK, D)
    mixture = lax.optimization_barrier(jnp.sum(gates[:, :, None] * picked, axis=1))
    return (residual + mixture).astype(jnp.bfloat16)
```

```python
import functools
import math

import jax
import jax.numpy as jnp
from jax import lax
from jax.experimental import pallas as pl
from jax.experimental.pallas import tpu as pltpu
from jax.sharding import PartitionSpec as P

D = 1024
HD = 64
EPSILON = 1e-05
LOWEST = -1e30
ALPHA = math.log2(math.e) / math.sqrt(HD)
BF = jnp.bfloat16
F32 = jnp.float32
MESH = pl.DeviceIdType.MESH
VMEM = pltpu.VMEM


def whole():
    return pl.BlockSpec(memory_space=pltpu.VMEM)


def anywhere():
    return pl.BlockSpec(memory_space=pl.ANY)


def project_kernel(x_ref, gain_ref, wq_ref, wk_ref, wv_ref, qt_ref, kp_ref, vt_ref):
    x = x_ref[...].astype(F32)
    inv = lax.rsqrt(jnp.mean(x * x, axis=-1, keepdims=True) + EPSILON)
    n = (x * inv * gain_ref[...]).astype(BF)
    q = jnp.dot(n, wq_ref[...], preferred_element_type=F32)
    qt = q.T.astype(BF)
    for head in range(4):
        for block in range(4):
            qt_ref[block % 2, head, :, (block // 2) * 128 : (block // 2) * 128 + 128] = qt[
                head * HD : head * HD + HD, block * 128 : block * 128 + 128
            ]
    k = jnp.dot(n, wk_ref[...], preferred_element_type=F32)
    for head in range(4):
        for half in range(2):
            kh = k[half * 256 : half * 256 + 256, head * HD : head * HD + HD]
            kp_ref[head, half] = jnp.concatenate([kh[0:128], kh[128:256]], axis=1).astype(BF)
    vt = jnp.dot(n, wv_ref[...], preferred_element_type=F32).T.astype(BF)
    for head in range(4):
        for half in range(2):
            for u in range(2):
                at = half * 256 + u * 128
                vt_ref[head, half, u] = vt[head * HD : head * HD + HD, at : at + 128]


def project(x, gain, wq, wk, wv):
    return pl.pallas_call(
        project_kernel,
        out_shape=(
            jax.ShapeDtypeStruct((2, 4, HD, 256), BF),
            jax.ShapeDtypeStruct((4, 2, 128, 128), BF),
            jax.ShapeDtypeStruct((4, 2, 2, HD, 128), BF),
        ),
        in_specs=[whole()] * 5,
        out_specs=(whole(), whole(), whole()),
        name="project",
    )(x, gain.reshape(1, D), wq, wk, wv)


def attention_kernel(
    qt_ref,
    kp_ref,
    vt_ref,
    wo_ref,
    at_ref,
    wo_all_ref,
    qg,
    kg,
    vg,
    q2,
    s_ref,
    acc,
    mx,
    ls,
    ost,
    x_send,
    x_recv,
    ring_send,
    ring_recv,
    sib_send,
    sib_recv,
    o_send,
    o_recv,
    w_send,
    w_recv,
    w_own,
):
    ctx = lax.axis_index("ctx")
    exp = lax.axis_index("exp")
    ylo = ctx // 16
    x = (ctx // 4) % 4
    z = ctx % 4
    yhi = exp // 2
    core = exp % 2
    mine = ylo * 4 + z

    def device(to_ylo, to_x, to_z, to_yhi, to_core):
        return (to_ylo * 16 + to_x * 4 + to_z, to_yhi * 2 + to_core)

    right = device(ylo, (x + 1) % 4, z, yhi, core)
    left = device(ylo, (x + 3) % 4, z, yhi, core)
    sibling = device(ylo, x, z, yhi, 1 - core)

    barrier = pltpu.get_barrier_semaphore()

    def greet(i, carry):
        to = device(i // 16, x, (i // 4) % 4, (i // 2) % 2, i % 2)

        @pl.when(i != ylo * 16 + z * 4 + yhi * 2 + core)
        def _():
            pl.semaphore_signal(barrier, inc=1, device_id=to, device_id_type=MESH)

        return carry

    lax.fori_loop(0, 32, greet, 0)
    pl.semaphore_signal(barrier, inc=1, device_id=right, device_id_type=MESH)
    pl.semaphore_signal(barrier, inc=1, device_id=left, device_id_type=MESH)
    pl.semaphore_wait(barrier, 33)

    def head_copies(i):
        head, half = i // 2, i % 2
        to = device(core, x, head, yhi, half)
        parts = (
            (qt_ref.at[half, head], qg.at[mine]),
            (kp_ref.at[head, half], kg.at[0, half, pl.ds(pl.multiple_of(mine * 128, 128), 128), :]),
            (
                vt_ref.at[head, half],
                vg.at[0, half, :, :, pl.ds(pl.multiple_of(mine * 128, 128), 128)],
            ),
        )
        own = (core == ylo) & (head == z) & (half == core)
        remote = [
            pltpu.make_async_remote_copy(
                src_ref=src,
                dst_ref=dst,
                send_sem=x_send.at[n, i],
                recv_sem=x_recv.at[n, mine],
                device_id=to,
                device_id_type=MESH,
            )
            for n, (src, dst) in enumerate(parts)
        ]
        local = [
            pltpu.make_async_copy(src, dst, x_recv.at[n, mine])
            for n, (src, dst) in enumerate(parts)
        ]
        return own, remote, local

    def send_heads(i, carry):
        own, remote, local = head_copies(i)

        @pl.when(own)
        def _():
            for copy in local:
                copy.start()

        @pl.when(jnp.logical_not(own))
        def _():
            for copy in remote:
                copy.start()

        return carry

    lax.fori_loop(0, 8, send_heads, 0)

    def await_heads(j, carry):
        pltpu.make_async_copy(qg.at[j], qg.at[j], x_recv.at[0, j]).wait()
        at = pl.ds(pl.multiple_of(j * 128, 128), 128)
        kd = kg.at[0, core, at, :]
        pltpu.make_async_copy(kd, kd, x_recv.at[1, j]).wait()
        vd = vg.at[0, core, :, :, at]
        pltpu.make_async_copy(vd, vd, x_recv.at[2, j]).wait()
        return carry

    lax.fori_loop(0, 8, await_heads, 0)

    def remote(src, dst, send, recv, to):
        return pltpu.make_async_remote_copy(
            src_ref=src,
            dst_ref=dst,
            send_sem=send,
            recv_sem=recv,
            device_id=to,
            device_id_type=MESH,
        )

    def to_sibling(slot):
        return [
            remote(g.at[slot, core], g.at[slot, core], sib_send.at[n, slot], sib_recv.at[n, slot], sibling)
            for n, g in enumerate((kg, vg))
        ]

    def from_sibling(slot):
        return [
            remote(g.at[slot, 1 - core], g.at[slot, 1 - core], sib_send.at[n, slot], sib_recv.at[n, slot], sibling)
            for n, g in enumerate((kg, vg))
        ]

    k_right = remote(kg.at[0, core], kg.at[1, core], ring_send.at[0, 0], ring_recv.at[0, 0], right)
    v_right = remote(vg.at[0, core], vg.at[1, core], ring_send.at[1, 0], ring_recv.at[1, 0], right)
    k_left = remote(kg.at[0, core], kg.at[2, core], ring_send.at[0, 1], ring_recv.at[0, 1], left)
    v_left = remote(vg.at[0, core], vg.at[2, core], ring_send.at[1, 1], ring_recv.at[1, 1], left)
    k_on = remote(kg.at[1, core], kg.at[3, core], ring_send.at[0, 2], ring_recv.at[0, 2], right)
    v_on = remote(vg.at[2, core], vg.at[3, core], ring_send.at[1, 2], ring_recv.at[1, 2], left)
    for copy in (k_right, k_left, v_right, v_left):
        copy.start()
    for copy in to_sibling(0):
        copy.start()

    w_copies = [
        remote(
            wo_ref,
            wo_all_ref.at[exp],
            w_send.at[step - 1],
            w_recv.at[step - 1],
            (ctx, (exp + step) % 4),
        )
        for step in range(1, 4)
    ]
    w_local = pltpu.make_async_copy(wo_ref, wo_all_ref.at[exp], w_own)
    for copy in w_copies:
        copy.start()
    w_local.start()

    zero = jnp.zeros((HD, 256), BF)
    for j in range(8):
        q2[j, 0, 0:HD] = qg[j]
        q2[j, 0, HD : 2 * HD] = zero
        q2[j, 1, 0:HD] = zero
        q2[j, 1, HD : 2 * HD] = qg[j]
    acc[...] = jnp.zeros_like(acc)
    mx[...] = jnp.full_like(mx, LOWEST)
    ls[...] = jnp.zeros_like(ls)

    def score(phase, j, p):
        keys = kg[phase // 2, (phase + core) % 2]
        for u in range(2):
            s_ref[p, u] = lax.dot_general(
                keys, q2[j, u], (((1,), (0,)), ((), ())), preferred_element_type=F32
            )

    def absorb(phase, j, p):
        s0 = s_ref[p, 0]
        s1 = s_ref[p, 1]
        old = mx[j]
        new = jnp.maximum(
            old,
            jnp.maximum(jnp.max(s0, axis=0, keepdims=True), jnp.max(s1, axis=0, keepdims=True)),
        )
        fade = jnp.exp2((old - new) * ALPHA)
        e0 = jnp.exp2((s0 - new) * ALPHA)
        e1 = jnp.exp2((s1 - new) * ALPHA)
        slot, half = phase // 2, (phase + core) % 2
        ls[j] = ls[j] * fade + (
            jnp.sum(e0, axis=0, keepdims=True) + jnp.sum(e1, axis=0, keepdims=True)
        )
        acc[j] = acc[j] * fade + (
            jnp.dot(vg[slot, half, 0], e0.astype(BF), preferred_element_type=F32)
            + jnp.dot(vg[slot, half, 1], e1.astype(BF), preferred_element_type=F32)
        )
        mx[j] = new

    score(0, 0, 0)

    def turn(g, carry):
        phase, pair = g // 4, g % 4
        last = pair == 3

        for slot in (0, 1, 2, 3):

            @pl.when(last & (phase == 2 * slot))
            def _(slot=slot):
                for copy in from_sibling(slot):
                    copy.wait_recv()

        @pl.when(last & (phase == 1))
        def _():
            for copy in (k_right, k_left, v_right, v_left):
                copy.wait_recv()
            k_on.start()
            v_on.start()
            for slot in (1, 2):
                for copy in to_sibling(slot):
                    copy.start()

        @pl.when(last & (phase == 5))
        def _():
            k_on.wait_recv()
            v_on.wait_recv()
            for copy in to_sibling(3):
                copy.start()

        score(phase, 2 * pair + 1, 1)
        absorb(phase, 2 * pair, 0)
        later = jnp.minimum(g + 1, 31)
        score(later // 4, 2 * (later % 4), 0)
        absorb(phase, 2 * pair + 1, 1)
        return carry

    lax.fori_loop(0, 32, turn, 0)

    for j in range(8):
        o = (acc[j] / ls[j]).astype(BF)
        ost[j, 0] = o[:, 0:128]
        ost[j, 1] = o[:, 128:256]

    head = yhi * 8 + mine

    def out_copy(i):
        j, to_yhi = i % 8, i // 8
        to = device(j // 4, x, j % 4, to_yhi, core)
        return (
            remote(ost.at[j, to_yhi], at_ref.at[head], o_send.at[i], o_recv.at[head], to),
            pltpu.make_async_copy(ost.at[j, to_yhi], at_ref.at[head], o_recv.at[head]),
        )

    def send_out(i, carry):
        away, local = out_copy(i)

        @pl.when(i == head)
        def _():
            local.start()

        @pl.when(i != head)
        def _():
            away.start()

        return carry

    lax.fori_loop(0, 16, send_out, 0)

    def await_out(i, carry):
        pltpu.make_async_copy(at_ref.at[i], at_ref.at[i], o_recv.at[i]).wait()
        return carry

    lax.fori_loop(0, 16, await_out, 0)

    def sent_heads(i, carry):
        own, away, local = head_copies(i)

        @pl.when(jnp.logical_not(own))
        def _():
            for copy in away:
                copy.wait_send()

        return carry

    lax.fori_loop(0, 8, sent_heads, 0)

    def sent_out(i, carry):
        away, local = out_copy(i)

        @pl.when(i != head)
        def _():
            away.wait_send()

        return carry

    lax.fori_loop(0, 16, sent_out, 0)
    for copy in (k_right, k_left, v_right, v_left, k_on, v_on):
        copy.wait_send()
    for slot in range(4):
        for copy in to_sibling(slot):
            copy.wait_send()
    w_local.wait()
    for copy in w_copies:
        copy.wait_send()
    for step in range(1, 4):
        slot = (exp + 4 - step) % 4
        remote(
            wo_ref,
            wo_all_ref.at[slot],
            w_send.at[step - 1],
            w_recv.at[step - 1],
            (ctx, slot),
        ).wait_recv()


def attention(qt, kp, vt, wo):
    return pl.pallas_call(
        attention_kernel,
        out_shape=(
            jax.ShapeDtypeStruct((16, HD, 128), BF),
            jax.ShapeDtypeStruct((4, 256, D), BF),
        ),
        in_specs=[whole(), whole(), whole(), anywhere()],
        out_specs=(anywhere(), anywhere()),
        scratch_shapes=[
            VMEM((8, HD, 256), BF),
            VMEM((4, 2, 1024, 128), BF),
            VMEM((4, 2, 2, HD, 1024), BF),
            VMEM((8, 2, 128, 256), BF),
            VMEM((2, 2, 1024, 256), F32),
            VMEM((8, HD, 256), F32),
            VMEM((8, 1, 256), F32),
            VMEM((8, 1, 256), F32),
            VMEM((8, 2, HD, 128), BF),
            pltpu.SemaphoreType.DMA((3, 8)),
            pltpu.SemaphoreType.DMA((3, 8)),
            pltpu.SemaphoreType.DMA((2, 3)),
            pltpu.SemaphoreType.DMA((2, 3)),
            pltpu.SemaphoreType.DMA((2, 4)),
            pltpu.SemaphoreType.DMA((2, 4)),
            pltpu.SemaphoreType.DMA((16,)),
            pltpu.SemaphoreType.DMA((16,)),
            pltpu.SemaphoreType.DMA((3,)),
            pltpu.SemaphoreType.DMA((3,)),
            pltpu.SemaphoreType.DMA,
        ],
        compiler_params=pltpu.CompilerParams(
            collective_id=0, has_side_effects=True, vmem_limit_bytes=40 << 20
        ),
        name="attention",
    )(qt, kp, vt, wo)


def route_kernel(at_ref, wo_ref, hit_ref, gain_ref, wr_ref, routes_ref, res_ref, out_ref, hi_ref, lo_ref):
    mixed = lax.dot_general(
        at_ref[...], wo_ref[...], (((0,), (0,)), ((), ())), preferred_element_type=F32
    )
    residual = hit_ref[...].astype(F32) + mixed
    res_ref[...] = residual
    inv = lax.rsqrt(jnp.mean(residual * residual, axis=-1, keepdims=True) + EPSILON)
    normed = (residual * inv * gain_ref[...]).astype(BF)
    logits = jnp.dot(normed, wr_ref[...], preferred_element_type=F32)
    rows, experts = logits.shape
    ids = lax.broadcasted_iota(jnp.int32, (rows, experts), 1)
    picks = (routes_ref[:, 0:1] == ids) | (routes_ref[:, 1:2] == ids)
    top = jnp.max(jnp.where(picks, logits, -jnp.inf), axis=-1, keepdims=True)
    weights = jnp.where(picks, jnp.exp(jnp.where(picks, logits - top, 0.0)), 0.0)
    gates = weights / jnp.sum(weights, axis=-1, keepdims=True)
    gate_hi = gates.astype(BF)
    gate_lo = (gates - gate_hi.astype(F32)).astype(BF)
    marks = jnp.where(picks, 1.0, 0.0).astype(BF)
    before = lax.broadcasted_iota(jnp.int32, (rows, rows), 0) > lax.broadcasted_iota(
        jnp.int32, (rows, rows), 1
    )
    slots = jnp.dot(
        jnp.where(before, 1.0, 0.0).astype(BF), marks, preferred_element_type=F32
    ).astype(BF)
    places = out_ref.shape[0]
    cap = places // experts
    spread = jnp.where(
        lax.broadcasted_iota(jnp.int32, (experts, places), 1) // cap
        == lax.broadcasted_iota(jnp.int32, (experts, places), 0),
        1.0,
        0.0,
    ).astype(BF)
    wide = lambda v: jnp.dot(v, spread, preferred_element_type=F32)
    order = (lax.broadcasted_iota(jnp.int32, (rows, places), 1) % cap).astype(F32)
    here = (wide(marks) > 0.5) & (wide(slots) == order)
    table = jnp.where(here, 1.0, 0.0).astype(BF)
    out_ref[...] = lax.dot_general(
        table, normed, (((0,), (0,)), ((), ())), preferred_element_type=F32
    ).astype(BF)
    hi_ref[...] = jnp.where(here, wide(gate_hi), 0.0).astype(BF)
    lo_ref[...] = jnp.where(here, wide(gate_lo), 0.0).astype(BF)


def route(at, wo, hit, gain, wr, routes):
    rows = hit.shape[0]
    places = wr.shape[1] * 8
    return pl.pallas_call(
        route_kernel,
        out_shape=(
            jax.ShapeDtypeStruct((rows, D), F32),
            jax.ShapeDtypeStruct((places, D), BF),
            jax.ShapeDtypeStruct((rows, places), BF),
            jax.ShapeDtypeStruct((rows, places), BF),
        ),
        in_specs=[whole()] * 6,
        out_specs=(whole(),) * 4,
        name="route",
    )(at, wo, hit, gain.reshape(1, D), wr, routes)


def combine_kernel(res_ref, hi_ref, lo_ref, back_ref, out_ref):
    back = back_ref[...]
    mixture = jnp.dot(hi_ref[...], back, preferred_element_type=F32) + jnp.dot(
        lo_ref[...], back, preferred_element_type=F32
    )
    out_ref[...] = (res_ref[...] + mixture).astype(BF)


def run_experts(received, gate_mats, up_mats, down_mats):
    gate_act = jnp.einsum("sjcd,jdf->sjcf", received, gate_mats, preferred_element_type=F32)
    up_act = jnp.einsum("sjcd,jdf->sjcf", received, up_mats, preferred_element_type=F32)
    hidden = (jax.nn.silu(gate_act) * up_act).astype(BF)
    return jnp.einsum("sjcf,jfd->sjcd", hidden, down_mats, preferred_element_type=F32)


def body(
    hit_features,
    norm_attn,
    w_query,
    w_key,
    w_value,
    w_out,
    norm_ffn,
    w_router,
    w_gate,
    w_up,
    w_down,
    routes,
):
    ctx_count = lax.axis_size("ctx")
    exp_count = lax.axis_size("exp")
    rows_dev = hit_features.shape[0] // exp_count
    qt, kp, vt = project(hit_features, norm_attn, w_query, w_key, w_value)
    at, wo = attention(qt, kp, vt, w_out)
    own_rows = lax.dynamic_slice_in_dim(
        hit_features, lax.axis_index("exp") * rows_dev, rows_dev, 0
    )
    residual, outgoing, gate_hi, gate_lo = route(
        at.reshape(D, rows_dev), wo.reshape(D, D), own_rows, norm_ffn, w_router, routes
    )
    local_experts = w_gate.shape[0]
    grid = outgoing.reshape(ctx_count, local_experts, -1, D)
    copies = jnp.broadcast_to(grid[:, None], (ctx_count, exp_count) + grid.shape[1:]).reshape(
        (ctx_count * exp_count,) + grid.shape[1:]
    )
    produced = run_experts(
        lax.all_to_all(copies, ("ctx", "exp"), split_axis=0, concat_axis=0, tiled=True),
        w_gate,
        w_up,
        w_down,
    )
    returned = lax.all_to_all(
        produced.astype(BF), ("ctx", "exp"), split_axis=0, concat_axis=0, tiled=True
    ).astype(F32)
    combined = jnp.sum(returned.reshape((ctx_count, exp_count) + grid.shape[1:]), axis=1)
    return pl.pallas_call(
        combine_kernel,
        out_shape=jax.ShapeDtypeStruct((rows_dev, D), BF),
        in_specs=[whole()] * 4,
        out_specs=whole(),
        name="combine",
    )(residual, gate_hi, gate_lo, combined.reshape(outgoing.shape).astype(BF))


def solution(mesh):
    return jax.shard_map(
        body,
        mesh=mesh,
        in_specs=(
            P("ctx", None),
            P(),
            P(None, "exp"),
            P(None, "exp"),
            P(None, "exp"),
            P("exp", None),
            P(),
            P(),
            P("ctx", None, "exp"),
            P("ctx", None, "exp"),
            P("ctx", "exp", None),
            P(("ctx", "exp"), None),
        ),
        out_specs=P(("ctx", "exp"), None),
        check_vma=False,
    )
```

```python
import functools
import math

import jax
import jax.numpy as jnp
from jax import lax
from jax.experimental import pallas as pl
from jax.experimental.pallas import tpu as pltpu
from jax.sharding import PartitionSpec as P

D = 1024
HD = 64
EPSILON = 1e-05
LOWEST = -1e30
ALPHA = math.log2(math.e) / math.sqrt(HD)
BF = jnp.bfloat16
F32 = jnp.float32
MESH = pl.DeviceIdType.MESH
VMEM = pltpu.VMEM


def whole():
    return pl.BlockSpec(memory_space=pltpu.VMEM)


def anywhere():
    return pl.BlockSpec(memory_space=pl.ANY)


def project_kernel(x_ref, gain_ref, wq_ref, wk_ref, wv_ref, qt_ref, kp_ref, vt_ref):
    x = x_ref[...].astype(F32)
    inv = lax.rsqrt(jnp.mean(x * x, axis=-1, keepdims=True) + EPSILON)
    n = (x * inv * gain_ref[...]).astype(BF)
    q = jnp.dot(n, wq_ref[...], preferred_element_type=F32)
    qt = q.T.astype(BF)
    for head in range(4):
        for block in range(4):
            qt_ref[block % 2, head, :, (block // 2) * 128 : (block // 2) * 128 + 128] = qt[
                head * HD : head * HD + HD, block * 128 : block * 128 + 128
            ]
    k = jnp.dot(n, wk_ref[...], preferred_element_type=F32)
    for head in range(4):
        for half in range(2):
            kh = k[half * 256 : half * 256 + 256, head * HD : head * HD + HD]
            kp_ref[head, half] = jnp.concatenate([kh[0:128], kh[128:256]], axis=1).astype(BF)
    vt = jnp.dot(n, wv_ref[...], preferred_element_type=F32).T.astype(BF)
    for head in range(4):
        for half in range(2):
            for u in range(2):
                at = half * 256 + u * 128
                vt_ref[head, half, u] = vt[head * HD : head * HD + HD, at : at + 128]


def project(x, gain, wq, wk, wv):
    return pl.pallas_call(
        project_kernel,
        out_shape=(
            jax.ShapeDtypeStruct((2, 4, HD, 256), BF),
            jax.ShapeDtypeStruct((4, 2, 128, 128), BF),
            jax.ShapeDtypeStruct((4, 2, 2, HD, 128), BF),
        ),
        in_specs=[whole()] * 5,
        out_specs=(whole(), whole(), whole()),
        name="project",
    )(x, gain.reshape(1, D), wq, wk, wv)


def attention_kernel(
    qt_ref,
    kp_ref,
    vt_ref,
    wo_ref,
    at_ref,
    wo_all_ref,
    qg,
    kg,
    vg,
    q2,
    s_ref,
    acc,
    mx,
    ls,
    ost,
    x_send,
    x_recv,
    ring_send,
    ring_recv,
    sib_send,
    sib_recv,
    o_send,
    o_recv,
    w_send,
    w_recv,
    w_own,
):
    ctx = lax.axis_index("ctx")
    exp = lax.axis_index("exp")
    ylo = ctx // 16
    x = (ctx // 4) % 4
    z = ctx % 4
    yhi = exp // 2
    core = exp % 2
    mine = ylo * 4 + z

    def device(to_ylo, to_x, to_z, to_yhi, to_core):
        return (to_ylo * 16 + to_x * 4 + to_z, to_yhi * 2 + to_core)

    right = device(ylo, (x + 1) % 4, z, yhi, core)
    left = device(ylo, (x + 3) % 4, z, yhi, core)
    sibling = device(ylo, x, z, yhi, 1 - core)

    barrier = pltpu.get_barrier_semaphore()

    def greet(i, carry):
        to = device(i // 16, x, (i // 4) % 4, (i // 2) % 2, i % 2)

        @pl.when(i != ylo * 16 + z * 4 + yhi * 2 + core)
        def _():
            pl.semaphore_signal(barrier, inc=1, device_id=to, device_id_type=MESH)

        return carry

    lax.fori_loop(0, 32, greet, 0)
    pl.semaphore_signal(barrier, inc=1, device_id=right, device_id_type=MESH)
    pl.semaphore_signal(barrier, inc=1, device_id=left, device_id_type=MESH)
    pl.semaphore_wait(barrier, 33)

    def head_copies(i):
        head, half = i // 2, i % 2
        to = device(core, x, head, yhi, half)
        parts = (
            (qt_ref.at[half, head], qg.at[mine]),
            (kp_ref.at[head, half], kg.at[0, half, pl.ds(pl.multiple_of(mine * 128, 128), 128), :]),
            (
                vt_ref.at[head, half],
                vg.at[0, half, :, :, pl.ds(pl.multiple_of(mine * 128, 128), 128)],
            ),
        )
        own = (core == ylo) & (head == z) & (half == core)
        remote = [
            pltpu.make_async_remote_copy(
                src_ref=src,
                dst_ref=dst,
                send_sem=x_send.at[n, i],
                recv_sem=x_recv.at[n, mine],
                device_id=to,
                device_id_type=MESH,
            )
            for n, (src, dst) in enumerate(parts)
        ]
        local = [
            pltpu.make_async_copy(src, dst, x_recv.at[n, mine])
            for n, (src, dst) in enumerate(parts)
        ]
        return own, remote, local

    def send_heads(i, carry):
        own, remote, local = head_copies(i)

        @pl.when(own)
        def _():
            for copy in local:
                copy.start()

        @pl.when(jnp.logical_not(own))
        def _():
            for copy in remote:
                copy.start()

        return carry

    lax.fori_loop(0, 8, send_heads, 0)

    def await_heads(j, carry):
        pltpu.make_async_copy(qg.at[j], qg.at[j], x_recv.at[0, j]).wait()
        at = pl.ds(pl.multiple_of(j * 128, 128), 128)
        kd = kg.at[0, core, at, :]
        pltpu.make_async_copy(kd, kd, x_recv.at[1, j]).wait()
        vd = vg.at[0, core, :, :, at]
        pltpu.make_async_copy(vd, vd, x_recv.at[2, j]).wait()
        return carry

    lax.fori_loop(0, 8, await_heads, 0)

    def remote(src, dst, send, recv, to):
        return pltpu.make_async_remote_copy(
            src_ref=src,
            dst_ref=dst,
            send_sem=send,
            recv_sem=recv,
            device_id=to,
            device_id_type=MESH,
        )

    def to_sibling(slot):
        return [
            remote(g.at[slot, core], g.at[slot, core], sib_send.at[n, slot], sib_recv.at[n, slot], sibling)
            for n, g in enumerate((kg, vg))
        ]

    def from_sibling(slot):
        return [
            remote(g.at[slot, 1 - core], g.at[slot, 1 - core], sib_send.at[n, slot], sib_recv.at[n, slot], sibling)
            for n, g in enumerate((kg, vg))
        ]

    k_right = remote(kg.at[0, core], kg.at[1, core], ring_send.at[0, 0], ring_recv.at[0, 0], right)
    v_right = remote(vg.at[0, core], vg.at[1, core], ring_send.at[1, 0], ring_recv.at[1, 0], right)
    k_left = remote(kg.at[0, core], kg.at[2, core], ring_send.at[0, 1], ring_recv.at[0, 1], left)
    v_left = remote(vg.at[0, core], vg.at[2, core], ring_send.at[1, 1], ring_recv.at[1, 1], left)
    k_on = remote(kg.at[1, core], kg.at[3, core], ring_send.at[0, 2], ring_recv.at[0, 2], right)
    v_on = remote(vg.at[2, core], vg.at[3, core], ring_send.at[1, 2], ring_recv.at[1, 2], left)
    for copy in (k_right, k_left, v_right, v_left):
        copy.start()
    for copy in to_sibling(0):
        copy.start()

    w_copies = [
        remote(
            wo_ref,
            wo_all_ref.at[exp],
            w_send.at[step - 1],
            w_recv.at[step - 1],
            (ctx, (exp + step) % 4),
        )
        for step in range(1, 4)
    ]
    w_local = pltpu.make_async_copy(wo_ref, wo_all_ref.at[exp], w_own)
    for copy in w_copies:
        copy.start()
    w_local.start()

    zero = jnp.zeros((HD, 256), BF)
    for j in range(8):
        q2[j, 0, 0:HD] = qg[j]
        q2[j, 0, HD : 2 * HD] = zero
        q2[j, 1, 0:HD] = zero
        q2[j, 1, HD : 2 * HD] = qg[j]
    acc[...] = jnp.zeros_like(acc)
    mx[...] = jnp.full_like(mx, LOWEST)
    ls[...] = jnp.zeros_like(ls)

    def score(phase, j, p):
        keys = kg[phase // 2, (phase + core) % 2]
        for u in range(2):
            s_ref[p, u] = lax.dot_general(
                keys, q2[j, u], (((1,), (0,)), ((), ())), preferred_element_type=F32
            )

    def absorb(phase, j, p):
        s0 = s_ref[p, 0]
        s1 = s_ref[p, 1]
        old = mx[j]
        new = jnp.maximum(
            old,
            jnp.maximum(jnp.max(s0, axis=0, keepdims=True), jnp.max(s1, axis=0, keepdims=True)),
        )
        fade = jnp.exp2((old - new) * ALPHA)
        e0 = jnp.exp2((s0 - new) * ALPHA)
        e1 = jnp.exp2((s1 - new) * ALPHA)
        slot, half = phase // 2, (phase + core) % 2
        ls[j] = ls[j] * fade + (
            jnp.sum(e0, axis=0, keepdims=True) + jnp.sum(e1, axis=0, keepdims=True)
        )
        acc[j] = acc[j] * fade + (
            jnp.dot(vg[slot, half, 0], e0.astype(BF), preferred_element_type=F32)
            + jnp.dot(vg[slot, half, 1], e1.astype(BF), preferred_element_type=F32)
        )
        mx[j] = new

    score(0, 0, 0)

    def turn(g, carry):
        phase, pair = g // 4, g % 4
        last = pair == 3

        for slot in (0, 1, 2, 3):

            @pl.when(last & (phase == 2 * slot))
            def _(slot=slot):
                for copy in from_sibling(slot):
                    copy.wait_recv()

        @pl.when(last & (phase == 1))
        def _():
            for copy in (k_right, k_left, v_right, v_left):
                copy.wait_recv()
            k_on.start()
            v_on.start()
            for slot in (1, 2):
                for copy in to_sibling(slot):
                    copy.start()

        @pl.when(last & (phase == 5))
        def _():
            k_on.wait_recv()
            v_on.wait_recv()
            for copy in to_sibling(3):
                copy.start()

        score(phase, 2 * pair + 1, 1)
        absorb(phase, 2 * pair, 0)
        later = jnp.minimum(g + 1, 31)
        score(later // 4, 2 * (later % 4), 0)
        absorb(phase, 2 * pair + 1, 1)
        return carry

    lax.fori_loop(0, 32, turn, 0)

    for j in range(8):
        o = (acc[j] / ls[j]).astype(BF)
        ost[j, 0] = o[:, 0:128]
        ost[j, 1] = o[:, 128:256]

    head = yhi * 8 + mine

    def out_copy(i):
        j, to_yhi = i % 8, i // 8
        to = device(j // 4, x, j % 4, to_yhi, core)
        return (
            remote(ost.at[j, to_yhi], at_ref.at[head], o_send.at[i], o_recv.at[head], to),
            pltpu.make_async_copy(ost.at[j, to_yhi], at_ref.at[head], o_recv.at[head]),
        )

    def send_out(i, carry):
        away, local = out_copy(i)

        @pl.when(i == head)
        def _():
            local.start()

        @pl.when(i != head)
        def _():
            away.start()

        return carry

    lax.fori_loop(0, 16, send_out, 0)

    def await_out(i, carry):
        pltpu.make_async_copy(at_ref.at[i], at_ref.at[i], o_recv.at[i]).wait()
        return carry

    lax.fori_loop(0, 16, await_out, 0)

    def sent_heads(i, carry):
        own, away, local = head_copies(i)

        @pl.when(jnp.logical_not(own))
        def _():
            for copy in away:
                copy.wait_send()

        return carry

    lax.fori_loop(0, 8, sent_heads, 0)

    def sent_out(i, carry):
        away, local = out_copy(i)

        @pl.when(i != head)
        def _():
            away.wait_send()

        return carry

    lax.fori_loop(0, 16, sent_out, 0)
    for copy in (k_right, k_left, v_right, v_left, k_on, v_on):
        copy.wait_send()
    for slot in range(4):
        for copy in to_sibling(slot):
            copy.wait_send()
    w_local.wait()
    for copy in w_copies:
        copy.wait_send()
    for step in range(1, 4):
        slot = (exp + 4 - step) % 4
        remote(
            wo_ref,
            wo_all_ref.at[slot],
            w_send.at[step - 1],
            w_recv.at[step - 1],
            (ctx, slot),
        ).wait_recv()


def attention(qt, kp, vt, wo):
    return pl.pallas_call(
        attention_kernel,
        out_shape=(
            jax.ShapeDtypeStruct((16, HD, 128), BF),
            jax.ShapeDtypeStruct((4, 256, D), BF),
        ),
        in_specs=[whole(), whole(), whole(), anywhere()],
        out_specs=(anywhere(), anywhere()),
        scratch_shapes=[
            VMEM((8, HD, 256), BF),
            VMEM((4, 2, 1024, 128), BF),
            VMEM((4, 2, 2, HD, 1024), BF),
            VMEM((8, 2, 128, 256), BF),
            VMEM((2, 2, 1024, 256), F32),
            VMEM((8, HD, 256), F32),
            VMEM((8, 1, 256), F32),
            VMEM((8, 1, 256), F32),
            VMEM((8, 2, HD, 128), BF),
            pltpu.SemaphoreType.DMA((3, 8)),
            pltpu.SemaphoreType.DMA((3, 8)),
            pltpu.SemaphoreType.DMA((2, 3)),
            pltpu.SemaphoreType.DMA((2, 3)),
            pltpu.SemaphoreType.DMA((2, 4)),
            pltpu.SemaphoreType.DMA((2, 4)),
            pltpu.SemaphoreType.DMA((16,)),
            pltpu.SemaphoreType.DMA((16,)),
            pltpu.SemaphoreType.DMA((3,)),
            pltpu.SemaphoreType.DMA((3,)),
            pltpu.SemaphoreType.DMA,
        ],
        compiler_params=pltpu.CompilerParams(
            collective_id=0, has_side_effects=True, vmem_limit_bytes=40 << 20
        ),
        cost_estimate=pl.CostEstimate(
            flops=60 * 10**9, bytes_accessed=200 * 10**6, transcendentals=0
        ),
        name="attention",
    )(qt, kp, vt, wo)


def places_of(ctx, exp):
    return ctx * 2 + exp // 2, exp % 2


def peer(i, ctx, exp):
    ylo, x, z, yhi = ctx // 16, (ctx // 4) % 4, ctx % 4, exp // 2
    o = (i * 27) % 64
    to_x = (x + o % 4) % 4
    to_y = (yhi * 2 + ylo + (o // 4) % 4) % 4
    to_z = (z + o // 16) % 4
    to_ctx = (to_y % 2) * 16 + to_x * 4 + to_z
    return to_ctx * 2 + to_y // 2, (to_ctx, (to_y // 2) * 2 + exp % 2)


def greet_peers(barrier, ctx, exp):
    def greet(i, carry):
        pl.semaphore_signal(
            barrier, inc=1, device_id=peer(i, ctx, exp)[1], device_id_type=MESH
        )
        return carry

    lax.fori_loop(1, 64, greet, 0)


def route_kernel(
    at_ref,
    wo_ref,
    hit_ref,
    gain_ref,
    wr_ref,
    routes_ref,
    res_ref,
    hi_ref,
    lo_ref,
    got_ref,
    out,
    send,
    recv,
):
    ctx = lax.axis_index("ctx")
    exp = lax.axis_index("exp")
    place, _ = places_of(ctx, exp)
    barrier = pltpu.get_barrier_semaphore()
    greet_peers(barrier, ctx, exp)

    mixed = lax.dot_general(
        at_ref[...], wo_ref[...], (((0,), (0,)), ((), ())), preferred_element_type=F32
    )
    residual = hit_ref[...].astype(F32) + mixed
    res_ref[...] = residual
    inv = lax.rsqrt(jnp.mean(residual * residual, axis=-1, keepdims=True) + EPSILON)
    normed = (residual * inv * gain_ref[...]).astype(BF)
    rows = normed.shape[0]
    experts, cap = out.shape[0], out.shape[1]
    places = experts * cap
    ids = lax.broadcasted_iota(jnp.int32, (rows, experts), 1)
    picks = (routes_ref[:, 0:1] == ids) | (routes_ref[:, 1:2] == ids)
    marks = jnp.where(picks, 1.0, 0.0).astype(BF)
    before = lax.broadcasted_iota(jnp.int32, (rows, rows), 0) > lax.broadcasted_iota(
        jnp.int32, (rows, rows), 1
    )
    slots = jnp.dot(
        jnp.where(before, 1.0, 0.0).astype(BF), marks, preferred_element_type=F32
    ).astype(BF)
    spread = jnp.where(
        lax.broadcasted_iota(jnp.int32, (experts, places), 1) // cap
        == lax.broadcasted_iota(jnp.int32, (experts, places), 0),
        1.0,
        0.0,
    ).astype(BF)
    wide = lambda v: jnp.dot(v, spread, preferred_element_type=F32)
    order = (lax.broadcasted_iota(jnp.int32, (rows, places), 1) % cap).astype(F32)
    here = (wide(marks) > 0.5) & (wide(slots) == order)
    table = jnp.where(here, 1.0, 0.0).astype(BF)
    picked = lax.dot_general(
        table, normed, (((0,), (0,)), ((), ())), preferred_element_type=F32
    )
    out[...] = picked.reshape(out.shape).astype(BF)

    pl.semaphore_wait(barrier, 63)

    def row_copy(i):
        to, device = peer(i, ctx, exp)
        return pltpu.make_async_remote_copy(
            src_ref=out.at[to],
            dst_ref=got_ref.at[place],
            send_sem=send.at[i],
            recv_sem=recv.at[place],
            device_id=device,
            device_id_type=MESH,
        )

    def send_rows(i, carry):
        row_copy(i).start()
        return carry

    lax.fori_loop(1, 64, send_rows, 0)
    pltpu.make_async_copy(out.at[place], got_ref.at[place], recv.at[place]).start()

    logits = jnp.dot(normed, wr_ref[...], preferred_element_type=F32)
    top = jnp.max(jnp.where(picks, logits, -jnp.inf), axis=-1, keepdims=True)
    weights = jnp.where(picks, jnp.exp(jnp.where(picks, logits - top, 0.0)), 0.0)
    gates = weights / jnp.sum(weights, axis=-1, keepdims=True)
    gate_hi = gates.astype(BF)
    gate_lo = (gates - gate_hi.astype(F32)).astype(BF)
    hi_ref[...] = jnp.where(here, wide(gate_hi), 0.0).astype(BF)
    lo_ref[...] = jnp.where(here, wide(gate_lo), 0.0).astype(BF)

    def await_rows(i, carry):
        pltpu.make_async_copy(got_ref.at[i], got_ref.at[i], recv.at[i]).wait()
        return carry

    lax.fori_loop(0, 64, await_rows, 0)

    def sent_rows(i, carry):
        row_copy(i).wait_send()
        return carry

    lax.fori_loop(1, 64, sent_rows, 0)


def route(at, wo, hit, gain, wr, routes):
    rows = hit.shape[0]
    experts = wr.shape[1]
    places = experts * 8
    return pl.pallas_call(
        route_kernel,
        out_shape=(
            jax.ShapeDtypeStruct((rows, D), F32),
            jax.ShapeDtypeStruct((rows, places), BF),
            jax.ShapeDtypeStruct((rows, places), BF),
            jax.ShapeDtypeStruct((experts, 8, D), BF),
        ),
        in_specs=[whole()] * 6,
        out_specs=(whole(), whole(), whole(), anywhere()),
        scratch_shapes=[
            VMEM((experts, 8, D), BF),
            pltpu.SemaphoreType.DMA((64,)),
            pltpu.SemaphoreType.DMA((64,)),
        ],
        compiler_params=pltpu.CompilerParams(
            collective_id=1, has_side_effects=True, vmem_limit_bytes=32 << 20
        ),
        cost_estimate=pl.CostEstimate(
            flops=4 * 10**9, bytes_accessed=40 * 10**6, transcendentals=0
        ),
        name="route",
    )(at, wo, hit, gain.reshape(1, D), wr, routes)


def expert_kernel(
    got_ref,
    res_ref,
    hi_ref,
    lo_ref,
    gate_ref,
    up_ref,
    down_ref,
    gates_ref,
    ups_ref,
    downs_ref,
    out_ref,
    wg,
    wu,
    wd,
    stage,
    back,
    w_sem,
    send,
    recv,
):
    ctx = lax.axis_index("ctx")
    exp = lax.axis_index("exp")
    place, core = places_of(ctx, exp)
    ylo, x, z, yhi = ctx // 16, (ctx // 4) % 4, ctx % 4, exp // 2
    barrier = pltpu.get_barrier_semaphore()
    greet_peers(barrier, ctx, exp)

    loads = []
    for n, (own, others, held) in enumerate(
        ((gate_ref, gates_ref, wg), (up_ref, ups_ref, wu), (down_ref, downs_ref, wd))
    ):
        for q in range(4):
            src = own.at[yhi] if q == 0 else others[q - 1]
            copy = pltpu.make_async_copy(src, held.at[q], w_sem.at[n, q])
            loads.append((q, n, copy))
    loads.sort(key=lambda load: load[0])
    for _, _, copy in loads:
        copy.start()
    arrive = {(q, n): copy for q, n, copy in loads}

    def back_copy(g, i):
        to_z = (z + i % 4) % 4
        to_x = (x + (i // 4) % 4) % 4
        to_yhi = (yhi + i // 16) % 2
        to_ctx = g * 16 + to_x * 4 + to_z
        to = to_ctx * 2 + to_yhi
        return to, pltpu.make_async_remote_copy(
            src_ref=stage.at[to],
            dst_ref=back.at[place],
            send_sem=send.at[to],
            recv_sem=recv.at[place],
            device_id=(to_ctx, to_yhi * 2 + core),
            device_id_type=MESH,
        )

    cap = stage.shape[1]
    group = 32
    for g in range(2):
        rows = (
            got_ref[g * group : (g + 1) * group]
            .astype(F32)
            .reshape(group * cap, D)
            .astype(BF)
        )
        total = None
        for q in range(4):
            if g == 0:
                arrive[(q, 0)].wait()
                arrive[(q, 1)].wait()
            gate = jnp.dot(rows, wg[q], preferred_element_type=F32)
            up = jnp.dot(rows, wu[q], preferred_element_type=F32)
            hidden = (gate / (1.0 + jnp.exp(-gate)) * up).astype(BF)
            if g == 0:
                arrive[(q, 2)].wait()
            part = jnp.dot(hidden, wd[q], preferred_element_type=F32)
            total = part if total is None else total + part
        stage[g * group : (g + 1) * group] = total.reshape(group, cap, D).astype(BF)
        if g == 0:
            pl.semaphore_wait(barrier, 63)

        def send_back(i, carry, g=g):
            to, copy = back_copy(g, i)

            @pl.when(to != place)
            def _():
                copy.start()

            return carry

        lax.fori_loop(0, group, send_back, 0)

        @pl.when(ylo == g)
        def _():
            pltpu.make_async_copy(stage.at[place], back.at[place], recv.at[place]).start()

    residual = res_ref[...]
    hi = hi_ref[...]
    lo = lo_ref[...]

    def await_back(i, carry):
        pltpu.make_async_copy(back.at[i], back.at[i], recv.at[i]).wait()
        return carry

    lax.fori_loop(0, 64, await_back, 0)
    rows = back[...].astype(F32).reshape(64 * cap, D).astype(BF)
    mixture = jnp.dot(hi, rows, preferred_element_type=F32) + jnp.dot(
        lo, rows, preferred_element_type=F32
    )
    out_ref[...] = (residual + mixture).astype(BF)

    for g in range(2):

        def sent_back(i, carry, g=g):
            to, copy = back_copy(g, i)

            @pl.when(to != place)
            def _():
                copy.wait_send()

            return carry

        lax.fori_loop(0, group, sent_back, 0)


def run_experts(got, residual, gate_hi, gate_lo, own, gates, ups, downs):
    rows = residual.shape[0]

    def kernel(*refs):
        got_ref, res_ref, hi_ref, lo_ref, gate_ref, up_ref, down_ref = refs[:7]
        expert_kernel(
            *refs[:7], refs[7:10], refs[10:13], refs[13:16], *refs[16:]
        )

    quarter = own[0].shape[2]
    return pl.pallas_call(
        kernel,
        out_shape=jax.ShapeDtypeStruct((rows, D), BF),
        in_specs=[whole()] * 4 + [anywhere()] * 12,
        out_specs=whole(),
        scratch_shapes=[
            VMEM((4, D, quarter), BF),
            VMEM((4, D, quarter), BF),
            VMEM((4, quarter, D), BF),
            VMEM(got.shape, BF),
            VMEM(got.shape, BF),
            pltpu.SemaphoreType.DMA((3, 4)),
            pltpu.SemaphoreType.DMA((64,)),
            pltpu.SemaphoreType.DMA((64,)),
        ],
        compiler_params=pltpu.CompilerParams(
            collective_id=2, has_side_effects=True, vmem_limit_bytes=48 << 20
        ),
        name="experts",
    )(got, residual, gate_hi, gate_lo, *own, *gates, *ups, *downs)


def body(
    hit_features,
    norm_attn,
    w_query,
    w_key,
    w_value,
    w_out,
    norm_ffn,
    w_router,
    w_gate,
    w_up,
    w_down,
    routes,
):
    rows_dev = hit_features.shape[0] // lax.axis_size("exp")
    yhi = lax.axis_index("exp") // 2
    weights = (w_gate, w_up, w_down)
    across = [(e, (e + 2) % 4) for e in range(4)]
    beside = [(e, e + 1 - 2 * (e % 2)) for e in range(4)]
    pick = lambda w, n: lax.dynamic_index_in_dim(w, n, 0, keepdims=False)
    far = [lax.ppermute(pick(w, 1 - yhi), "exp", across) for w in weights]
    near = [lax.ppermute(pick(w, yhi), "exp", beside) for w in weights]
    diagonal = [lax.ppermute(w, "exp", beside) for w in far]
    qt, kp, vt = project(hit_features, norm_attn, w_query, w_key, w_value)
    at, wo = attention(qt, kp, vt, w_out)
    own_rows = lax.dynamic_slice_in_dim(
        hit_features, lax.axis_index("exp") * rows_dev, rows_dev, 0
    )
    residual, gate_hi, gate_lo, got = route(
        at.reshape(D, rows_dev), wo.reshape(D, D), own_rows, norm_ffn, w_router, routes
    )
    return run_experts(
        got, residual, gate_hi, gate_lo, weights, *zip(far, near, diagonal)
    )


def solution(mesh):
    return jax.shard_map(
        body,
        mesh=mesh,
        in_specs=(
            P("ctx", None),
            P(),
            P(None, "exp"),
            P(None, "exp"),
            P(None, "exp"),
            P("exp", None),
            P(),
            P(),
            P("ctx", None, "exp"),
            P("ctx", None, "exp"),
            P("ctx", "exp", None),
            P(("ctx", "exp"), None),
        ),
        out_specs=P(("ctx", "exp"), None),
        check_vma=False,
    )
```

```python
import functools
import math

import jax
import jax.numpy as jnp
from jax import lax
from jax.experimental import pallas as pl
from jax.experimental.pallas import tpu as pltpu
from jax.sharding import PartitionSpec as P

D = 1024
HD = 64
EPSILON = 1e-05
LOWEST = -1e30
ALPHA = math.log2(math.e) / math.sqrt(HD)
BF = jnp.bfloat16
F32 = jnp.float32
MESH = pl.DeviceIdType.MESH
VMEM = pltpu.VMEM


def whole():
    return pl.BlockSpec(memory_space=pltpu.VMEM)


def anywhere():
    return pl.BlockSpec(memory_space=pl.ANY)


def project_kernel(
    x_ref,
    gain_ref,
    wq_ref,
    wk_ref,
    wv_ref,
    gate_ref,
    up_ref,
    down_ref,
    qt_ref,
    kp_ref,
    vt_ref,
    pack_ref,
    held,
    sem,
):
    other = 1 - lax.axis_index("exp") // 2
    half = pack_ref.shape[2]
    parts = (
        (gate_ref.at[other], held.at[0]),
        (up_ref.at[other], held.at[1]),
        (down_ref.at[other, :, pl.ds(0, half)], held.at[2, pl.ds(0, half)]),
        (down_ref.at[other, :, pl.ds(half, half)], held.at[2, pl.ds(half, half)]),
    )
    taken = [pltpu.make_async_copy(src, dst, sem.at[n]) for n, (src, dst) in enumerate(parts)]
    for copy in taken:
        copy.start()
    x = x_ref[...].astype(F32)
    inv = lax.rsqrt(jnp.mean(x * x, axis=-1, keepdims=True) + EPSILON)
    n = (x * inv * gain_ref[...]).astype(BF)
    q = jnp.dot(n, wq_ref[...], preferred_element_type=F32)
    qt = q.T.astype(BF)
    for head in range(4):
        for block in range(4):
            qt_ref[block % 2, head, :, (block // 2) * 128 : (block // 2) * 128 + 128] = qt[
                head * HD : head * HD + HD, block * 128 : block * 128 + 128
            ]
    for copy in taken:
        copy.wait()
    given = pltpu.make_async_copy(held, pack_ref, sem.at[4])
    given.start()
    k = jnp.dot(n, wk_ref[...], preferred_element_type=F32)
    for head in range(4):
        for half in range(2):
            kh = k[half * 256 : half * 256 + 256, head * HD : head * HD + HD]
            kp_ref[head, half] = jnp.concatenate([kh[0:128], kh[128:256]], axis=1).astype(BF)
    vt = jnp.dot(n, wv_ref[...], preferred_element_type=F32).T.astype(BF)
    for head in range(4):
        for half in range(2):
            for u in range(2):
                at = half * 256 + u * 128
                vt_ref[head, half, u] = vt[head * HD : head * HD + HD, at : at + 128]
    given.wait()


def project(x, gain, wq, wk, wv, w_gate, w_up, w_down):
    packed = (3,) + w_gate.shape[1:]
    return pl.pallas_call(
        project_kernel,
        out_shape=(
            jax.ShapeDtypeStruct((2, 4, HD, 256), BF),
            jax.ShapeDtypeStruct((4, 2, 128, 128), BF),
            jax.ShapeDtypeStruct((4, 2, 2, HD, 128), BF),
            jax.ShapeDtypeStruct(packed, BF),
        ),
        in_specs=[whole()] * 5 + [anywhere()] * 3,
        out_specs=(whole(), whole(), whole(), anywhere()),
        scratch_shapes=[VMEM(packed, BF), pltpu.SemaphoreType.DMA((5,))],
        compiler_params=pltpu.CompilerParams(vmem_limit_bytes=60 << 20),
        name="project",
    )(x, gain.reshape(1, D), wq, wk, wv, w_gate, w_up, w_down)


def attention_kernel(
    qt_ref,
    kp_ref,
    vt_ref,
    wo_ref,
    at_ref,
    wo_all_ref,
    qg,
    kg,
    vg,
    q2,
    s_ref,
    acc,
    mx,
    ls,
    ost,
    x_send,
    x_recv,
    ring_send,
    ring_recv,
    sib_send,
    sib_recv,
    o_send,
    o_recv,
    w_send,
    w_recv,
    w_own,
):
    ctx = lax.axis_index("ctx")
    exp = lax.axis_index("exp")
    ylo = ctx // 16
    x = (ctx // 4) % 4
    z = ctx % 4
    yhi = exp // 2
    core = exp % 2
    mine = ylo * 4 + z

    def device(to_ylo, to_x, to_z, to_yhi, to_core):
        return (to_ylo * 16 + to_x * 4 + to_z, to_yhi * 2 + to_core)

    right = device(ylo, (x + 1) % 4, z, yhi, core)
    left = device(ylo, (x + 3) % 4, z, yhi, core)
    sibling = device(ylo, x, z, yhi, 1 - core)

    barrier = pltpu.get_barrier_semaphore()

    def greet(i, carry):
        to = device(i // 16, x, (i // 4) % 4, (i // 2) % 2, i % 2)

        @pl.when(i != ylo * 16 + z * 4 + yhi * 2 + core)
        def _():
            pl.semaphore_signal(barrier, inc=1, device_id=to, device_id_type=MESH)

        return carry

    lax.fori_loop(0, 32, greet, 0)
    pl.semaphore_signal(barrier, inc=1, device_id=right, device_id_type=MESH)
    pl.semaphore_signal(barrier, inc=1, device_id=left, device_id_type=MESH)
    pl.semaphore_wait(barrier, 33)

    def head_copies(i):
        head, half = i // 2, i % 2
        to = device(core, x, head, yhi, half)
        parts = (
            (qt_ref.at[half, head], qg.at[mine]),
            (kp_ref.at[head, half], kg.at[0, half, pl.ds(pl.multiple_of(mine * 128, 128), 128), :]),
            (
                vt_ref.at[head, half],
                vg.at[0, half, :, :, pl.ds(pl.multiple_of(mine * 128, 128), 128)],
            ),
        )
        own = (core == ylo) & (head == z) & (half == core)
        remote = [
            pltpu.make_async_remote_copy(
                src_ref=src,
                dst_ref=dst,
                send_sem=x_send.at[n, i],
                recv_sem=x_recv.at[n, mine],
                device_id=to,
                device_id_type=MESH,
            )
            for n, (src, dst) in enumerate(parts)
        ]
        local = [
            pltpu.make_async_copy(src, dst, x_recv.at[n, mine])
            for n, (src, dst) in enumerate(parts)
        ]
        return own, remote, local

    def send_heads(i, carry):
        own, remote, local = head_copies(i)

        @pl.when(own)
        def _():
            for copy in local:
                copy.start()

        @pl.when(jnp.logical_not(own))
        def _():
            for copy in remote:
                copy.start()

        return carry

    lax.fori_loop(0, 8, send_heads, 0)

    def await_heads(j, carry):
        pltpu.make_async_copy(qg.at[j], qg.at[j], x_recv.at[0, j]).wait()
        at = pl.ds(pl.multiple_of(j * 128, 128), 128)
        kd = kg.at[0, core, at, :]
        pltpu.make_async_copy(kd, kd, x_recv.at[1, j]).wait()
        vd = vg.at[0, core, :, :, at]
        pltpu.make_async_copy(vd, vd, x_recv.at[2, j]).wait()
        return carry

    lax.fori_loop(0, 8, await_heads, 0)

    def remote(src, dst, send, recv, to):
        return pltpu.make_async_remote_copy(
            src_ref=src,
            dst_ref=dst,
            send_sem=send,
            recv_sem=recv,
            device_id=to,
            device_id_type=MESH,
        )

    def to_sibling(slot):
        return [
            remote(g.at[slot, core], g.at[slot, core], sib_send.at[n, slot], sib_recv.at[n, slot], sibling)
            for n, g in enumerate((kg, vg))
        ]

    def from_sibling(slot):
        return [
            remote(g.at[slot, 1 - core], g.at[slot, 1 - core], sib_send.at[n, slot], sib_recv.at[n, slot], sibling)
            for n, g in enumerate((kg, vg))
        ]

    k_right = remote(kg.at[0, core], kg.at[1, core], ring_send.at[0, 0], ring_recv.at[0, 0], right)
    v_right = remote(vg.at[0, core], vg.at[1, core], ring_send.at[1, 0], ring_recv.at[1, 0], right)
    k_left = remote(kg.at[0, core], kg.at[2, core], ring_send.at[0, 1], ring_recv.at[0, 1], left)
    v_left = remote(vg.at[0, core], vg.at[2, core], ring_send.at[1, 1], ring_recv.at[1, 1], left)
    k_on = remote(kg.at[1, core], kg.at[3, core], ring_send.at[0, 2], ring_recv.at[0, 2], right)
    v_on = remote(vg.at[2, core], vg.at[3, core], ring_send.at[1, 2], ring_recv.at[1, 2], left)
    for copy in (k_right, k_left, v_right, v_left):
        copy.start()
    for copy in to_sibling(0):
        copy.start()

    far_chip = device(ylo, x, z, 1 - yhi, core)
    far_exp = (exp + 2) % 4
    w_local = pltpu.make_async_copy(wo_ref, wo_all_ref.at[exp], w_own)
    w_across = remote(wo_ref, wo_all_ref.at[exp], w_send.at[0], w_recv.at[0], far_chip)
    w_beside = remote(wo_ref, wo_all_ref.at[exp], w_send.at[1], w_recv.at[1], sibling)
    w_on = remote(
        wo_all_ref.at[far_exp], wo_all_ref.at[far_exp], w_send.at[2], w_recv.at[2], sibling
    )
    w_across.start()
    w_beside.start()
    w_local.start()

    zero = jnp.zeros((HD, 256), BF)
    for j in range(8):
        q2[j, 0, 0:HD] = qg[j]
        q2[j, 0, HD : 2 * HD] = zero
        q2[j, 1, 0:HD] = zero
        q2[j, 1, HD : 2 * HD] = qg[j]
    acc[...] = jnp.zeros_like(acc)
    mx[...] = jnp.full_like(mx, LOWEST)
    ls[...] = jnp.zeros_like(ls)

    def score(phase, j, p):
        keys = kg[phase // 2, (phase + core) % 2]
        for u in range(2):
            s_ref[p, u] = lax.dot_general(
                keys, q2[j, u], (((1,), (0,)), ((), ())), preferred_element_type=F32
            )

    def absorb(phase, j, p):
        s0 = s_ref[p, 0]
        s1 = s_ref[p, 1]
        old = mx[j]
        new = jnp.maximum(
            old,
            jnp.maximum(jnp.max(s0, axis=0, keepdims=True), jnp.max(s1, axis=0, keepdims=True)),
        )
        fade = jnp.exp2((old - new) * ALPHA)
        e0 = jnp.exp2((s0 - new) * ALPHA)
        e1 = jnp.exp2((s1 - new) * ALPHA)
        slot, half = phase // 2, (phase + core) % 2
        ls[j] = ls[j] * fade + (
            jnp.sum(e0, axis=0, keepdims=True) + jnp.sum(e1, axis=0, keepdims=True)
        )
        acc[j] = acc[j] * fade + (
            jnp.dot(vg[slot, half, 0], e0.astype(BF), preferred_element_type=F32)
            + jnp.dot(vg[slot, half, 1], e1.astype(BF), preferred_element_type=F32)
        )
        mx[j] = new

    score(0, 0, 0)

    def turn(g, carry):
        phase, pair = g // 4, g % 4
        last = pair == 3

        for slot in (0, 1, 2, 3):

            @pl.when(last & (phase == 2 * slot))
            def _(slot=slot):
                for copy in from_sibling(slot):
                    copy.wait_recv()

        @pl.when(last & (phase == 1))
        def _():
            for copy in (k_right, k_left, v_right, v_left):
                copy.wait_recv()
            k_on.start()
            v_on.start()
            for slot in (1, 2):
                for copy in to_sibling(slot):
                    copy.start()

        @pl.when(last & (phase == 5))
        def _():
            k_on.wait_recv()
            v_on.wait_recv()
            w_across.wait_recv()
            w_on.start()
            for copy in to_sibling(3):
                copy.start()

        score(phase, 2 * pair + 1, 1)
        absorb(phase, 2 * pair, 0)
        later = jnp.minimum(g + 1, 31)
        score(later // 4, 2 * (later % 4), 0)
        absorb(phase, 2 * pair + 1, 1)
        return carry

    lax.fori_loop(0, 32, turn, 0)

    for j in range(8):
        o = (acc[j] / ls[j]).astype(BF)
        ost[j, 0] = o[:, 0:128]
        ost[j, 1] = o[:, 128:256]

    head = yhi * 8 + mine

    def out_copy(i):
        j, to_yhi = i % 8, i // 8
        to = device(j // 4, x, j % 4, to_yhi, core)
        return (
            remote(ost.at[j, to_yhi], at_ref.at[head], o_send.at[i], o_recv.at[head], to),
            pltpu.make_async_copy(ost.at[j, to_yhi], at_ref.at[head], o_recv.at[head]),
        )

    def send_out(i, carry):
        away, local = out_copy(i)

        @pl.when(i == head)
        def _():
            local.start()

        @pl.when(i != head)
        def _():
            away.start()

        return carry

    lax.fori_loop(0, 16, send_out, 0)

    def await_out(i, carry):
        pltpu.make_async_copy(at_ref.at[i], at_ref.at[i], o_recv.at[i]).wait()
        return carry

    lax.fori_loop(0, 16, await_out, 0)

    def sent_heads(i, carry):
        own, away, local = head_copies(i)

        @pl.when(jnp.logical_not(own))
        def _():
            for copy in away:
                copy.wait_send()

        return carry

    lax.fori_loop(0, 8, sent_heads, 0)

    def sent_out(i, carry):
        away, local = out_copy(i)

        @pl.when(i != head)
        def _():
            away.wait_send()

        return carry

    lax.fori_loop(0, 16, sent_out, 0)
    for copy in (k_right, k_left, v_right, v_left, k_on, v_on):
        copy.wait_send()
    for slot in range(4):
        for copy in to_sibling(slot):
            copy.wait_send()
    w_local.wait()
    w_beside.wait_recv()
    w_on.wait_recv()
    for copy in (w_across, w_beside, w_on):
        copy.wait_send()


def attention(qt, kp, vt, wo):
    return pl.pallas_call(
        attention_kernel,
        out_shape=(
            jax.ShapeDtypeStruct((16, HD, 128), BF),
            jax.ShapeDtypeStruct((4, 256, D), BF),
        ),
        in_specs=[anywhere()] * 4,
        out_specs=(anywhere(), anywhere()),
        scratch_shapes=[
            VMEM((8, HD, 256), BF),
            VMEM((4, 2, 1024, 128), BF),
            VMEM((4, 2, 2, HD, 1024), BF),
            VMEM((8, 2, 128, 256), BF),
            VMEM((2, 2, 1024, 256), F32),
            VMEM((8, HD, 256), F32),
            VMEM((8, 1, 256), F32),
            VMEM((8, 1, 256), F32),
            VMEM((8, 2, HD, 128), BF),
            pltpu.SemaphoreType.DMA((3, 8)),
            pltpu.SemaphoreType.DMA((3, 8)),
            pltpu.SemaphoreType.DMA((2, 3)),
            pltpu.SemaphoreType.DMA((2, 3)),
            pltpu.SemaphoreType.DMA((2, 4)),
            pltpu.SemaphoreType.DMA((2, 4)),
            pltpu.SemaphoreType.DMA((16,)),
            pltpu.SemaphoreType.DMA((16,)),
            pltpu.SemaphoreType.DMA((3,)),
            pltpu.SemaphoreType.DMA((3,)),
            pltpu.SemaphoreType.DMA,
        ],
        compiler_params=pltpu.CompilerParams(
            collective_id=0, has_side_effects=True, vmem_limit_bytes=60 << 20
        ),
        cost_estimate=pl.CostEstimate(
            flops=60 * 10**9, bytes_accessed=200 * 10**6, transcendentals=0
        ),
        name="attention",
    )(qt, kp, vt, wo)


def shifted(o, sign, ctx, exp):
    ylo, x, z, yhi = ctx // 16, (ctx // 4) % 4, ctx % 4, exp // 2
    to_x = (x + 4 + sign * (o % 4)) % 4
    to_y = (yhi * 2 + ylo + 4 + sign * ((o // 4) % 4)) % 4
    to_z = (z + 4 + sign * (o // 16)) % 4
    to_ctx = (to_y % 2) * 16 + to_x * 4 + to_z
    return to_ctx * 2 + to_y // 2, (to_ctx, (to_y // 2) * 2 + exp % 2)


def peer(i, ctx, exp):
    return shifted((i * 27) % 64, 1, ctx, exp)


def greet_peers(barrier, ctx, exp):
    def greet(i, carry):
        pl.semaphore_signal(
            barrier, inc=1, device_id=peer(i, ctx, exp)[1], device_id_type=MESH
        )
        return carry

    beside = (ctx, exp + 1 - 2 * (exp % 2))
    pl.semaphore_signal(barrier, inc=1, device_id=beside, device_id_type=MESH)
    lax.fori_loop(1, 64, greet, 0)
    return beside


def route_kernel(
    at_hbm,
    wo_hbm,
    hit_hbm,
    gain_ref,
    wr_ref,
    routes_ref,
    res_ref,
    hi_ref,
    lo_ref,
    got_ref,
    at_ref,
    wo_ref,
    hit_ref,
    out,
    load,
    send,
    recv,
    sib_send,
    sib_recv,
):
    ctx = lax.axis_index("ctx")
    exp = lax.axis_index("exp")
    place, core = ctx * 2 + exp // 2, exp % 2
    rows = hit_ref.shape[0]
    loads = [
        pltpu.make_async_copy(at_hbm, at_ref, load.at[0]),
        pltpu.make_async_copy(wo_hbm, wo_ref, load.at[1]),
        pltpu.make_async_copy(
            hit_hbm.at[pl.ds(pl.multiple_of(exp * rows, rows), rows)], hit_ref, load.at[2]
        ),
    ]
    for copy in loads:
        copy.start()
    barrier = pltpu.get_barrier_semaphore()
    beside = greet_peers(barrier, ctx, exp)

    experts, cap = out.shape[0], out.shape[1]
    places = experts * cap
    ids = lax.broadcasted_iota(jnp.int32, (experts, rows), 0)
    picks = (routes_ref[0:1, :] == ids) | (routes_ref[1:2, :] == ids)
    marks = jnp.where(picks, 1.0, 0.0).astype(BF)
    before = lax.broadcasted_iota(jnp.int32, (rows, rows), 0) < lax.broadcasted_iota(
        jnp.int32, (rows, rows), 1
    )
    slots = jnp.dot(
        marks, jnp.where(before, 1.0, 0.0).astype(BF), preferred_element_type=F32
    ).astype(BF)
    spread = jnp.where(
        lax.broadcasted_iota(jnp.int32, (places, experts), 0) // cap
        == lax.broadcasted_iota(jnp.int32, (places, experts), 1),
        1.0,
        0.0,
    ).astype(BF)
    wide = lambda v: jnp.dot(spread, v, preferred_element_type=F32)
    order = (lax.broadcasted_iota(jnp.int32, (places, rows), 0) % cap).astype(F32)
    here = (wide(marks) > 0.5) & (wide(slots) == order)
    table = jnp.where(here, 1.0, 0.0).astype(BF)

    for copy in loads:
        copy.wait()
    mixed = lax.dot_general(
        at_ref[...].reshape(D, rows),
        wo_ref[...].reshape(D, D),
        (((0,), (0,)), ((), ())),
        preferred_element_type=F32,
    )
    residual = hit_ref[...].astype(F32) + mixed
    res_ref[...] = residual
    inv = lax.rsqrt(jnp.mean(residual * residual, axis=-1, keepdims=True) + EPSILON)
    normed = (residual * inv * gain_ref[...]).astype(BF)
    picked = jnp.dot(table, normed, preferred_element_type=F32)
    out[...] = picked.reshape(out.shape).astype(BF)

    pl.semaphore_wait(barrier, 64)

    def row_copy(i):
        to, device = peer(i, ctx, exp)
        return pltpu.make_async_remote_copy(
            src_ref=out.at[to],
            dst_ref=got_ref.at[core, place],
            send_sem=send.at[i],
            recv_sem=recv.at[place],
            device_id=device,
            device_id_type=MESH,
        )

    def send_rows(i, carry):
        row_copy(i).start()
        return carry

    lax.fori_loop(1, 64, send_rows, 0)
    pltpu.make_async_copy(out.at[place], got_ref.at[core, place], recv.at[place]).start()

    logits = lax.dot_general(
        wr_ref[...], normed, (((1,), (1,)), ((), ())), preferred_element_type=F32
    )
    top = jnp.max(jnp.where(picks, logits, -jnp.inf), axis=0, keepdims=True)
    weights = jnp.where(picks, jnp.exp(jnp.where(picks, logits - top, 0.0)), 0.0)
    gates = weights / jnp.sum(weights, axis=0, keepdims=True)
    gate_hi = gates.astype(BF)
    gate_lo = (gates - gate_hi.astype(F32)).astype(BF)
    hi_ref[...] = jnp.where(here, wide(gate_hi), 0.0).astype(BF)
    lo_ref[...] = jnp.where(here, wide(gate_lo), 0.0).astype(BF)

    def beside_copy(n, of):
        return pltpu.make_async_remote_copy(
            src_ref=got_ref.at[of, n],
            dst_ref=got_ref.at[of, n],
            send_sem=sib_send.at[n],
            recv_sem=sib_recv.at[n],
            device_id=beside,
            device_id_type=MESH,
        )

    def pass_on(i, carry):
        n, _ = shifted((i * 27) % 64, -1, ctx, exp)
        block = got_ref.at[core, n]
        pltpu.make_async_copy(block, block, recv.at[n]).wait()
        beside_copy(n, core).start()
        return carry

    lax.fori_loop(0, 64, pass_on, 0)

    def finish(i, carry):
        beside_copy(i, 1 - core).wait_recv()
        beside_copy(i, core).wait_send()
        return carry

    lax.fori_loop(0, 64, finish, 0)

    def sent_rows(i, carry):
        row_copy(i).wait_send()
        return carry

    lax.fori_loop(1, 64, sent_rows, 0)


def route(at, wo, hit, gain, wr, routes):
    experts = wr.shape[0]
    rows = routes.shape[1]
    places = experts * 8
    return pl.pallas_call(
        route_kernel,
        out_shape=(
            jax.ShapeDtypeStruct((rows, D), F32),
            jax.ShapeDtypeStruct((places, rows), BF),
            jax.ShapeDtypeStruct((places, rows), BF),
            jax.ShapeDtypeStruct((2, experts, 8, D), BF),
        ),
        in_specs=[anywhere()] * 3 + [whole()] * 3,
        out_specs=(whole(), whole(), whole(), anywhere()),
        scratch_shapes=[
            VMEM(at.shape, BF),
            VMEM(wo.shape, BF),
            VMEM((rows, D), BF),
            VMEM((experts, 8, D), BF),
            pltpu.SemaphoreType.DMA((3,)),
            pltpu.SemaphoreType.DMA((64,)),
            pltpu.SemaphoreType.DMA((64,)),
            pltpu.SemaphoreType.DMA((64,)),
            pltpu.SemaphoreType.DMA((64,)),
        ],
        compiler_params=pltpu.CompilerParams(
            collective_id=1, has_side_effects=True, vmem_limit_bytes=60 << 20
        ),
        cost_estimate=pl.CostEstimate(
            flops=4 * 10**9, bytes_accessed=40 * 10**6, transcendentals=0
        ),
        name="route",
    )(at, wo, hit, gain.reshape(1, D), wr, routes)


def expert_kernel(
    got_hbm,
    res_ref,
    hi_ref,
    lo_ref,
    gate_ref,
    up_ref,
    down_ref,
    far_ref,
    out_ref,
    got,
    wg,
    wu,
    wd,
    give,
    take,
    stage,
    back,
    w_sem,
    g_sem,
    send,
    recv,
    p_send,
    p_recv,
):
    ctx = lax.axis_index("ctx")
    exp = lax.axis_index("exp")
    place, core = ctx * 2 + exp // 2, exp % 2
    ylo, x, z, yhi = ctx // 16, (ctx // 4) % 4, ctx % 4, exp // 2
    half = far_ref.shape[2]
    got_in = [
        pltpu.make_async_copy(got_hbm.at[1 - core], got.at[0], g_sem.at[0]),
        pltpu.make_async_copy(got_hbm.at[core], got.at[1], g_sem.at[1]),
    ]
    low, high = pl.ds(0, half), pl.ds(half, half)
    loads = [
        [
            (gate_ref.at[yhi], wg.at[0]),
            (far_ref.at[0], wg.at[1]),
        ],
        [
            (up_ref.at[yhi], wu.at[0]),
            (far_ref.at[1], wu.at[1]),
        ],
        [
            (down_ref.at[yhi], wd.at[0]),
            (far_ref.at[2, low], wd.at[1, :, low]),
            (far_ref.at[2, high], wd.at[1, :, high]),
        ],
    ]
    loads = [
        [pltpu.make_async_copy(src, dst, w_sem.at[n, q]) for q, (src, dst) in enumerate(group)]
        for n, group in enumerate(loads)
    ]
    got_in[0].start()
    for n, q in ((0, 0), (1, 0), (2, 0), (0, 1), (1, 1), (2, 1), (2, 2)):
        loads[n][q].start()
    got_in[1].start()
    barrier = pltpu.get_barrier_semaphore()
    beside = greet_peers(barrier, ctx, exp)

    def back_copy(g, i):
        to_z = (z + i % 4) % 4
        to_x = (x + (i // 4) % 4) % 4
        to_yhi = (yhi + i // 16) % 2
        to_ctx = g * 16 + to_x * 4 + to_z
        to = to_ctx * 2 + to_yhi
        return to, pltpu.make_async_remote_copy(
            src_ref=stage.at[to],
            dst_ref=back.at[place],
            send_sem=send.at[to],
            recv_sem=recv.at[place],
            device_id=(to_ctx, to_yhi * 2 + core),
            device_id_type=MESH,
        )

    def part_copy(g):
        return pltpu.make_async_remote_copy(
            src_ref=give.at[g],
            dst_ref=take.at[g],
            send_sem=p_send.at[g],
            recv_sem=p_recv.at[g],
            device_id=beside,
            device_id_type=MESH,
        )

    cap = stage.shape[1]
    group = 32

    def partial(whose, g, first):
        rows = (
            got[whose, g * group : (g + 1) * group]
            .astype(F32)
            .reshape(group * cap, D)
            .astype(BF)
        )
        total = None
        for q in range(2):
            if first:
                loads[0][q].wait()
                loads[1][q].wait()
            gate = jnp.dot(rows, wg[q], preferred_element_type=F32)
            up = jnp.dot(rows, wu[q], preferred_element_type=F32)
            hidden = (gate / (1.0 + jnp.exp(-gate)) * up).astype(BF)
            if first:
                for copy in loads[2][q:] if q else loads[2][:1]:
                    copy.wait()
            part = jnp.dot(hidden, wd[q], preferred_element_type=F32)
            total = part if total is None else total + part
        return total

    for g in range(2):
        if g == 0:
            got_in[0].wait()
        give[g] = partial(0, g, g == 0).reshape(group, cap, D).astype(BF)
        if g == 0:
            pl.semaphore_wait(barrier, 64)
            got_in[1].wait()
        part_copy(g).start()
    for g in range(2):
        total = partial(1, g, False)
        part_copy(g).wait_recv()
        both = total + take[g].astype(F32).reshape(group * cap, D)
        stage[g * group : (g + 1) * group] = both.reshape(group, cap, D).astype(BF)

        def send_back(i, carry, g=g):
            to, copy = back_copy(g, i)

            @pl.when(to != place)
            def _():
                copy.start()

            return carry

        lax.fori_loop(0, group, send_back, 0)

        @pl.when(ylo == g)
        def _():
            pltpu.make_async_copy(stage.at[place], back.at[place], recv.at[place]).start()

    residual = res_ref[...]

    def await_back(i, carry):
        pltpu.make_async_copy(back.at[i], back.at[i], recv.at[i]).wait()
        return carry

    lax.fori_loop(0, 64, await_back, 0)
    rows = back[...].astype(F32).reshape(64 * cap, D).astype(BF)
    over = (((0,), (0,)), ((), ()))
    mixture = lax.dot_general(
        hi_ref[...], rows, over, preferred_element_type=F32
    ) + lax.dot_general(lo_ref[...], rows, over, preferred_element_type=F32)
    out_ref[...] = (residual + mixture).astype(BF)

    for g in range(2):

        def sent_back(i, carry, g=g):
            to, copy = back_copy(g, i)

            @pl.when(to != place)
            def _():
                copy.wait_send()

            return carry

        lax.fori_loop(0, group, sent_back, 0)
        part_copy(g).wait_send()


def run_experts(got, residual, gate_hi, gate_lo, w_gate, w_up, w_down, far):
    rows = residual.shape[0]
    quarter = w_gate.shape[2]
    return pl.pallas_call(
        expert_kernel,
        out_shape=jax.ShapeDtypeStruct((rows, D), BF),
        in_specs=[anywhere()] + [whole()] * 3 + [anywhere()] * 4,
        out_specs=whole(),
        scratch_shapes=[
            VMEM(got.shape, BF),
            VMEM((2, D, quarter), BF),
            VMEM((2, D, quarter), BF),
            VMEM((2, quarter, D), BF),
            VMEM((2, 32) + got.shape[2:], BF),
            VMEM((2, 32) + got.shape[2:], BF),
            VMEM(got.shape[1:], BF),
            VMEM(got.shape[1:], BF),
            pltpu.SemaphoreType.DMA((3, 3)),
            pltpu.SemaphoreType.DMA((2,)),
            pltpu.SemaphoreType.DMA((64,)),
            pltpu.SemaphoreType.DMA((64,)),
            pltpu.SemaphoreType.DMA((2,)),
            pltpu.SemaphoreType.DMA((2,)),
        ],
        compiler_params=pltpu.CompilerParams(
            collective_id=2, has_side_effects=True, vmem_limit_bytes=52 << 20
        ),
        name="experts",
    )(got, residual, gate_hi, gate_lo, w_gate, w_up, w_down, far)


def body(
    hit_features,
    norm_attn,
    w_query,
    w_key,
    w_value,
    w_out,
    norm_ffn,
    w_router,
    w_gate,
    w_up,
    w_down,
    routes,
):
    qt, kp, vt, packed = project(
        hit_features, norm_attn, w_query, w_key, w_value, w_gate, w_up, w_down
    )
    far = lax.ppermute(packed, "exp", [(e, (e + 2) % 4) for e in range(4)])
    at, wo = attention(qt, kp, vt, w_out)
    residual, gate_hi, gate_lo, got = route(
        at, wo, hit_features, norm_ffn, w_router.T, routes.T
    )
    return run_experts(got, residual, gate_hi, gate_lo, w_gate, w_up, w_down, far)


def solution(mesh):
    return jax.shard_map(
        body,
        mesh=mesh,
        in_specs=(
            P("ctx", None),
            P(),
            P(None, "exp"),
            P(None, "exp"),
            P(None, "exp"),
            P("exp", None),
            P(),
            P(),
            P("ctx", None, "exp"),
            P("ctx", None, "exp"),
            P("ctx", "exp", None),
            P(("ctx", "exp"), None),
        ),
        out_specs=P(("ctx", "exp"), None),
        check_vma=False,
    )
```

```python
import functools
import math

import jax
import jax.numpy as jnp
from jax import lax
from jax.experimental import pallas as pl
from jax.experimental.pallas import tpu as pltpu
from jax.sharding import PartitionSpec as P

D = 1024
HD = 64
EPSILON = 1e-05
LOWEST = -1e30
ALPHA = math.log2(math.e) / math.sqrt(HD)
BF = jnp.bfloat16
F32 = jnp.float32
MESH = pl.DeviceIdType.MESH
VMEM = pltpu.VMEM


def whole():
    return pl.BlockSpec(memory_space=pltpu.VMEM)


def anywhere():
    return pl.BlockSpec(memory_space=pl.ANY)


def project_kernel(x_ref, gain_ref, wq_ref, wk_ref, wv_ref, qt_ref, kp_ref, vt_ref):
    x = x_ref[...].astype(F32)
    inv = lax.rsqrt(jnp.mean(x * x, axis=-1, keepdims=True) + EPSILON)
    n = (x * inv * gain_ref[...]).astype(BF)
    q = jnp.dot(n, wq_ref[...], preferred_element_type=F32)
    qt = q.T.astype(BF)
    for head in range(4):
        for block in range(4):
            qt_ref[block % 2, head, :, (block // 2) * 128 : (block // 2) * 128 + 128] = qt[
                head * HD : head * HD + HD, block * 128 : block * 128 + 128
            ]
    k = jnp.dot(n, wk_ref[...], preferred_element_type=F32)
    for head in range(4):
        for half in range(2):
            kh = k[half * 256 : half * 256 + 256, head * HD : head * HD + HD]
            kp_ref[head, half] = jnp.concatenate([kh[0:128], kh[128:256]], axis=1).astype(BF)
    vt = jnp.dot(n, wv_ref[...], preferred_element_type=F32).T.astype(BF)
    for head in range(4):
        for half in range(2):
            for u in range(2):
                at = half * 256 + u * 128
                vt_ref[head, half, u] = vt[head * HD : head * HD + HD, at : at + 128]


def project(x, gain, wq, wk, wv):
    return pl.pallas_call(
        project_kernel,
        out_shape=(
            jax.ShapeDtypeStruct((2, 4, HD, 256), BF),
            jax.ShapeDtypeStruct((4, 2, 128, 128), BF),
            jax.ShapeDtypeStruct((4, 2, 2, HD, 128), BF),
        ),
        in_specs=[whole()] * 5,
        out_specs=(whole(), whole(), whole()),
        name="project",
    )(x, gain.reshape(1, D), wq, wk, wv)


def attention_kernel(
    qt_ref,
    kp_ref,
    vt_ref,
    wo_ref,
    gate_ref,
    up_ref,
    down_ref,
    at_ref,
    wo_all_ref,
    gates_ref,
    ups_ref,
    downs_ref,
    qg,
    kg,
    vg,
    q2,
    s_ref,
    acc,
    mx,
    ls,
    ost,
    x_send,
    x_recv,
    ring_send,
    ring_recv,
    sib_send,
    sib_recv,
    o_send,
    o_recv,
    w_send,
    w_recv,
    w_own,
    e_send,
    e_recv,
):
    ctx = lax.axis_index("ctx")
    exp = lax.axis_index("exp")
    ylo = ctx // 16
    x = (ctx // 4) % 4
    z = ctx % 4
    yhi = exp // 2
    core = exp % 2
    mine = ylo * 4 + z

    def device(to_ylo, to_x, to_z, to_yhi, to_core):
        return (to_ylo * 16 + to_x * 4 + to_z, to_yhi * 2 + to_core)

    right = device(ylo, (x + 1) % 4, z, yhi, core)
    left = device(ylo, (x + 3) % 4, z, yhi, core)
    sibling = device(ylo, x, z, yhi, 1 - core)

    barrier = pltpu.get_barrier_semaphore()

    def greet(i, carry):
        to = device(i // 16, x, (i // 4) % 4, (i // 2) % 2, i % 2)

        @pl.when(i != ylo * 16 + z * 4 + yhi * 2 + core)
        def _():
            pl.semaphore_signal(barrier, inc=1, device_id=to, device_id_type=MESH)

        return carry

    lax.fori_loop(0, 32, greet, 0)
    pl.semaphore_signal(barrier, inc=1, device_id=right, device_id_type=MESH)
    pl.semaphore_signal(barrier, inc=1, device_id=left, device_id_type=MESH)
    pl.semaphore_wait(barrier, 33)

    def head_copies(i):
        head, half = i // 2, i % 2
        to = device(core, x, head, yhi, half)
        parts = (
            (qt_ref.at[half, head], qg.at[mine]),
            (kp_ref.at[head, half], kg.at[0, half, pl.ds(pl.multiple_of(mine * 128, 128), 128), :]),
            (
                vt_ref.at[head, half],
                vg.at[0, half, :, :, pl.ds(pl.multiple_of(mine * 128, 128), 128)],
            ),
        )
        own = (core == ylo) & (head == z) & (half == core)
        remote = [
            pltpu.make_async_remote_copy(
                src_ref=src,
                dst_ref=dst,
                send_sem=x_send.at[n, i],
                recv_sem=x_recv.at[n, mine],
                device_id=to,
                device_id_type=MESH,
            )
            for n, (src, dst) in enumerate(parts)
        ]
        local = [
            pltpu.make_async_copy(src, dst, x_recv.at[n, mine])
            for n, (src, dst) in enumerate(parts)
        ]
        return own, remote, local

    def send_heads(i, carry):
        own, remote, local = head_copies(i)

        @pl.when(own)
        def _():
            for copy in local:
                copy.start()

        @pl.when(jnp.logical_not(own))
        def _():
            for copy in remote:
                copy.start()

        return carry

    lax.fori_loop(0, 8, send_heads, 0)

    def await_heads(j, carry):
        pltpu.make_async_copy(qg.at[j], qg.at[j], x_recv.at[0, j]).wait()
        at = pl.ds(pl.multiple_of(j * 128, 128), 128)
        kd = kg.at[0, core, at, :]
        pltpu.make_async_copy(kd, kd, x_recv.at[1, j]).wait()
        vd = vg.at[0, core, :, :, at]
        pltpu.make_async_copy(vd, vd, x_recv.at[2, j]).wait()
        return carry

    lax.fori_loop(0, 8, await_heads, 0)

    def remote(src, dst, send, recv, to):
        return pltpu.make_async_remote_copy(
            src_ref=src,
            dst_ref=dst,
            send_sem=send,
            recv_sem=recv,
            device_id=to,
            device_id_type=MESH,
        )

    def to_sibling(slot):
        return [
            remote(g.at[slot, core], g.at[slot, core], sib_send.at[n, slot], sib_recv.at[n, slot], sibling)
            for n, g in enumerate((kg, vg))
        ]

    def from_sibling(slot):
        return [
            remote(g.at[slot, 1 - core], g.at[slot, 1 - core], sib_send.at[n, slot], sib_recv.at[n, slot], sibling)
            for n, g in enumerate((kg, vg))
        ]

    k_right = remote(kg.at[0, core], kg.at[1, core], ring_send.at[0, 0], ring_recv.at[0, 0], right)
    v_right = remote(vg.at[0, core], vg.at[1, core], ring_send.at[1, 0], ring_recv.at[1, 0], right)
    k_left = remote(kg.at[0, core], kg.at[2, core], ring_send.at[0, 1], ring_recv.at[0, 1], left)
    v_left = remote(vg.at[0, core], vg.at[2, core], ring_send.at[1, 1], ring_recv.at[1, 1], left)
    k_on = remote(kg.at[1, core], kg.at[3, core], ring_send.at[0, 2], ring_recv.at[0, 2], right)
    v_on = remote(vg.at[2, core], vg.at[3, core], ring_send.at[1, 2], ring_recv.at[1, 2], left)
    for copy in (k_right, k_left, v_right, v_left):
        copy.start()
    for copy in to_sibling(0):
        copy.start()

    far_chip = device(ylo, x, z, 1 - yhi, core)
    far_exp = (exp + 2) % 4
    w_local = pltpu.make_async_copy(wo_ref, wo_all_ref.at[exp], w_own)
    w_across = remote(wo_ref, wo_all_ref.at[exp], w_send.at[0], w_recv.at[0], far_chip)
    w_beside = remote(wo_ref, wo_all_ref.at[exp], w_send.at[1], w_recv.at[1], sibling)
    w_on = remote(
        wo_all_ref.at[far_exp], wo_all_ref.at[far_exp], w_send.at[2], w_recv.at[2], sibling
    )
    w_across.start()
    w_beside.start()
    w_local.start()
    e_beside = [
        remote(src, dst, e_send.at[n], e_recv.at[n], sibling)
        for n, (src, dst) in enumerate(
            ((gate_ref, gates_ref), (up_ref, ups_ref), (down_ref, downs_ref))
        )
    ]
    for copy in e_beside:
        copy.start()

    zero = jnp.zeros((HD, 256), BF)
    for j in range(8):
        q2[j, 0, 0:HD] = qg[j]
        q2[j, 0, HD : 2 * HD] = zero
        q2[j, 1, 0:HD] = zero
        q2[j, 1, HD : 2 * HD] = qg[j]
    acc[...] = jnp.zeros_like(acc)
    mx[...] = jnp.full_like(mx, LOWEST)
    ls[...] = jnp.zeros_like(ls)

    def score(phase, j, p):
        keys = kg[phase // 2, (phase + core) % 2]
        for u in range(2):
            s_ref[p, u] = lax.dot_general(
                keys, q2[j, u], (((1,), (0,)), ((), ())), preferred_element_type=F32
            )

    def absorb(phase, j, p):
        s0 = s_ref[p, 0]
        s1 = s_ref[p, 1]
        old = mx[j]
        new = jnp.maximum(
            old,
            jnp.maximum(jnp.max(s0, axis=0, keepdims=True), jnp.max(s1, axis=0, keepdims=True)),
        )
        fade = jnp.exp2((old - new) * ALPHA)
        e0 = jnp.exp2((s0 - new) * ALPHA)
        e1 = jnp.exp2((s1 - new) * ALPHA)
        slot, half = phase // 2, (phase + core) % 2
        ls[j] = ls[j] * fade + (
            jnp.sum(e0, axis=0, keepdims=True) + jnp.sum(e1, axis=0, keepdims=True)
        )
        acc[j] = acc[j] * fade + (
            jnp.dot(vg[slot, half, 0], e0.astype(BF), preferred_element_type=F32)
            + jnp.dot(vg[slot, half, 1], e1.astype(BF), preferred_element_type=F32)
        )
        mx[j] = new

    score(0, 0, 0)

    def turn(g, carry):
        phase, pair = g // 4, g % 4
        last = pair == 3

        for slot in (0, 1, 2, 3):

            @pl.when(last & (phase == 2 * slot))
            def _(slot=slot):
                for copy in from_sibling(slot):
                    copy.wait_recv()

        @pl.when(last & (phase == 1))
        def _():
            for copy in (k_right, k_left, v_right, v_left):
                copy.wait_recv()
            k_on.start()
            v_on.start()
            for slot in (1, 2):
                for copy in to_sibling(slot):
                    copy.start()

        @pl.when(last & (phase == 5))
        def _():
            k_on.wait_recv()
            v_on.wait_recv()
            w_across.wait_recv()
            w_on.start()
            for copy in to_sibling(3):
                copy.start()

        score(phase, 2 * pair + 1, 1)
        absorb(phase, 2 * pair, 0)
        later = jnp.minimum(g + 1, 31)
        score(later // 4, 2 * (later % 4), 0)
        absorb(phase, 2 * pair + 1, 1)
        return carry

    lax.fori_loop(0, 32, turn, 0)

    for j in range(8):
        o = (acc[j] / ls[j]).astype(BF)
        ost[j, 0] = o[:, 0:128]
        ost[j, 1] = o[:, 128:256]

    head = yhi * 8 + mine

    def out_copy(i):
        j, to_yhi = i % 8, i // 8
        to = device(j // 4, x, j % 4, to_yhi, core)
        return (
            remote(ost.at[j, to_yhi], at_ref.at[head], o_send.at[i], o_recv.at[head], to),
            pltpu.make_async_copy(ost.at[j, to_yhi], at_ref.at[head], o_recv.at[head]),
        )

    def send_out(i, carry):
        away, local = out_copy(i)

        @pl.when(i == head)
        def _():
            local.start()

        @pl.when(i != head)
        def _():
            away.start()

        return carry

    lax.fori_loop(0, 16, send_out, 0)

    def await_out(i, carry):
        pltpu.make_async_copy(at_ref.at[i], at_ref.at[i], o_recv.at[i]).wait()
        return carry

    lax.fori_loop(0, 16, await_out, 0)

    def sent_heads(i, carry):
        own, away, local = head_copies(i)

        @pl.when(jnp.logical_not(own))
        def _():
            for copy in away:
                copy.wait_send()

        return carry

    lax.fori_loop(0, 8, sent_heads, 0)

    def sent_out(i, carry):
        away, local = out_copy(i)

        @pl.when(i != head)
        def _():
            away.wait_send()

        return carry

    lax.fori_loop(0, 16, sent_out, 0)
    for copy in (k_right, k_left, v_right, v_left, k_on, v_on):
        copy.wait_send()
    for slot in range(4):
        for copy in to_sibling(slot):
            copy.wait_send()
    w_local.wait()
    w_beside.wait_recv()
    w_on.wait_recv()
    for copy in (w_across, w_beside, w_on):
        copy.wait_send()
    for copy in e_beside:
        copy.wait()


def attention(qt, kp, vt, wo, experts):
    return pl.pallas_call(
        attention_kernel,
        out_shape=(
            jax.ShapeDtypeStruct((16, HD, 128), BF),
            jax.ShapeDtypeStruct((4, 256, D), BF),
        )
        + tuple(jax.ShapeDtypeStruct(w.shape, BF) for w in experts),
        in_specs=[anywhere()] * 7,
        out_specs=(anywhere(),) * 5,
        scratch_shapes=[
            VMEM((8, HD, 256), BF),
            VMEM((4, 2, 1024, 128), BF),
            VMEM((4, 2, 2, HD, 1024), BF),
            VMEM((8, 2, 128, 256), BF),
            VMEM((2, 2, 1024, 256), F32),
            VMEM((8, HD, 256), F32),
            VMEM((8, 1, 256), F32),
            VMEM((8, 1, 256), F32),
            VMEM((8, 2, HD, 128), BF),
            pltpu.SemaphoreType.DMA((3, 8)),
            pltpu.SemaphoreType.DMA((3, 8)),
            pltpu.SemaphoreType.DMA((2, 3)),
            pltpu.SemaphoreType.DMA((2, 3)),
            pltpu.SemaphoreType.DMA((2, 4)),
            pltpu.SemaphoreType.DMA((2, 4)),
            pltpu.SemaphoreType.DMA((16,)),
            pltpu.SemaphoreType.DMA((16,)),
            pltpu.SemaphoreType.DMA((3,)),
            pltpu.SemaphoreType.DMA((3,)),
            pltpu.SemaphoreType.DMA,
            pltpu.SemaphoreType.DMA((3,)),
            pltpu.SemaphoreType.DMA((3,)),
        ],
        compiler_params=pltpu.CompilerParams(
            collective_id=0, has_side_effects=True, vmem_limit_bytes=60 << 20
        ),
        cost_estimate=pl.CostEstimate(
            flops=60 * 10**9, bytes_accessed=200 * 10**6, transcendentals=0
        ),
        name="attention",
    )(qt, kp, vt, wo, *experts)


def shifted(i, sign, ctx, exp):
    o = (i * 27) % 64
    ylo, x, z, yhi = ctx // 16, (ctx // 4) % 4, ctx % 4, exp // 2
    to_x = (x + 4 + sign * (o % 4)) % 4
    to_y = (yhi * 2 + ylo + 4 + sign * ((o // 4) % 4)) % 4
    to_z = (z + 4 + sign * (o // 16)) % 4
    to_ctx = (to_y % 2) * 16 + to_x * 4 + to_z
    return to_ctx, (to_y // 2) * 2 + exp % 2


def mixture_kernel(
    at_hbm,
    wo_hbm,
    hit_hbm,
    gain_ref,
    wr_ref,
    routes_ref,
    gate_ref,
    up_ref,
    down_ref,
    gates_ref,
    ups_ref,
    downs_ref,
    out_ref,
    at_ref,
    wo_ref,
    hit_ref,
    wg,
    wu,
    wd,
    rows_out,
    got,
    stage,
    back,
    load,
    w_sem,
    send,
    recv,
    b_send,
    b_recv,
):
    ctx = lax.axis_index("ctx")
    exp = lax.axis_index("exp")
    yhi = exp // 2
    rows = hit_ref.shape[0]
    loads = [
        pltpu.make_async_copy(at_hbm, at_ref, load.at[0]),
        pltpu.make_async_copy(wo_hbm, wo_ref, load.at[1]),
        pltpu.make_async_copy(
            hit_hbm.at[pl.ds(pl.multiple_of(exp * rows, rows), rows)], hit_ref, load.at[2]
        ),
    ]
    weight_loads = [
        pltpu.make_async_copy(src, dst.at[q], w_sem.at[n, q])
        for n, (own, near, dst) in enumerate(
            ((gate_ref, gates_ref, wg), (up_ref, ups_ref, wu), (down_ref, downs_ref, wd))
        )
        for q, src in enumerate((own, near))
    ]
    for copy in loads:
        copy.start()
    barrier = pltpu.get_barrier_semaphore()

    def greet(i, carry):
        pl.semaphore_signal(
            barrier, inc=1, device_id=shifted(i, 1, ctx, exp), device_id_type=MESH
        )
        return carry

    lax.fori_loop(1, 64, greet, 0)

    experts, cap = rows_out.shape[0], rows_out.shape[1]
    places = experts * cap
    ids = lax.broadcasted_iota(jnp.int32, (experts, rows), 0)
    picks = (routes_ref[0:1, :] == ids) | (routes_ref[1:2, :] == ids)
    marks = jnp.where(picks, 1.0, 0.0).astype(BF)
    before = lax.broadcasted_iota(jnp.int32, (rows, rows), 0) < lax.broadcasted_iota(
        jnp.int32, (rows, rows), 1
    )
    slots = jnp.dot(
        marks, jnp.where(before, 1.0, 0.0).astype(BF), preferred_element_type=F32
    ).astype(BF)
    spread = jnp.where(
        lax.broadcasted_iota(jnp.int32, (places, experts), 0) // cap
        == lax.broadcasted_iota(jnp.int32, (places, experts), 1),
        1.0,
        0.0,
    ).astype(BF)
    wide = lambda v: jnp.dot(spread, v, preferred_element_type=F32)
    order = (lax.broadcasted_iota(jnp.int32, (places, rows), 0) % cap).astype(F32)
    here = (wide(marks) > 0.5) & (wide(slots) == order)
    table = jnp.where(here, 1.0, 0.0).astype(BF)

    for copy in loads:
        copy.wait()
    for copy in weight_loads:
        copy.start()
    mixed = lax.dot_general(
        at_ref[...].reshape(D, rows),
        wo_ref[...].reshape(D, D),
        (((0,), (0,)), ((), ())),
        preferred_element_type=F32,
    )
    residual = hit_ref[...].astype(F32) + mixed
    inv = lax.rsqrt(jnp.mean(residual * residual, axis=-1, keepdims=True) + EPSILON)
    normed = (residual * inv * gain_ref[...]).astype(BF)
    picked = jnp.dot(table, normed, preferred_element_type=F32)
    rows_out[...] = picked.reshape(rows_out.shape).astype(BF)

    pl.semaphore_wait(barrier, 63)

    def pair(n):
        return pl.ds(pl.multiple_of(2 * n, 2), 2)

    def row_copy(i):
        to = shifted(i, 1, ctx, exp)
        return pltpu.make_async_remote_copy(
            src_ref=rows_out.at[pair(to[0])],
            dst_ref=got.at[i],
            send_sem=send.at[i],
            recv_sem=recv.at[i],
            device_id=to,
            device_id_type=MESH,
        )

    def back_copy(i):
        return pltpu.make_async_remote_copy(
            src_ref=stage.at[i],
            dst_ref=back.at[yhi, pair(ctx)],
            send_sem=b_send.at[i],
            recv_sem=b_recv.at[i],
            device_id=shifted(i, -1, ctx, exp),
            device_id_type=MESH,
        )

    def send_rows(i, carry):
        row_copy(i).start()
        return carry

    pltpu.make_async_copy(rows_out.at[pair(ctx)], got.at[0], recv.at[0]).start()
    lax.fori_loop(1, 64, send_rows, 0)

    logits = lax.dot_general(
        wr_ref[...], normed, (((1,), (1,)), ((), ())), preferred_element_type=F32
    )
    top = jnp.max(jnp.where(picks, logits, -jnp.inf), axis=0, keepdims=True)
    weights = jnp.where(picks, jnp.exp(jnp.where(picks, logits - top, 0.0)), 0.0)
    gates = weights / jnp.sum(weights, axis=0, keepdims=True)
    gate_hi = gates.astype(BF)
    gate_lo = (gates - gate_hi.astype(F32)).astype(BF)
    hi = jnp.where(here, wide(gate_hi), 0.0).astype(BF)
    lo = jnp.where(here, wide(gate_lo), 0.0).astype(BF)
    for copy in weight_loads:
        copy.wait()

    group = 32

    def serve(g, carry):
        first = g * group

        def await_rows(i, carry):
            pltpu.make_async_copy(got.at[first + i], got.at[first + i], recv.at[first + i]).wait()
            return carry

        lax.fori_loop(0, group, await_rows, 0)
        at = pl.ds(pl.multiple_of(first, group), group)

        def expert(j, carry):
            mine = got[at, j].astype(F32).reshape(group * cap, D).astype(BF)
            total = None
            for q in range(2):
                gate = jnp.dot(mine, wg[q, j], preferred_element_type=F32)
                up = jnp.dot(mine, wu[q, j], preferred_element_type=F32)
                hidden = (gate / (1.0 + jnp.exp(-gate)) * up).astype(BF)
                part = jnp.dot(hidden, wd[q, j], preferred_element_type=F32)
                total = part if total is None else total + part
            stage[at, j] = total.reshape(group, cap, D).astype(BF)
            return carry

        lax.fori_loop(0, 2, expert, 0)

        @pl.when(g == 0)
        def _():
            pltpu.make_async_copy(stage.at[0], back.at[yhi, pair(ctx)], b_recv.at[0]).start()

        def send_back(i, carry):
            @pl.when(first + i > 0)
            def _():
                back_copy(first + i).start()

            return carry

        lax.fori_loop(0, group, send_back, 0)
        return carry

    lax.fori_loop(0, 2, serve, 0)

    def await_back(i, carry):
        from_ctx, from_exp = shifted(i, 1, ctx, exp)
        block = back.at[from_exp // 2, pair(from_ctx)]
        pltpu.make_async_copy(block, block, b_recv.at[i]).wait()
        return carry

    lax.fori_loop(0, 64, await_back, 0)
    total = residual
    for n in range(2):
        mine = back[n].astype(F32).reshape(places, D).astype(BF)
        for gate in (hi, lo):
            total = total + lax.dot_general(
                gate, mine, (((0,), (0,)), ((), ())), preferred_element_type=F32
            )
    out_ref[...] = total.astype(BF)

    def sent(i, carry):
        row_copy(i).wait_send()
        back_copy(i).wait_send()
        return carry

    lax.fori_loop(1, 64, sent, 0)


def mixture(at, wo, hit, gain, wr, routes, own, near):
    experts = wr.shape[0]
    rows = routes.shape[1]
    cap = 8
    return pl.pallas_call(
        mixture_kernel,
        out_shape=jax.ShapeDtypeStruct((rows, D), BF),
        in_specs=[anywhere()] * 3 + [whole()] * 3 + [anywhere()] * 6,
        out_specs=whole(),
        scratch_shapes=[
            VMEM(at.shape, BF),
            VMEM(wo.shape, BF),
            VMEM((rows, D), BF),
            VMEM((2,) + own[0].shape, BF),
            VMEM((2,) + own[1].shape, BF),
            VMEM((2,) + own[2].shape, BF),
            VMEM((experts, cap, D), BF),
            VMEM((64, 2, cap, D), BF),
            VMEM((64, 2, cap, D), BF),
            VMEM((2, experts, cap, D), BF),
            pltpu.SemaphoreType.DMA((3,)),
            pltpu.SemaphoreType.DMA((3, 2)),
            pltpu.SemaphoreType.DMA((64,)),
            pltpu.SemaphoreType.DMA((64,)),
            pltpu.SemaphoreType.DMA((64,)),
            pltpu.SemaphoreType.DMA((64,)),
        ],
        compiler_params=pltpu.CompilerParams(
            collective_id=1, has_side_effects=True, vmem_limit_bytes=60 << 20
        ),
        name="mixture",
    )(at, wo, hit, gain.reshape(1, D), wr, routes, *own, *near)


def body(
    hit_features,
    norm_attn,
    w_query,
    w_key,
    w_value,
    w_out,
    norm_ffn,
    w_router,
    w_gate,
    w_up,
    w_down,
    routes,
):
    qt, kp, vt = project(hit_features, norm_attn, w_query, w_key, w_value)
    own = (w_gate, w_up, w_down)
    at, wo, *near = attention(qt, kp, vt, w_out, own)
    return mixture(at, wo, hit_features, norm_ffn, w_router.T, routes.T, own, near)


def solution(mesh):
    return jax.shard_map(
        body,
        mesh=mesh,
        in_specs=(
            P("ctx", None),
            P(),
            P(None, "exp"),
            P(None, "exp"),
            P(None, "exp"),
            P("exp", None),
            P(),
            P(),
            P("ctx", None, "exp"),
            P("ctx", None, "exp"),
            P("ctx", "exp", None),
            P(("ctx", "exp"), None),
        ),
        out_specs=P(("ctx", "exp"), None),
        check_vma=False,
    )
```

```python
import functools
import math

import jax
import jax.numpy as jnp
from jax import lax
from jax.experimental import pallas as pl
from jax.experimental.pallas import tpu as pltpu
from jax.sharding import PartitionSpec as P

D = 1024
HD = 64
EPSILON = 1e-05
LOWEST = -1e30
ALPHA = math.log2(math.e) / math.sqrt(HD)
BF = jnp.bfloat16
F32 = jnp.float32
MESH = pl.DeviceIdType.MESH
VMEM = pltpu.VMEM


def whole():
    return pl.BlockSpec(memory_space=pltpu.VMEM)


def anywhere():
    return pl.BlockSpec(memory_space=pl.ANY)


def shifted(i, sign, ctx, exp):
    o = (i * 27) % 64
    ylo, x, z, yhi = ctx // 16, (ctx // 4) % 4, ctx % 4, exp // 2
    to_x = (x + 4 + sign * (o % 4)) % 4
    to_y = (yhi * 2 + ylo + 4 + sign * ((o // 4) % 4)) % 4
    to_z = (z + 4 + sign * (o // 16)) % 4
    to_ctx = (to_y % 2) * 16 + to_x * 4 + to_z
    return to_ctx, (to_y // 2) * 2 + exp % 2


def layer_kernel(
    hit_hbm,
    gain_attn_ref,
    wq_hbm,
    wk_hbm,
    wv_hbm,
    wo_ref,
    gain_ref,
    wr_ref,
    routes_ref,
    gate_ref,
    up_ref,
    down_ref,
    out_ref,
    x_ref,
    wq_ref,
    wk_ref,
    wv_ref,
    qt_ref,
    kp_ref,
    vt_ref,
    qg,
    kg,
    vg,
    q2,
    s_ref,
    acc,
    mx,
    ls,
    ost,
    at_ref,
    wo_all,
    wg,
    wu,
    wd,
    rows_out,
    got,
    stage,
    back,
    load,
    x_send,
    x_recv,
    ring_send,
    ring_recv,
    sib_send,
    sib_recv,
    o_send,
    o_recv,
    w_send,
    w_recv,
    w_own,
    e_send,
    e_recv,
    w_sem,
    send,
    recv,
    b_send,
    b_recv,
):
    ctx = lax.axis_index("ctx")
    exp = lax.axis_index("exp")
    ylo = ctx // 16
    x = (ctx // 4) % 4
    z = ctx % 4
    yhi = exp // 2
    core = exp % 2
    mine = ylo * 4 + z

    def device(to_ylo, to_x, to_z, to_yhi, to_core):
        return (to_ylo * 16 + to_x * 4 + to_z, to_yhi * 2 + to_core)

    right = device(ylo, (x + 1) % 4, z, yhi, core)
    left = device(ylo, (x + 3) % 4, z, yhi, core)
    sibling = device(ylo, x, z, yhi, 1 - core)

    barrier = pltpu.get_barrier_semaphore()

    def greet(i, carry):
        pl.semaphore_signal(
            barrier, inc=1, device_id=shifted(i, 1, ctx, exp), device_id_type=MESH
        )
        return carry

    def greet_plane(i, carry):
        to = device(i // 8, x, (i // 2) % 4, i % 2, 1 - core)
        pl.semaphore_signal(barrier, inc=1, device_id=to, device_id_type=MESH)
        return carry

    loads = [
        pltpu.make_async_copy(src, dst, load.at[m])
        for m, (src, dst) in enumerate(
            ((hit_hbm, x_ref), (wq_hbm, wq_ref), (wk_hbm, wk_ref), (wv_hbm, wv_ref))
        )
    ]
    for copy in loads:
        copy.start()
    lax.fori_loop(0, 16, greet_plane, 0)
    lax.fori_loop(1, 64, greet, 0)

    for copy in loads[:2]:
        copy.wait()
    xs = x_ref[...].astype(F32)
    inv = lax.rsqrt(jnp.mean(xs * xs, axis=-1, keepdims=True) + EPSILON)
    n = (xs * inv * gain_attn_ref[...]).astype(BF)
    qt = jnp.dot(n, wq_ref[...], preferred_element_type=F32).T.astype(BF)
    for head in range(4):
        for block in range(4):
            qt_ref[block % 2, head, :, (block // 2) * 128 : (block // 2) * 128 + 128] = qt[
                head * HD : head * HD + HD, block * 128 : block * 128 + 128
            ]
    loads[2].wait()
    k = jnp.dot(n, wk_ref[...], preferred_element_type=F32)
    for head in range(4):
        for half in range(2):
            kh = k[half * 256 : half * 256 + 256, head * HD : head * HD + HD]
            kp_ref[head, half] = jnp.concatenate([kh[0:128], kh[128:256]], axis=1).astype(BF)
    loads[3].wait()
    vt = jnp.dot(n, wv_ref[...], preferred_element_type=F32).T.astype(BF)
    for head in range(4):
        for half in range(2):
            for u in range(2):
                at = half * 256 + u * 128
                vt_ref[head, half, u] = vt[head * HD : head * HD + HD, at : at + 128]

    pl.semaphore_wait(barrier, 79)

    def head_copies(i):
        head, half = (z + 1 + i // 2) % 4, i % 2
        to = device(core, x, head, yhi, half)
        parts = (
            (qt_ref.at[half, head], qg.at[mine]),
            (kp_ref.at[head, half], kg.at[0, half, pl.ds(pl.multiple_of(mine * 128, 128), 128), :]),
            (
                vt_ref.at[head, half],
                vg.at[0, half, :, :, pl.ds(pl.multiple_of(mine * 128, 128), 128)],
            ),
        )
        own = (core == ylo) & (head == z) & (half == core)
        remote = [
            pltpu.make_async_remote_copy(
                src_ref=src,
                dst_ref=dst,
                send_sem=x_send.at[n, i],
                recv_sem=x_recv.at[n, mine],
                device_id=to,
                device_id_type=MESH,
            )
            for n, (src, dst) in enumerate(parts)
        ]
        local = [
            pltpu.make_async_copy(src, dst, x_recv.at[n, mine])
            for n, (src, dst) in enumerate(parts)
        ]
        return own, remote, local

    def send_heads(i, carry):
        own, remote, local = head_copies(i)

        @pl.when(own)
        def _():
            for copy in local:
                copy.start()

        @pl.when(jnp.logical_not(own))
        def _():
            for copy in remote:
                copy.start()

        return carry

    lax.fori_loop(0, 8, send_heads, 0)

    def await_heads(j, carry):
        pltpu.make_async_copy(qg.at[j], qg.at[j], x_recv.at[0, j]).wait()
        at = pl.ds(pl.multiple_of(j * 128, 128), 128)
        kd = kg.at[0, core, at, :]
        pltpu.make_async_copy(kd, kd, x_recv.at[1, j]).wait()
        vd = vg.at[0, core, :, :, at]
        pltpu.make_async_copy(vd, vd, x_recv.at[2, j]).wait()
        return carry

    lax.fori_loop(0, 8, await_heads, 0)

    def remote(src, dst, send, recv, to):
        return pltpu.make_async_remote_copy(
            src_ref=src,
            dst_ref=dst,
            send_sem=send,
            recv_sem=recv,
            device_id=to,
            device_id_type=MESH,
        )

    def to_sibling(slot):
        return [
            remote(g.at[slot, core], g.at[slot, core], sib_send.at[n, slot], sib_recv.at[n, slot], sibling)
            for n, g in enumerate((kg, vg))
        ]

    def from_sibling(slot):
        return [
            remote(g.at[slot, 1 - core], g.at[slot, 1 - core], sib_send.at[n, slot], sib_recv.at[n, slot], sibling)
            for n, g in enumerate((kg, vg))
        ]

    k_right = remote(kg.at[0, core], kg.at[1, core], ring_send.at[0, 0], ring_recv.at[0, 0], right)
    v_right = remote(vg.at[0, core], vg.at[1, core], ring_send.at[1, 0], ring_recv.at[1, 0], right)
    k_left = remote(kg.at[0, core], kg.at[2, core], ring_send.at[0, 1], ring_recv.at[0, 1], left)
    v_left = remote(vg.at[0, core], vg.at[2, core], ring_send.at[1, 1], ring_recv.at[1, 1], left)
    k_on = remote(kg.at[1, core], kg.at[3, core], ring_send.at[0, 2], ring_recv.at[0, 2], right)
    v_on = remote(vg.at[2, core], vg.at[3, core], ring_send.at[1, 2], ring_recv.at[1, 2], left)
    for copy in (k_right, k_left, v_right, v_left):
        copy.start()
    for copy in to_sibling(0):
        copy.start()

    far_chip = device(ylo, x, z, 1 - yhi, core)
    far_exp = (exp + 2) % 4
    w_local = pltpu.make_async_copy(wo_ref, wo_all.at[exp], w_own)
    w_across = remote(wo_ref, wo_all.at[exp], w_send.at[0], w_recv.at[0], far_chip)
    w_beside = remote(wo_ref, wo_all.at[exp], w_send.at[1], w_recv.at[1], sibling)
    w_on = remote(
        wo_all.at[far_exp], wo_all.at[far_exp], w_send.at[2], w_recv.at[2], sibling
    )
    w_across.start()
    w_beside.start()
    w_local.start()
    e_beside = [
        remote(src, dst, e_send.at[n], e_recv.at[n], sibling)
        for n, (src, dst) in enumerate(
            ((gate_ref, wg.at[1]), (up_ref, wu.at[1]), (down_ref, wd.at[1]))
        )
    ]
    weight_loads = [
        pltpu.make_async_copy(src, dst.at[0], w_sem.at[n])
        for n, (src, dst) in enumerate(((gate_ref, wg), (up_ref, wu), (down_ref, wd)))
    ]
    for copy in weight_loads:
        copy.start()
    for copy in e_beside:
        copy.start()

    zero = jnp.zeros((HD, 256), BF)
    for j in range(8):
        q2[j, 0, 0:HD] = qg[j]
        q2[j, 0, HD : 2 * HD] = zero
        q2[j, 1, 0:HD] = zero
        q2[j, 1, HD : 2 * HD] = qg[j]
    acc[...] = jnp.zeros_like(acc)
    mx[...] = jnp.full_like(mx, LOWEST)
    ls[...] = jnp.zeros_like(ls)

    def score(phase, tile, p):
        j = (tile + mine) % 8
        keys = kg[phase // 2, (phase + core) % 2]
        for u in range(2):
            s_ref[p, u] = lax.dot_general(
                keys, q2[j, u], (((1,), (0,)), ((), ())), preferred_element_type=F32
            )

    def absorb(phase, tile, p):
        j = (tile + mine) % 8
        s0 = s_ref[p, 0]
        s1 = s_ref[p, 1]
        old = mx[j]
        new = jnp.maximum(
            old,
            jnp.maximum(jnp.max(s0, axis=0, keepdims=True), jnp.max(s1, axis=0, keepdims=True)),
        )
        fade = jnp.exp2((old - new) * ALPHA)
        e0 = jnp.exp2((s0 - new) * ALPHA)
        e1 = jnp.exp2((s1 - new) * ALPHA)
        slot, half = phase // 2, (phase + core) % 2
        ls[j] = ls[j] * fade + (
            jnp.sum(e0, axis=0, keepdims=True) + jnp.sum(e1, axis=0, keepdims=True)
        )
        acc[j] = acc[j] * fade + (
            jnp.dot(vg[slot, half, 0], e0.astype(BF), preferred_element_type=F32)
            + jnp.dot(vg[slot, half, 1], e1.astype(BF), preferred_element_type=F32)
        )
        mx[j] = new

    head = yhi * 8 + mine

    def out_copy(i):
        j, to_yhi = i % 8, i // 8
        to = device(j // 4, x, j % 4, to_yhi, core)
        return (
            remote(ost.at[j, to_yhi], at_ref.at[head], o_send.at[i], o_recv.at[head], to),
            pltpu.make_async_copy(ost.at[j, to_yhi], at_ref.at[head], o_recv.at[head]),
        )

    def send_out(tile):
        j = (tile + mine) % 8
        o = (acc[j] / ls[j]).astype(BF)
        ost[j, 0] = o[:, 0:128]
        ost[j, 1] = o[:, 128:256]
        for to_yhi in range(2):
            i = to_yhi * 8 + j
            away, local = out_copy(i)

            @pl.when(i == head)
            def _(local=local):
                local.start()

            @pl.when(i != head)
            def _(away=away):
                away.start()

    score(0, 0, 0)

    def turn(g, carry):
        phase, pair = g // 4, g % 4
        last = pair == 3

        for slot in (0, 1, 2, 3):

            @pl.when(last & (phase == 2 * slot))
            def _(slot=slot):
                for copy in from_sibling(slot):
                    copy.wait_recv()

        @pl.when(last & (phase == 1))
        def _():
            for copy in (k_right, k_left, v_right, v_left):
                copy.wait_recv()
            k_on.start()
            v_on.start()
            for slot in (1, 2):
                for copy in to_sibling(slot):
                    copy.start()

        @pl.when(last & (phase == 5))
        def _():
            k_on.wait_recv()
            v_on.wait_recv()
            w_across.wait_recv()
            w_on.start()
            for copy in to_sibling(3):
                copy.start()

        score(phase, 2 * pair + 1, 1)
        absorb(phase, 2 * pair, 0)
        later = jnp.minimum(g + 1, 31)
        score(later // 4, 2 * (later % 4), 0)
        absorb(phase, 2 * pair + 1, 1)

        @pl.when(phase == 7)
        def _():
            send_out(2 * pair)
            send_out(2 * pair + 1)

        return carry

    lax.fori_loop(0, 32, turn, 0)

    rows = at_ref.shape[2]
    experts, cap = rows_out.shape[0], rows_out.shape[1]
    places = experts * cap
    ids = lax.broadcasted_iota(jnp.int32, (experts, rows), 0)
    picks = (routes_ref[0:1, :] == ids) | (routes_ref[1:2, :] == ids)
    marks = jnp.where(picks, 1.0, 0.0).astype(BF)
    before = lax.broadcasted_iota(jnp.int32, (rows, rows), 0) < lax.broadcasted_iota(
        jnp.int32, (rows, rows), 1
    )
    slots = jnp.dot(
        marks, jnp.where(before, 1.0, 0.0).astype(BF), preferred_element_type=F32
    ).astype(BF)
    spread = jnp.where(
        lax.broadcasted_iota(jnp.int32, (places, experts), 0) // cap
        == lax.broadcasted_iota(jnp.int32, (places, experts), 1),
        1.0,
        0.0,
    ).astype(BF)
    wide = lambda v: jnp.dot(spread, v, preferred_element_type=F32)
    order = (lax.broadcasted_iota(jnp.int32, (places, rows), 0) % cap).astype(F32)
    here = (wide(marks) > 0.5) & (wide(slots) == order)
    table = jnp.where(here, 1.0, 0.0).astype(BF)

    def await_out(i, carry):
        pltpu.make_async_copy(at_ref.at[i], at_ref.at[i], o_recv.at[i]).wait()
        return carry

    lax.fori_loop(0, 16, await_out, 0)

    w_local.wait()
    w_beside.wait_recv()
    w_on.wait_recv()
    mixed = lax.dot_general(
        at_ref[...].reshape(D, rows),
        wo_all[...].reshape(D, D),
        (((0,), (0,)), ((), ())),
        preferred_element_type=F32,
    )
    own_rows = x_ref[pl.ds(pl.multiple_of(exp * rows, rows), rows), :]
    residual = own_rows.astype(F32) + mixed
    inv = lax.rsqrt(jnp.mean(residual * residual, axis=-1, keepdims=True) + EPSILON)
    normed = (residual * inv * gain_ref[...]).astype(BF)
    picked = jnp.dot(table, normed, preferred_element_type=F32)
    rows_out[...] = picked.reshape(rows_out.shape).astype(BF)

    def pair(n):
        return pl.ds(pl.multiple_of(2 * n, 2), 2)

    def row_copy(i):
        to = shifted(i, 1, ctx, exp)
        return pltpu.make_async_remote_copy(
            src_ref=rows_out.at[pair(to[0])],
            dst_ref=got.at[i],
            send_sem=send.at[i],
            recv_sem=recv.at[i],
            device_id=to,
            device_id_type=MESH,
        )

    def back_copy(i):
        return pltpu.make_async_remote_copy(
            src_ref=stage.at[i],
            dst_ref=back.at[yhi, pair(ctx)],
            send_sem=b_send.at[i],
            recv_sem=b_recv.at[i],
            device_id=shifted(i, -1, ctx, exp),
            device_id_type=MESH,
        )

    def send_rows(i, carry):
        row_copy(i).start()
        return carry

    pltpu.make_async_copy(rows_out.at[pair(ctx)], got.at[0], recv.at[0]).start()
    lax.fori_loop(1, 64, send_rows, 0)

    logits = lax.dot_general(
        wr_ref[...], normed, (((1,), (1,)), ((), ())), preferred_element_type=F32
    )
    top = jnp.max(jnp.where(picks, logits, -jnp.inf), axis=0, keepdims=True)
    weights = jnp.where(picks, jnp.exp(jnp.where(picks, logits - top, 0.0)), 0.0)
    gates = weights / jnp.sum(weights, axis=0, keepdims=True)
    gate_hi = gates.astype(BF)
    gate_lo = (gates - gate_hi.astype(F32)).astype(BF)
    hi = jnp.where(here, wide(gate_hi), 0.0).astype(BF)
    lo = jnp.where(here, wide(gate_lo), 0.0).astype(BF)
    for copy in weight_loads:
        copy.wait()
    for copy in e_beside:
        copy.wait_recv()

    group = 32

    def serve(g, carry):
        first = g * group

        def await_rows(i, carry):
            pltpu.make_async_copy(got.at[first + i], got.at[first + i], recv.at[first + i]).wait()
            return carry

        lax.fori_loop(0, group, await_rows, 0)
        at = pl.ds(pl.multiple_of(first, group), group)

        def expert(j, carry):
            mine = got[at, j].astype(F32).reshape(group * cap, D).astype(BF)
            total = None
            for q in range(2):
                gate = jnp.dot(mine, wg[q, j], preferred_element_type=F32)
                up = jnp.dot(mine, wu[q, j], preferred_element_type=F32)
                hidden = (gate / (1.0 + jnp.exp(-gate)) * up).astype(BF)
                part = jnp.dot(hidden, wd[q, j], preferred_element_type=F32)
                total = part if total is None else total + part
            stage[at, j] = total.reshape(group, cap, D).astype(BF)
            return carry

        lax.fori_loop(0, 2, expert, 0)

        @pl.when(g == 0)
        def _():
            pltpu.make_async_copy(stage.at[0], back.at[yhi, pair(ctx)], b_recv.at[0]).start()

        def send_back(i, carry):
            @pl.when(first + i > 0)
            def _():
                back_copy(first + i).start()

            return carry

        lax.fori_loop(0, group, send_back, 0)
        return carry

    lax.fori_loop(0, 2, serve, 0)

    def await_back(i, carry):
        from_ctx, from_exp = shifted(i, 1, ctx, exp)
        block = back.at[from_exp // 2, pair(from_ctx)]
        pltpu.make_async_copy(block, block, b_recv.at[i]).wait()
        return carry

    lax.fori_loop(0, 64, await_back, 0)
    total = residual
    for n in range(2):
        served = back[n].astype(F32).reshape(places, D).astype(BF)
        for gate in (hi, lo):
            total = total + lax.dot_general(
                gate, served, (((0,), (0,)), ((), ())), preferred_element_type=F32
            )
    out_ref[...] = total.astype(BF)

    def sent(i, carry):
        row_copy(i).wait_send()
        back_copy(i).wait_send()
        return carry

    lax.fori_loop(1, 64, sent, 0)

    def sent_heads(i, carry):
        own, away, local = head_copies(i)

        @pl.when(jnp.logical_not(own))
        def _():
            for copy in away:
                copy.wait_send()

        return carry

    lax.fori_loop(0, 8, sent_heads, 0)

    def sent_out(i, carry):
        away, local = out_copy(i)

        @pl.when(i != head)
        def _():
            away.wait_send()

        return carry

    lax.fori_loop(0, 16, sent_out, 0)
    for copy in (k_right, k_left, v_right, v_left, k_on, v_on):
        copy.wait_send()
    for slot in range(4):
        for copy in to_sibling(slot):
            copy.wait_send()
    for copy in (w_across, w_beside, w_on):
        copy.wait_send()
    for copy in e_beside:
        copy.wait_send()


def layer(hit, gain_attn, wq, wk, wv, wo, gain, wr, w_gate, w_up, w_down, routes):
    experts = wr.shape[1]
    rows = routes.shape[0]
    cap = 8
    dma = pltpu.SemaphoreType.DMA
    return pl.pallas_call(
        layer_kernel,
        out_shape=jax.ShapeDtypeStruct((rows, D), BF),
        in_specs=[
            anywhere(),
            whole(),
            anywhere(),
            anywhere(),
            anywhere(),
            anywhere(),
            whole(),
            whole(),
            whole(),
            anywhere(),
            anywhere(),
            anywhere(),
        ],
        out_specs=whole(),
        scratch_shapes=[
            VMEM(hit.shape, BF),
            VMEM(wq.shape, BF),
            VMEM(wk.shape, BF),
            VMEM(wv.shape, BF),
            VMEM((2, 4, HD, 256), BF),
            VMEM((4, 2, 128, 128), BF),
            VMEM((4, 2, 2, HD, 128), BF),
            VMEM((8, HD, 256), BF),
            VMEM((4, 2, 1024, 128), BF),
            VMEM((4, 2, 2, HD, 1024), BF),
            VMEM((8, 2, 128, 256), BF),
            VMEM((2, 2, 1024, 256), F32),
            VMEM((8, HD, 256), F32),
            VMEM((8, 1, 256), F32),
            VMEM((8, 1, 256), F32),
            VMEM((8, 2, HD, 128), BF),
            VMEM((16, HD, 128), BF),
            VMEM((4,) + wo.shape, BF),
            VMEM((2,) + w_gate.shape, BF),
            VMEM((2,) + w_up.shape, BF),
            VMEM((2,) + w_down.shape, BF),
            VMEM((experts, cap, D), BF),
            VMEM((64, 2, cap, D), BF),
            VMEM((64, 2, cap, D), BF),
            VMEM((2, experts, cap, D), BF),
            dma((4,)),
            dma((3, 8)),
            dma((3, 8)),
            dma((2, 3)),
            dma((2, 3)),
            dma((2, 4)),
            dma((2, 4)),
            dma((16,)),
            dma((16,)),
            dma((3,)),
            dma((3,)),
            dma,
            dma((3,)),
            dma((3,)),
            dma((3,)),
            dma((64,)),
            dma((64,)),
            dma((64,)),
            dma((64,)),
        ],
        compiler_params=pltpu.CompilerParams(
            collective_id=0, has_side_effects=True, vmem_limit_bytes=60 << 20
        ),
        name="layer",
    )(
        hit,
        gain_attn.reshape(1, D),
        wq,
        wk,
        wv,
        wo,
        gain.reshape(1, D),
        wr.T,
        routes.T,
        w_gate,
        w_up,
        w_down,
    )


def solution(mesh):
    return jax.shard_map(
        layer,
        mesh=mesh,
        in_specs=(
            P("ctx", None),
            P(),
            P(None, "exp"),
            P(None, "exp"),
            P(None, "exp"),
            P("exp", None),
            P(),
            P(),
            P("ctx", None, "exp"),
            P("ctx", None, "exp"),
            P("ctx", "exp", None),
            P(("ctx", "exp"), None),
        ),
        out_specs=P(("ctx", "exp"), None),
        check_vma=False,
    )
```

```python
import functools
import math

import jax
import jax.numpy as jnp
from jax import lax
from jax.experimental import pallas as pl
from jax.experimental.pallas import tpu as pltpu
from jax.sharding import PartitionSpec as P

D = 1024
HD = 64
EPSILON = 1e-05
LOWEST = -1e30
ALPHA = math.log2(math.e) / math.sqrt(HD)
BF = jnp.bfloat16
F32 = jnp.float32
MESH = pl.DeviceIdType.MESH
VMEM = pltpu.VMEM


def whole():
    return pl.BlockSpec(memory_space=pltpu.VMEM)


def anywhere():
    return pl.BlockSpec(memory_space=pl.ANY)


def shifted(i, sign, ctx, exp):
    o = (i * 11) % 32
    ylo, x, z, yhi = ctx // 16, (ctx // 4) % 4, ctx % 4, exp // 2
    to_x = (x + 4 + sign * (o % 4)) % 4
    to_y = (yhi * 2 + ylo + 4 + sign * (((o // 4) % 2) * 2 + i // 32)) % 4
    to_z = (z + 4 + sign * (o // 8)) % 4
    to_ctx = (to_y % 2) * 16 + to_x * 4 + to_z
    return to_ctx, (to_y // 2) * 2 + exp % 2


def layer_kernel(
    hit_hbm,
    gain_attn_ref,
    wq_hbm,
    wk_hbm,
    wv_hbm,
    wo_ref,
    gain_ref,
    wr_ref,
    routes_ref,
    gate_ref,
    up_ref,
    down_ref,
    out_ref,
    x_ref,
    wq_ref,
    wk_ref,
    wv_ref,
    qt_ref,
    kp_ref,
    vt_ref,
    qg,
    kg,
    vg,
    q2,
    s_ref,
    acc,
    mx,
    ls,
    ost,
    at_ref,
    wo_all,
    wg,
    wu,
    wd,
    rows_out,
    got,
    stage,
    back,
    table_ref,
    res_ref,
    normed_ref,
    load,
    x_send,
    x_recv,
    ring_send,
    ring_recv,
    sib_send,
    sib_recv,
    o_send,
    o_recv,
    w_send,
    w_recv,
    w_own,
    e_send,
    e_recv,
    w_sem,
    send,
    recv,
    b_send,
    b_recv,
):
    ctx = lax.axis_index("ctx")
    exp = lax.axis_index("exp")
    ylo = ctx // 16
    x = (ctx // 4) % 4
    z = ctx % 4
    yhi = exp // 2
    core = exp % 2
    mine = ylo * 4 + z

    def device(to_ylo, to_x, to_z, to_yhi, to_core):
        return (to_ylo * 16 + to_x * 4 + to_z, to_yhi * 2 + to_core)

    right = device(ylo, (x + 1) % 4, z, yhi, core)
    left = device(ylo, (x + 3) % 4, z, yhi, core)
    sibling = device(ylo, x, z, yhi, 1 - core)

    barrier = pltpu.get_barrier_semaphore()

    def greet(i, carry):
        pl.semaphore_signal(
            barrier, inc=1, device_id=shifted(i, 1, ctx, exp), device_id_type=MESH
        )
        return carry

    def greet_plane(i, carry):
        to = device(i // 8, x, (i // 2) % 4, i % 2, 1 - core)
        pl.semaphore_signal(barrier, inc=1, device_id=to, device_id_type=MESH)
        return carry

    loads = [
        pltpu.make_async_copy(src, dst, load.at[m])
        for m, (src, dst) in enumerate(
            ((hit_hbm, x_ref), (wq_hbm, wq_ref), (wk_hbm, wk_ref), (wv_hbm, wv_ref))
        )
    ]
    for copy in loads:
        copy.start()
    lax.fori_loop(0, 16, greet_plane, 0)
    lax.fori_loop(1, 64, greet, 0)

    for copy in loads[:2]:
        copy.wait()
    xs = x_ref[...].astype(F32)
    inv = lax.rsqrt(jnp.mean(xs * xs, axis=-1, keepdims=True) + EPSILON)
    n = (xs * inv * gain_attn_ref[...]).astype(BF)
    qt = jnp.dot(n, wq_ref[...], preferred_element_type=F32).T.astype(BF)
    for head in range(4):
        for block in range(4):
            qt_ref[block % 2, head, :, (block // 2) * 128 : (block // 2) * 128 + 128] = qt[
                head * HD : head * HD + HD, block * 128 : block * 128 + 128
            ]
    loads[2].wait()
    k = jnp.dot(n, wk_ref[...], preferred_element_type=F32)
    for head in range(4):
        for half in range(2):
            kh = k[half * 256 : half * 256 + 256, head * HD : head * HD + HD]
            kp_ref[head, half] = jnp.concatenate([kh[0:128], kh[128:256]], axis=1).astype(BF)
    loads[3].wait()
    vt = jnp.dot(n, wv_ref[...], preferred_element_type=F32).T.astype(BF)
    for head in range(4):
        for half in range(2):
            for u in range(2):
                at = half * 256 + u * 128
                vt_ref[head, half, u] = vt[head * HD : head * HD + HD, at : at + 128]

    pl.semaphore_wait(barrier, 79)

    def head_copies(i):
        head, half = (z + 1 + i // 2) % 4, i % 2
        to = device(core, x, head, yhi, half)
        parts = (
            (qt_ref.at[half, head], qg.at[mine]),
            (kp_ref.at[head, half], kg.at[0, half, pl.ds(pl.multiple_of(mine * 128, 128), 128), :]),
            (
                vt_ref.at[head, half],
                vg.at[0, half, :, :, pl.ds(pl.multiple_of(mine * 128, 128), 128)],
            ),
        )
        own = (core == ylo) & (head == z) & (half == core)
        remote = [
            pltpu.make_async_remote_copy(
                src_ref=src,
                dst_ref=dst,
                send_sem=x_send.at[n, i],
                recv_sem=x_recv.at[n, mine],
                device_id=to,
                device_id_type=MESH,
            )
            for n, (src, dst) in enumerate(parts)
        ]
        local = [
            pltpu.make_async_copy(src, dst, x_recv.at[n, mine])
            for n, (src, dst) in enumerate(parts)
        ]
        return own, remote, local

    def send_heads(i, carry):
        own, remote, local = head_copies(i)

        @pl.when(own)
        def _():
            for copy in local:
                copy.start()

        @pl.when(jnp.logical_not(own))
        def _():
            for copy in remote:
                copy.start()

        return carry

    lax.fori_loop(0, 8, send_heads, 0)

    rows = at_ref.shape[2]
    experts, cap = rows_out.shape[0], rows_out.shape[1]
    places = experts * cap
    ids = lax.broadcasted_iota(jnp.int32, (experts, rows), 0)
    picks = (routes_ref[0:1, :] == ids) | (routes_ref[1:2, :] == ids)
    marks = jnp.where(picks, 1.0, 0.0).astype(BF)
    before = lax.broadcasted_iota(jnp.int32, (rows, rows), 0) < lax.broadcasted_iota(
        jnp.int32, (rows, rows), 1
    )
    slots = jnp.dot(
        marks, jnp.where(before, 1.0, 0.0).astype(BF), preferred_element_type=F32
    ).astype(BF)
    spread = jnp.where(
        lax.broadcasted_iota(jnp.int32, (places, experts), 0) // cap
        == lax.broadcasted_iota(jnp.int32, (places, experts), 1),
        1.0,
        0.0,
    ).astype(BF)
    wide = lambda v: jnp.dot(spread, v, preferred_element_type=F32)
    order = (lax.broadcasted_iota(jnp.int32, (places, rows), 0) % cap).astype(F32)
    here = (wide(marks) > 0.5) & (wide(slots) == order)
    table_ref[...] = jnp.where(here, 1.0, 0.0).astype(BF)

    def await_heads(j, carry):
        pltpu.make_async_copy(qg.at[j], qg.at[j], x_recv.at[0, j]).wait()
        at = pl.ds(pl.multiple_of(j * 128, 128), 128)
        kd = kg.at[0, core, at, :]
        pltpu.make_async_copy(kd, kd, x_recv.at[1, j]).wait()
        vd = vg.at[0, core, :, :, at]
        pltpu.make_async_copy(vd, vd, x_recv.at[2, j]).wait()
        return carry

    lax.fori_loop(0, 8, await_heads, 0)

    def remote(src, dst, send, recv, to):
        return pltpu.make_async_remote_copy(
            src_ref=src,
            dst_ref=dst,
            send_sem=send,
            recv_sem=recv,
            device_id=to,
            device_id_type=MESH,
        )

    def to_sibling(slot):
        return [
            remote(g.at[slot, core], g.at[slot, core], sib_send.at[n, slot], sib_recv.at[n, slot], sibling)
            for n, g in enumerate((kg, vg))
        ]

    def from_sibling(slot):
        return [
            remote(g.at[slot, 1 - core], g.at[slot, 1 - core], sib_send.at[n, slot], sib_recv.at[n, slot], sibling)
            for n, g in enumerate((kg, vg))
        ]

    k_right = remote(kg.at[0, core], kg.at[1, core], ring_send.at[0, 0], ring_recv.at[0, 0], right)
    v_right = remote(vg.at[0, core], vg.at[1, core], ring_send.at[1, 0], ring_recv.at[1, 0], right)
    k_left = remote(kg.at[0, core], kg.at[2, core], ring_send.at[0, 1], ring_recv.at[0, 1], left)
    v_left = remote(vg.at[0, core], vg.at[2, core], ring_send.at[1, 1], ring_recv.at[1, 1], left)
    k_on = remote(kg.at[1, core], kg.at[3, core], ring_send.at[0, 2], ring_recv.at[0, 2], right)
    v_on = remote(vg.at[2, core], vg.at[3, core], ring_send.at[1, 2], ring_recv.at[1, 2], left)
    for copy in (k_right, k_left, v_right, v_left):
        copy.start()
    for copy in to_sibling(0):
        copy.start()

    far_chip = device(ylo, x, z, 1 - yhi, core)
    far_exp = (exp + 2) % 4
    w_local = pltpu.make_async_copy(wo_ref, wo_all.at[exp], w_own)
    w_across = remote(wo_ref, wo_all.at[exp], w_send.at[0], w_recv.at[0], far_chip)
    w_beside = remote(wo_ref, wo_all.at[exp], w_send.at[1], w_recv.at[1], sibling)
    w_on = remote(
        wo_all.at[far_exp], wo_all.at[far_exp], w_send.at[2], w_recv.at[2], sibling
    )
    w_across.start()
    w_beside.start()
    w_local.start()
    e_beside = [
        remote(src, dst, e_send.at[n], e_recv.at[n], sibling)
        for n, (src, dst) in enumerate(
            ((gate_ref, wg.at[1]), (up_ref, wu.at[1]), (down_ref, wd.at[1]))
        )
    ]
    weight_loads = [
        pltpu.make_async_copy(src, dst.at[0], w_sem.at[n])
        for n, (src, dst) in enumerate(((gate_ref, wg), (up_ref, wu), (down_ref, wd)))
    ]
    for copy in weight_loads:
        copy.start()
    for copy in e_beside:
        copy.start()

    zero = jnp.zeros((HD, 256), BF)
    for j in range(8):
        q2[j, 0, 0:HD] = qg[j]
        q2[j, 0, HD : 2 * HD] = zero
        q2[j, 1, 0:HD] = zero
        q2[j, 1, HD : 2 * HD] = qg[j]
    acc[...] = jnp.zeros_like(acc)
    mx[...] = jnp.full_like(mx, LOWEST)
    ls[...] = jnp.zeros_like(ls)

    def score(phase, tile, p):
        j = (tile // 4) * 4 + (tile + z) % 4
        keys = kg[phase // 2, (phase + core) % 2]
        for u in range(2):
            s_ref[p, u] = lax.dot_general(
                keys, q2[j, u], (((1,), (0,)), ((), ())), preferred_element_type=F32
            )

    def absorb(phase, tile, p):
        j = (tile // 4) * 4 + (tile + z) % 4
        s0 = s_ref[p, 0]
        s1 = s_ref[p, 1]
        old = mx[j]
        new = jnp.maximum(
            old,
            jnp.maximum(jnp.max(s0, axis=0, keepdims=True), jnp.max(s1, axis=0, keepdims=True)),
        )
        fade = jnp.exp2((old - new) * ALPHA)
        e0 = jnp.exp2((s0 - new) * ALPHA)
        e1 = jnp.exp2((s1 - new) * ALPHA)
        slot, half = phase // 2, (phase + core) % 2
        ls[j] = ls[j] * fade + (
            jnp.sum(e0, axis=0, keepdims=True) + jnp.sum(e1, axis=0, keepdims=True)
        )
        acc[j] = acc[j] * fade + (
            jnp.dot(vg[slot, half, 0], e0.astype(BF), preferred_element_type=F32)
            + jnp.dot(vg[slot, half, 1], e1.astype(BF), preferred_element_type=F32)
        )
        mx[j] = new

    head = yhi * 8 + mine

    def out_copy(i):
        j, to_yhi = i % 8, i // 8
        to = device(j // 4, x, j % 4, to_yhi, core)
        return (
            remote(ost.at[j, to_yhi], at_ref.at[head], o_send.at[i], o_recv.at[head], to),
            pltpu.make_async_copy(ost.at[j, to_yhi], at_ref.at[head], o_recv.at[head]),
        )

    def send_out(tile):
        j = (tile // 4) * 4 + (tile + z) % 4
        o = (acc[j] / ls[j]).astype(BF)
        ost[j, 0] = o[:, 0:128]
        ost[j, 1] = o[:, 128:256]
        for to_yhi in range(2):
            i = to_yhi * 8 + j
            away, local = out_copy(i)

            @pl.when(i == head)
            def _(local=local):
                local.start()

            @pl.when(i != head)
            def _(away=away):
                away.start()

    score(0, 0, 0)

    def pair(n):
        return pl.ds(pl.multiple_of(2 * n, 2), 2)

    def row_copy(i):
        to = shifted(i, 1, ctx, exp)
        return pltpu.make_async_remote_copy(
            src_ref=rows_out.at[pair(to[0])],
            dst_ref=got.at[i],
            send_sem=send.at[i],
            recv_sem=recv.at[i],
            device_id=to,
            device_id_type=MESH,
        )

    def back_copy(i):
        return pltpu.make_async_remote_copy(
            src_ref=stage.at[i],
            dst_ref=back.at[yhi, pair(ctx)],
            send_sem=b_send.at[i],
            recv_sem=b_recv.at[i],
            device_id=shifted(i, -1, ctx, exp),
            device_id_type=MESH,
        )

    def route_rows():
        def await_out(i, carry):
            pltpu.make_async_copy(at_ref.at[i], at_ref.at[i], o_recv.at[i]).wait()
            return carry

        lax.fori_loop(0, 16, await_out, 0)
        w_local.wait()
        w_beside.wait_recv()
        w_on.wait_recv()
        mixed = lax.dot_general(
            at_ref[...].reshape(D, rows),
            wo_all[...].reshape(D, D),
            (((0,), (0,)), ((), ())),
            preferred_element_type=F32,
        )
        own_rows = x_ref[pl.ds(pl.multiple_of(exp * rows, rows), rows), :]
        residual = own_rows.astype(F32) + mixed
        inv = lax.rsqrt(jnp.mean(residual * residual, axis=-1, keepdims=True) + EPSILON)
        res_ref[...] = residual
        normed = (residual * inv * gain_ref[...]).astype(BF)
        normed_ref[...] = normed
        picked = jnp.dot(table_ref[...], normed, preferred_element_type=F32)
        rows_out[...] = picked.reshape(rows_out.shape).astype(BF)
        pltpu.make_async_copy(rows_out.at[pair(ctx)], got.at[0], recv.at[0]).start()

        def send_rows(i, carry):
            row_copy((i % 2) * 32 + i // 2).start()
            return carry

        lax.fori_loop(1, 64, send_rows, 0)

    def step_of(g):
        late = jnp.minimum(g // 8, 1)
        k = jnp.maximum(g - 8, 0)
        phase = (1 - late) * (g // 4) + late * (2 + (k % 12) // 2)
        pair = (1 - late) * (g % 4) + late * ((k // 12) * 2 + k % 2)
        return phase, pair

    def turn(g, carry):
        phase, pair = step_of(g)

        for slot, at in ((0, 3), (1, 9), (2, 13), (3, 17)):

            @pl.when(g == at)
            def _(slot=slot):
                for copy in from_sibling(slot):
                    copy.wait_recv()

        @pl.when(g == 7)
        def _():
            for copy in (k_right, k_left, v_right, v_left):
                copy.wait_recv()
            k_on.start()
            v_on.start()
            for slot in (1, 2):
                for copy in to_sibling(slot):
                    copy.start()

        @pl.when(g == 15)
        def _():
            k_on.wait_recv()
            v_on.wait_recv()
            for copy in to_sibling(3):
                copy.start()
            w_across.wait_recv()
            w_on.start()

        @pl.when((g == 23) & (ylo == 0))
        def _():
            route_rows()

        score(phase, 2 * pair + 1, 1)
        absorb(phase, 2 * pair, 0)
        later = jnp.minimum(g + 1, 31)
        next_phase, next_pair = step_of(later)
        score(next_phase, 2 * next_pair, 0)
        absorb(phase, 2 * pair + 1, 1)

        @pl.when(phase == 7)
        def _():
            send_out(2 * pair)
            send_out(2 * pair + 1)

        return carry

    lax.fori_loop(0, 32, turn, 0)

    @pl.when(ylo == 1)
    def _():
        route_rows()


    normed = normed_ref[...]
    here = table_ref[...].astype(F32) > 0.5
    logits = lax.dot_general(
        wr_ref[...], normed, (((1,), (1,)), ((), ())), preferred_element_type=F32
    )
    top = jnp.max(jnp.where(picks, logits, -jnp.inf), axis=0, keepdims=True)
    weights = jnp.where(picks, jnp.exp(jnp.where(picks, logits - top, 0.0)), 0.0)
    gates = weights / jnp.sum(weights, axis=0, keepdims=True)
    gate_hi = gates.astype(BF)
    gate_lo = (gates - gate_hi.astype(F32)).astype(BF)
    hi = jnp.where(here, wide(gate_hi), 0.0).astype(BF)
    lo = jnp.where(here, wide(gate_lo), 0.0).astype(BF)
    for copy in weight_loads:
        copy.wait()
    for copy in e_beside:
        copy.wait_recv()

    group = 32

    def serve(g, carry):
        first = ((ylo + g) % 2) * group

        def await_rows(i, carry):
            pltpu.make_async_copy(got.at[first + i], got.at[first + i], recv.at[first + i]).wait()
            return carry

        lax.fori_loop(0, group, await_rows, 0)
        at = pl.ds(pl.multiple_of(first, group), group)

        def expert(j, carry):
            mine = got[at, j].astype(F32).reshape(group * cap, D).astype(BF)
            total = None
            for q in range(2):
                gate = jnp.dot(mine, wg[q, j], preferred_element_type=F32)
                up = jnp.dot(mine, wu[q, j], preferred_element_type=F32)
                hidden = (gate / (1.0 + jnp.exp(-gate)) * up).astype(BF)
                part = jnp.dot(hidden, wd[q, j], preferred_element_type=F32)
                total = part if total is None else total + part
            stage[at, j] = total.reshape(group, cap, D).astype(BF)
            return carry

        lax.fori_loop(0, 2, expert, 0)

        @pl.when(first == 0)
        def _():
            pltpu.make_async_copy(stage.at[0], back.at[yhi, pair(ctx)], b_recv.at[0]).start()

        def send_back(i, carry):
            @pl.when(first + i > 0)
            def _():
                back_copy(first + i).start()

            return carry

        lax.fori_loop(0, group, send_back, 0)
        return carry

    lax.fori_loop(0, 2, serve, 0)

    def await_back(i, carry):
        from_ctx, from_exp = shifted(i, 1, ctx, exp)
        block = back.at[from_exp // 2, pair(from_ctx)]
        pltpu.make_async_copy(block, block, b_recv.at[i]).wait()
        return carry

    lax.fori_loop(0, 64, await_back, 0)
    total = res_ref[...]
    for n in range(2):
        served = back[n].astype(F32).reshape(places, D).astype(BF)
        for gate in (hi, lo):
            total = total + lax.dot_general(
                gate, served, (((0,), (0,)), ((), ())), preferred_element_type=F32
            )
    out_ref[...] = total.astype(BF)

    def sent(i, carry):
        row_copy(i).wait_send()
        back_copy(i).wait_send()
        return carry

    lax.fori_loop(1, 64, sent, 0)

    def sent_heads(i, carry):
        own, away, local = head_copies(i)

        @pl.when(jnp.logical_not(own))
        def _():
            for copy in away:
                copy.wait_send()

        return carry

    lax.fori_loop(0, 8, sent_heads, 0)

    def sent_out(i, carry):
        away, local = out_copy(i)

        @pl.when(i != head)
        def _():
            away.wait_send()

        return carry

    lax.fori_loop(0, 16, sent_out, 0)
    for copy in (k_right, k_left, v_right, v_left, k_on, v_on):
        copy.wait_send()
    for slot in range(4):
        for copy in to_sibling(slot):
            copy.wait_send()
    for copy in (w_across, w_beside, w_on):
        copy.wait_send()
    for copy in e_beside:
        copy.wait_send()


def layer(hit, gain_attn, wq, wk, wv, wo, gain, wr, w_gate, w_up, w_down, routes):
    experts = wr.shape[1]
    rows = routes.shape[0]
    cap = 8
    dma = pltpu.SemaphoreType.DMA
    return pl.pallas_call(
        layer_kernel,
        out_shape=jax.ShapeDtypeStruct((rows, D), BF),
        in_specs=[
            anywhere(),
            whole(),
            anywhere(),
            anywhere(),
            anywhere(),
            anywhere(),
            whole(),
            whole(),
            whole(),
            anywhere(),
            anywhere(),
            anywhere(),
        ],
        out_specs=whole(),
        scratch_shapes=[
            VMEM(hit.shape, BF),
            VMEM(wq.shape, BF),
            VMEM(wk.shape, BF),
            VMEM(wv.shape, BF),
            VMEM((2, 4, HD, 256), BF),
            VMEM((4, 2, 128, 128), BF),
            VMEM((4, 2, 2, HD, 128), BF),
            VMEM((8, HD, 256), BF),
            VMEM((4, 2, 1024, 128), BF),
            VMEM((4, 2, 2, HD, 1024), BF),
            VMEM((8, 2, 128, 256), BF),
            VMEM((2, 2, 1024, 256), F32),
            VMEM((8, HD, 256), F32),
            VMEM((8, 1, 256), F32),
            VMEM((8, 1, 256), F32),
            VMEM((8, 2, HD, 128), BF),
            VMEM((16, HD, 128), BF),
            VMEM((4,) + wo.shape, BF),
            VMEM((2,) + w_gate.shape, BF),
            VMEM((2,) + w_up.shape, BF),
            VMEM((2,) + w_down.shape, BF),
            VMEM((experts, cap, D), BF),
            VMEM((64, 2, cap, D), BF),
            VMEM((64, 2, cap, D), BF),
            VMEM((2, experts, cap, D), BF),
            VMEM((experts * cap, rows), BF),
            VMEM((rows, D), F32),
            VMEM((rows, D), BF),
            dma((4,)),
            dma((3, 8)),
            dma((3, 8)),
            dma((2, 3)),
            dma((2, 3)),
            dma((2, 4)),
            dma((2, 4)),
            dma((16,)),
            dma((16,)),
            dma((3,)),
            dma((3,)),
            dma,
            dma((3,)),
            dma((3,)),
            dma((3,)),
            dma((64,)),
            dma((64,)),
            dma((64,)),
            dma((64,)),
        ],
        compiler_params=pltpu.CompilerParams(
            collective_id=0, has_side_effects=True, vmem_limit_bytes=60 << 20
        ),
        name="layer",
    )(
        hit,
        gain_attn.reshape(1, D),
        wq,
        wk,
        wv,
        wo,
        gain.reshape(1, D),
        wr.T,
        routes.T,
        w_gate,
        w_up,
        w_down,
    )


def solution(mesh):
    return jax.shard_map(
        layer,
        mesh=mesh,
        in_specs=(
            P("ctx", None),
            P(),
            P(None, "exp"),
            P(None, "exp"),
            P(None, "exp"),
            P("exp", None),
            P(),
            P(),
            P("ctx", None, "exp"),
            P("ctx", None, "exp"),
            P("ctx", "exp", None),
            P(("ctx", "exp"), None),
        ),
        out_specs=P(("ctx", "exp"), None),
        check_vma=False,
    )
```

```python
import functools
import math

import jax
import jax.numpy as jnp
from jax import lax
from jax.experimental import pallas as pl
from jax.experimental.pallas import tpu as pltpu
from jax.sharding import PartitionSpec as P

D = 1024
HD = 64
EPSILON = 1e-05
LOWEST = -1e30
ALPHA = math.log2(math.e) / math.sqrt(HD)
BF = jnp.bfloat16
F32 = jnp.float32
MESH = pl.DeviceIdType.MESH
VMEM = pltpu.VMEM


def whole():
    return pl.BlockSpec(memory_space=pltpu.VMEM)


def anywhere():
    return pl.BlockSpec(memory_space=pl.ANY)


def shifted(i, sign, ctx, exp):
    o = (i * 27) % 64
    ylo, x, z, yhi = ctx // 16, (ctx // 4) % 4, ctx % 4, exp // 2
    to_x = (x + 4 + sign * (o % 4)) % 4
    to_y = (yhi * 2 + ylo + 4 + sign * ((o // 4) % 4)) % 4
    to_z = (z + 4 + sign * (o // 16)) % 4
    to_ctx = (to_y % 2) * 16 + to_x * 4 + to_z
    return to_ctx, (to_y // 2) * 2 + exp % 2


def layer_kernel(
    hit_hbm,
    gain_attn_ref,
    wq_hbm,
    wk_hbm,
    wv_hbm,
    wo_ref,
    gain_ref,
    wr_ref,
    routes_ref,
    gate_ref,
    up_ref,
    down_ref,
    out_ref,
    x_ref,
    wq_ref,
    wk_ref,
    wv_ref,
    qt_ref,
    kp_ref,
    vt_ref,
    qg,
    kg,
    vg,
    q2,
    s_ref,
    acc,
    mx,
    ls,
    ost,
    at_ref,
    wo_all,
    wg,
    wu,
    wd,
    rows_out,
    got,
    stage,
    back,
    table_ref,
    res_ref,
    normed_ref,
    load,
    x_send,
    x_recv,
    ring_send,
    ring_recv,
    sib_send,
    sib_recv,
    o_send,
    o_recv,
    w_send,
    w_recv,
    w_own,
    e_send,
    e_recv,
    w_sem,
    send,
    recv,
    b_send,
    b_recv,
):
    ctx = lax.axis_index("ctx")
    exp = lax.axis_index("exp")
    ylo = ctx // 16
    x = (ctx // 4) % 4
    z = ctx % 4
    yhi = exp // 2
    core = exp % 2
    mine = ylo * 4 + z

    def device(to_ylo, to_x, to_z, to_yhi, to_core):
        return (to_ylo * 16 + to_x * 4 + to_z, to_yhi * 2 + to_core)

    right = device(ylo, (x + 1) % 4, z, yhi, core)
    left = device(ylo, (x + 3) % 4, z, yhi, core)
    sibling = device(ylo, x, z, yhi, 1 - core)

    barrier = pltpu.get_barrier_semaphore()

    def greet(i, carry):
        pl.semaphore_signal(
            barrier, inc=1, device_id=shifted(i, 1, ctx, exp), device_id_type=MESH
        )
        return carry

    def greet_plane(i, carry):
        to = device(i // 8, x, (i // 2) % 4, i % 2, 1 - core)
        pl.semaphore_signal(barrier, inc=1, device_id=to, device_id_type=MESH)
        return carry

    loads = [
        pltpu.make_async_copy(src, dst, load.at[m])
        for m, (src, dst) in enumerate(
            ((hit_hbm, x_ref), (wq_hbm, wq_ref), (wk_hbm, wk_ref), (wv_hbm, wv_ref))
        )
    ]
    for copy in loads:
        copy.start()
    lax.fori_loop(0, 16, greet_plane, 0)
    lax.fori_loop(1, 64, greet, 0)

    for copy in loads[:2]:
        copy.wait()
    xs = x_ref[...].astype(F32)
    inv = lax.rsqrt(jnp.mean(xs * xs, axis=-1, keepdims=True) + EPSILON)
    n = (xs * inv * gain_attn_ref[...]).astype(BF)
    qt = jnp.dot(n, wq_ref[...], preferred_element_type=F32).T.astype(BF)
    for head in range(4):
        for block in range(4):
            qt_ref[block % 2, head, :, (block // 2) * 128 : (block // 2) * 128 + 128] = qt[
                head * HD : head * HD + HD, block * 128 : block * 128 + 128
            ]
    loads[2].wait()
    k = jnp.dot(n, wk_ref[...], preferred_element_type=F32)
    for head in range(4):
        for half in range(2):
            kh = k[half * 256 : half * 256 + 256, head * HD : head * HD + HD]
            kp_ref[head, half] = jnp.concatenate([kh[0:128], kh[128:256]], axis=1).astype(BF)
    loads[3].wait()
    vt = jnp.dot(n, wv_ref[...], preferred_element_type=F32).T.astype(BF)
    for head in range(4):
        for half in range(2):
            for u in range(2):
                at = half * 256 + u * 128
                vt_ref[head, half, u] = vt[head * HD : head * HD + HD, at : at + 128]

    pl.semaphore_wait(barrier, 79)

    def head_copies(i):
        head, half = (z + 1 + i // 2) % 4, i % 2
        at = pl.ds(pl.multiple_of(mine * 128, 128), 128)
        parts = (
            (qt_ref.at[half, head], qg.at[half * 4 + z], half * 4 + z, ylo),
            (kp_ref.at[head, half], kg.at[0, half, at, :], mine, half),
            (vt_ref.at[head, half], vg.at[0, half, :, :, at], mine, half),
        )
        here = (core == ylo) & (head == z)
        own = [here, here & (half == core), here & (half == core)]
        away = [
            pltpu.make_async_remote_copy(
                src_ref=src,
                dst_ref=dst,
                send_sem=x_send.at[n, i],
                recv_sem=x_recv.at[n, at_sem],
                device_id=device(core, x, head, yhi, to_core),
                device_id_type=MESH,
            )
            for n, (src, dst, at_sem, to_core) in enumerate(parts)
        ]
        local = [
            pltpu.make_async_copy(src, dst, x_recv.at[n, at_sem])
            for n, (src, dst, at_sem, to_core) in enumerate(parts)
        ]
        return own, away, local

    def send_heads(i, carry):
        for own, away, local in zip(*head_copies(i)):

            @pl.when(own)
            def _(local=local):
                local.start()

            @pl.when(jnp.logical_not(own))
            def _(away=away):
                away.start()

        return carry

    lax.fori_loop(0, 8, send_heads, 0)

    rows = at_ref.shape[2]
    experts, cap = rows_out.shape[0], rows_out.shape[1]
    places = experts * cap
    ids = lax.broadcasted_iota(jnp.int32, (experts, rows), 0)
    picks = (routes_ref[0:1, :] == ids) | (routes_ref[1:2, :] == ids)
    marks = jnp.where(picks, 1.0, 0.0).astype(BF)
    before = lax.broadcasted_iota(jnp.int32, (rows, rows), 0) < lax.broadcasted_iota(
        jnp.int32, (rows, rows), 1
    )
    slots = jnp.dot(
        marks, jnp.where(before, 1.0, 0.0).astype(BF), preferred_element_type=F32
    ).astype(BF)
    spread = jnp.where(
        lax.broadcasted_iota(jnp.int32, (places, experts), 0) // cap
        == lax.broadcasted_iota(jnp.int32, (places, experts), 1),
        1.0,
        0.0,
    ).astype(BF)
    wide = lambda v: jnp.dot(spread, v, preferred_element_type=F32)
    order = (lax.broadcasted_iota(jnp.int32, (places, rows), 0) % cap).astype(F32)
    here = (wide(marks) > 0.5) & (wide(slots) == order)
    table_ref[...] = jnp.where(here, 1.0, 0.0).astype(BF)

    def await_heads(j, carry):
        pltpu.make_async_copy(qg.at[j], qg.at[j], x_recv.at[0, j]).wait()
        at = pl.ds(pl.multiple_of(j * 128, 128), 128)
        kd = kg.at[0, core, at, :]
        pltpu.make_async_copy(kd, kd, x_recv.at[1, j]).wait()
        vd = vg.at[0, core, :, :, at]
        pltpu.make_async_copy(vd, vd, x_recv.at[2, j]).wait()
        return carry

    lax.fori_loop(0, 8, await_heads, 0)

    def remote(src, dst, send, recv, to):
        return pltpu.make_async_remote_copy(
            src_ref=src,
            dst_ref=dst,
            send_sem=send,
            recv_sem=recv,
            device_id=to,
            device_id_type=MESH,
        )

    def to_sibling(slot):
        return [
            remote(g.at[slot, core], g.at[slot, core], sib_send.at[n, slot], sib_recv.at[n, slot], sibling)
            for n, g in enumerate((kg, vg))
        ]

    def from_sibling(slot):
        return [
            remote(g.at[slot, 1 - core], g.at[slot, 1 - core], sib_send.at[n, slot], sib_recv.at[n, slot], sibling)
            for n, g in enumerate((kg, vg))
        ]

    k_right = remote(kg.at[0, core], kg.at[1, core], ring_send.at[0, 0], ring_recv.at[0, 0], right)
    v_right = remote(vg.at[0, core], vg.at[1, core], ring_send.at[1, 0], ring_recv.at[1, 0], right)
    k_left = remote(kg.at[0, core], kg.at[2, core], ring_send.at[0, 1], ring_recv.at[0, 1], left)
    v_left = remote(vg.at[0, core], vg.at[2, core], ring_send.at[1, 1], ring_recv.at[1, 1], left)
    k_on = remote(kg.at[1, core], kg.at[3, core], ring_send.at[0, 2], ring_recv.at[0, 2], right)
    v_on = remote(vg.at[2, core], vg.at[3, core], ring_send.at[1, 2], ring_recv.at[1, 2], left)
    for copy in (k_right, k_left, v_right, v_left):
        copy.start()
    for copy in to_sibling(0):
        copy.start()

    far_chip = device(ylo, x, z, 1 - yhi, core)
    far_exp = (exp + 2) % 4
    w_local = pltpu.make_async_copy(wo_ref, wo_all.at[exp], w_own)
    w_across = remote(wo_ref, wo_all.at[exp], w_send.at[0], w_recv.at[0], far_chip)
    w_beside = remote(wo_ref, wo_all.at[exp], w_send.at[1], w_recv.at[1], sibling)
    w_on = remote(
        wo_all.at[far_exp], wo_all.at[far_exp], w_send.at[2], w_recv.at[2], sibling
    )
    w_across.start()
    w_beside.start()
    w_local.start()
    e_beside = [
        remote(src, dst, e_send.at[n], e_recv.at[n], sibling)
        for n, (src, dst) in enumerate(
            ((gate_ref, wg.at[1]), (up_ref, wu.at[1]), (down_ref, wd.at[1]))
        )
    ]
    weight_loads = [
        pltpu.make_async_copy(src, dst.at[0], w_sem.at[n])
        for n, (src, dst) in enumerate(((gate_ref, wg), (up_ref, wu), (down_ref, wd)))
    ]
    for copy in weight_loads:
        copy.start()
    for copy in e_beside:
        copy.start()

    zero = jnp.zeros((HD, 256), BF)
    for j in range(8):
        q2[j, 0, 0:HD] = qg[j]
        q2[j, 0, HD : 2 * HD] = zero
        q2[j, 1, 0:HD] = zero
        q2[j, 1, HD : 2 * HD] = qg[j]
    acc[...] = jnp.zeros_like(acc)
    mx[...] = jnp.full_like(mx, LOWEST)
    ls[...] = jnp.zeros_like(ls)

    def score(phase, tile, p):
        j = (tile // 4) * 4 + (tile + z) % 4
        keys = kg[phase // 2, (phase + core) % 2]
        for u in range(2):
            s_ref[p, u] = lax.dot_general(
                keys, q2[j, u], (((1,), (0,)), ((), ())), preferred_element_type=F32
            )

    def absorb(phase, tile, p):
        j = (tile // 4) * 4 + (tile + z) % 4
        s0 = s_ref[p, 0]
        s1 = s_ref[p, 1]
        old = mx[j]
        new = jnp.maximum(
            old,
            jnp.maximum(jnp.max(s0, axis=0, keepdims=True), jnp.max(s1, axis=0, keepdims=True)),
        )
        fade = jnp.exp2((old - new) * ALPHA)
        e0 = jnp.exp2((s0 - new) * ALPHA)
        e1 = jnp.exp2((s1 - new) * ALPHA)
        slot, half = phase // 2, (phase + core) % 2
        ls[j] = ls[j] * fade + (
            jnp.sum(e0, axis=0, keepdims=True) + jnp.sum(e1, axis=0, keepdims=True)
        )
        acc[j] = acc[j] * fade + (
            jnp.dot(vg[slot, half, 0], e0.astype(BF), preferred_element_type=F32)
            + jnp.dot(vg[slot, half, 1], e1.astype(BF), preferred_element_type=F32)
        )
        mx[j] = new

    head = yhi * 8 + mine

    def out_copy(i):
        j, to_yhi = i % 8, i // 8
        to = device(core, x, j % 4, to_yhi, j // 4)
        own = (core == ylo) & (j % 4 == z) & (to_yhi == yhi) & (j // 4 == core)
        return (
            own,
            remote(ost.at[j, to_yhi], at_ref.at[head], o_send.at[i], o_recv.at[head], to),
            pltpu.make_async_copy(ost.at[j, to_yhi], at_ref.at[head], o_recv.at[head]),
        )

    def send_out(tile):
        j = (tile // 4) * 4 + (tile + z) % 4
        o = (acc[j] / ls[j]).astype(BF)
        ost[j, 0] = o[:, 0:128]
        ost[j, 1] = o[:, 128:256]
        for to_yhi in range(2):
            i = to_yhi * 8 + j
            own, away, local = out_copy(i)

            @pl.when(own)
            def _(local=local):
                local.start()

            @pl.when(jnp.logical_not(own))
            def _(away=away):
                away.start()

    score(0, 0, 0)

    def pair(n):
        return pl.ds(pl.multiple_of(2 * n, 2), 2)

    def row_copy(i):
        to = shifted(i, 1, ctx, exp)
        return pltpu.make_async_remote_copy(
            src_ref=rows_out.at[pair(to[0])],
            dst_ref=got.at[i],
            send_sem=send.at[i],
            recv_sem=recv.at[i],
            device_id=to,
            device_id_type=MESH,
        )

    def back_copy(i):
        return pltpu.make_async_remote_copy(
            src_ref=stage.at[i],
            dst_ref=back.at[yhi, pair(ctx)],
            send_sem=b_send.at[i],
            recv_sem=b_recv.at[i],
            device_id=shifted(i, -1, ctx, exp),
            device_id_type=MESH,
        )

    def route_rows():
        def await_out(i, carry):
            pltpu.make_async_copy(at_ref.at[i], at_ref.at[i], o_recv.at[i]).wait()
            return carry

        lax.fori_loop(0, 16, await_out, 0)
        w_local.wait()
        w_beside.wait_recv()
        w_on.wait_recv()
        mixed = lax.dot_general(
            at_ref[...].reshape(D, rows),
            wo_all[...].reshape(D, D),
            (((0,), (0,)), ((), ())),
            preferred_element_type=F32,
        )
        own_rows = x_ref[pl.ds(pl.multiple_of(exp * rows, rows), rows), :]
        residual = own_rows.astype(F32) + mixed
        inv = lax.rsqrt(jnp.mean(residual * residual, axis=-1, keepdims=True) + EPSILON)
        res_ref[...] = residual
        normed = (residual * inv * gain_ref[...]).astype(BF)
        normed_ref[...] = normed
        picked = jnp.dot(table_ref[...], normed, preferred_element_type=F32)
        rows_out[...] = picked.reshape(rows_out.shape).astype(BF)
        pltpu.make_async_copy(rows_out.at[pair(ctx)], got.at[0], recv.at[0]).start()

        def send_rows(i, carry):
            row_copy(i).start()
            return carry

        lax.fori_loop(1, 64, send_rows, 0)

    def step_of(g):
        late = jnp.minimum(g // 8, 1)
        k = jnp.maximum(g - 8, 0)
        phase = (1 - late) * (g // 4) + late * (2 + (k % 12) // 2)
        pair = (1 - late) * (g % 4) + late * ((k // 12) * 2 + k % 2)
        return phase, pair

    def turn(g, carry):
        phase, pair = step_of(g)

        for slot, at in ((0, 3), (1, 9), (2, 13), (3, 17)):

            @pl.when(g == at)
            def _(slot=slot):
                for copy in from_sibling(slot):
                    copy.wait_recv()

        @pl.when(g == 7)
        def _():
            for copy in (k_right, k_left, v_right, v_left):
                copy.wait_recv()
            k_on.start()
            v_on.start()
            for slot in (1, 2):
                for copy in to_sibling(slot):
                    copy.start()

        @pl.when(g == 15)
        def _():
            k_on.wait_recv()
            v_on.wait_recv()
            for copy in to_sibling(3):
                copy.start()
            w_across.wait_recv()
            w_on.start()

        @pl.when((g == 23) & (core == 0))
        def _():
            route_rows()

        score(phase, 2 * pair + 1, 1)
        absorb(phase, 2 * pair, 0)
        later = jnp.minimum(g + 1, 31)
        next_phase, next_pair = step_of(later)
        score(next_phase, 2 * next_pair, 0)
        absorb(phase, 2 * pair + 1, 1)

        @pl.when(phase == 7)
        def _():
            send_out(2 * pair)
            send_out(2 * pair + 1)

        return carry

    lax.fori_loop(0, 32, turn, 0)

    @pl.when(core == 1)
    def _():
        route_rows()


    normed = normed_ref[...]
    here = table_ref[...].astype(F32) > 0.5
    logits = lax.dot_general(
        wr_ref[...], normed, (((1,), (1,)), ((), ())), preferred_element_type=F32
    )
    top = jnp.max(jnp.where(picks, logits, -jnp.inf), axis=0, keepdims=True)
    weights = jnp.where(picks, jnp.exp(jnp.where(picks, logits - top, 0.0)), 0.0)
    gates = weights / jnp.sum(weights, axis=0, keepdims=True)
    gate_hi = gates.astype(BF)
    gate_lo = (gates - gate_hi.astype(F32)).astype(BF)
    hi = jnp.where(here, wide(gate_hi), 0.0).astype(BF)
    lo = jnp.where(here, wide(gate_lo), 0.0).astype(BF)
    for copy in weight_loads:
        copy.wait()
    for copy in e_beside:
        copy.wait_recv()

    group = 32

    def serve(g, carry):
        first = g * group

        def await_rows(i, carry):
            pltpu.make_async_copy(got.at[first + i], got.at[first + i], recv.at[first + i]).wait()
            return carry

        lax.fori_loop(0, group, await_rows, 0)
        at = pl.ds(pl.multiple_of(first, group), group)

        def expert(j, carry):
            mine = got[at, j].astype(F32).reshape(group * cap, D).astype(BF)
            total = None
            for q in range(2):
                gate = jnp.dot(mine, wg[q, j], preferred_element_type=F32)
                up = jnp.dot(mine, wu[q, j], preferred_element_type=F32)
                hidden = (gate / (1.0 + jnp.exp(-gate)) * up).astype(BF)
                part = jnp.dot(hidden, wd[q, j], preferred_element_type=F32)
                total = part if total is None else total + part
            stage[at, j] = total.reshape(group, cap, D).astype(BF)
            return carry

        lax.fori_loop(0, 2, expert, 0)

        @pl.when(first == 0)
        def _():
            pltpu.make_async_copy(stage.at[0], back.at[yhi, pair(ctx)], b_recv.at[0]).start()

        def send_back(i, carry):
            @pl.when(first + i > 0)
            def _():
                back_copy(first + i).start()

            return carry

        lax.fori_loop(0, group, send_back, 0)
        return carry

    lax.fori_loop(0, 2, serve, 0)

    def await_back(i, carry):
        from_ctx, from_exp = shifted(i, 1, ctx, exp)
        block = back.at[from_exp // 2, pair(from_ctx)]
        pltpu.make_async_copy(block, block, b_recv.at[i]).wait()
        return carry

    lax.fori_loop(0, 64, await_back, 0)
    total = res_ref[...]
    for n in range(2):
        served = back[n].astype(F32).reshape(places, D).astype(BF)
        for gate in (hi, lo):
            total = total + lax.dot_general(
                gate, served, (((0,), (0,)), ((), ())), preferred_element_type=F32
            )
    out_ref[...] = total.astype(BF)

    def sent(i, carry):
        row_copy(i).wait_send()
        back_copy(i).wait_send()
        return carry

    lax.fori_loop(1, 64, sent, 0)

    def sent_heads(i, carry):
        for own, away, _ in zip(*head_copies(i)):

            @pl.when(jnp.logical_not(own))
            def _(away=away):
                away.wait_send()

        return carry

    lax.fori_loop(0, 8, sent_heads, 0)

    def sent_out(i, carry):
        own, away, local = out_copy(i)

        @pl.when(jnp.logical_not(own))
        def _():
            away.wait_send()

        return carry

    lax.fori_loop(0, 16, sent_out, 0)
    for copy in (k_right, k_left, v_right, v_left, k_on, v_on):
        copy.wait_send()
    for slot in range(4):
        for copy in to_sibling(slot):
            copy.wait_send()
    for copy in (w_across, w_beside, w_on):
        copy.wait_send()
    for copy in e_beside:
        copy.wait_send()


def layer(hit, gain_attn, wq, wk, wv, wo, gain, wr, w_gate, w_up, w_down, routes):
    experts = wr.shape[1]
    rows = routes.shape[0]
    cap = 8
    dma = pltpu.SemaphoreType.DMA
    return pl.pallas_call(
        layer_kernel,
        out_shape=jax.ShapeDtypeStruct((rows, D), BF),
        in_specs=[
            anywhere(),
            whole(),
            anywhere(),
            anywhere(),
            anywhere(),
            anywhere(),
            whole(),
            whole(),
            whole(),
            anywhere(),
            anywhere(),
            anywhere(),
        ],
        out_specs=whole(),
        scratch_shapes=[
            VMEM(hit.shape, BF),
            VMEM(wq.shape, BF),
            VMEM(wk.shape, BF),
            VMEM(wv.shape, BF),
            VMEM((2, 4, HD, 256), BF),
            VMEM((4, 2, 128, 128), BF),
            VMEM((4, 2, 2, HD, 128), BF),
            VMEM((8, HD, 256), BF),
            VMEM((4, 2, 1024, 128), BF),
            VMEM((4, 2, 2, HD, 1024), BF),
            VMEM((8, 2, 128, 256), BF),
            VMEM((2, 2, 1024, 256), F32),
            VMEM((8, HD, 256), F32),
            VMEM((8, 1, 256), F32),
            VMEM((8, 1, 256), F32),
            VMEM((8, 2, HD, 128), BF),
            VMEM((16, HD, 128), BF),
            VMEM((4,) + wo.shape, BF),
            VMEM((2,) + w_gate.shape, BF),
            VMEM((2,) + w_up.shape, BF),
            VMEM((2,) + w_down.shape, BF),
            VMEM((experts, cap, D), BF),
            VMEM((64, 2, cap, D), BF),
            VMEM((64, 2, cap, D), BF),
            VMEM((2, experts, cap, D), BF),
            VMEM((experts * cap, rows), BF),
            VMEM((rows, D), F32),
            VMEM((rows, D), BF),
            dma((4,)),
            dma((3, 8)),
            dma((3, 8)),
            dma((2, 3)),
            dma((2, 3)),
            dma((2, 4)),
            dma((2, 4)),
            dma((16,)),
            dma((16,)),
            dma((3,)),
            dma((3,)),
            dma,
            dma((3,)),
            dma((3,)),
            dma((3,)),
            dma((64,)),
            dma((64,)),
            dma((64,)),
            dma((64,)),
        ],
        compiler_params=pltpu.CompilerParams(
            collective_id=0, has_side_effects=True, vmem_limit_bytes=60 << 20
        ),
        name="layer",
    )(
        hit,
        gain_attn.reshape(1, D),
        wq,
        wk,
        wv,
        wo,
        gain.reshape(1, D),
        wr.T,
        routes.T,
        w_gate,
        w_up,
        w_down,
    )


def solution(mesh):
    return jax.shard_map(
        layer,
        mesh=mesh,
        in_specs=(
            P("ctx", None),
            P(),
            P(None, "exp"),
            P(None, "exp"),
            P(None, "exp"),
            P("exp", None),
            P(),
            P(),
            P("ctx", None, "exp"),
            P("ctx", None, "exp"),
            P("ctx", "exp", None),
            P(("ctx", "exp"), None),
        ),
        out_specs=P(("ctx", "exp"), None),
        check_vma=False,
    )
```

```python
import functools
import math

import jax
import jax.numpy as jnp
from jax import lax
from jax.experimental import pallas as pl
from jax.experimental.pallas import tpu as pltpu
from jax.sharding import PartitionSpec as P

D = 1024
HD = 64
EPSILON = 1e-05
LOWEST = -1e30
ALPHA = math.log2(math.e) / math.sqrt(HD)
BF = jnp.bfloat16
F32 = jnp.float32
MESH = pl.DeviceIdType.MESH
VMEM = pltpu.VMEM


def whole():
    return pl.BlockSpec(memory_space=pltpu.VMEM)


def anywhere():
    return pl.BlockSpec(memory_space=pl.ANY)


def shifted(i, sign, ctx, exp):
    o = (i * 27) % 64
    ylo, x, z, yhi = ctx // 16, (ctx // 4) % 4, ctx % 4, exp // 2
    to_x = (x + 4 + sign * (o % 4)) % 4
    to_y = (yhi * 2 + ylo + 4 + sign * ((o // 4) % 4)) % 4
    to_z = (z + 4 + sign * (o // 16)) % 4
    to_ctx = (to_y % 2) * 16 + to_x * 4 + to_z
    return to_ctx, (to_y // 2) * 2 + exp % 2


def layer_kernel(
    hit_hbm,
    gain_attn_ref,
    wq_hbm,
    wk_hbm,
    wv_hbm,
    wo_ref,
    gain_ref,
    wr_ref,
    routes_ref,
    gate_ref,
    up_ref,
    down_ref,
    out_ref,
    x_ref,
    wq_ref,
    wk_ref,
    wv_ref,
    qt_ref,
    kp_ref,
    vt_ref,
    qg,
    kg,
    vg,
    q2,
    s_ref,
    acc,
    mx,
    ls,
    ost,
    at_ref,
    wo_all,
    wg,
    wu,
    wd,
    rows_out,
    got,
    stage,
    back,
    table_ref,
    res_ref,
    normed_ref,
    load,
    x_send,
    x_recv,
    ring_send,
    ring_recv,
    sib_send,
    sib_recv,
    o_send,
    o_recv,
    w_send,
    w_recv,
    w_own,
    e_send,
    e_recv,
    w_sem,
    send,
    recv,
    b_send,
    b_recv,
    known,
):
    ctx = lax.axis_index("ctx")
    exp = lax.axis_index("exp")
    ylo = ctx // 16
    x = (ctx // 4) % 4
    z = ctx % 4
    yhi = exp // 2
    core = exp % 2
    mine = ylo * 4 + z

    def device(to_ylo, to_x, to_z, to_yhi, to_core):
        return (to_ylo * 16 + to_x * 4 + to_z, to_yhi * 2 + to_core)

    right = device(ylo, (x + 1) % 4, z, yhi, core)
    left = device(ylo, (x + 3) % 4, z, yhi, core)
    sibling = device(ylo, x, z, yhi, 1 - core)

    barrier = pltpu.get_barrier_semaphore()

    def greet(i, carry):
        @pl.when(i != mine * 2 + core)
        def _():
            to = device(i // 8, x, (i // 2) % 4, yhi, i % 2)
            pl.semaphore_signal(barrier, inc=1, device_id=to, device_id_type=MESH)

        return carry

    far_chip = device(ylo, x, z, 1 - yhi, core)

    def tell(sem, *others):
        for to in others:
            pl.semaphore_signal(sem, inc=1, device_id=to, device_id_type=MESH)

    loads = [
        pltpu.make_async_copy(src, dst, load.at[m])
        for m, (src, dst) in enumerate(
            ((hit_hbm, x_ref), (wq_hbm, wq_ref), (wk_hbm, wk_ref), (wv_hbm, wv_ref))
        )
    ]
    for copy in loads:
        copy.start()
    lax.fori_loop(0, 16, greet, 0)
    tell(barrier, left, right, far_chip)

    for copy in loads[:2]:
        copy.wait()
    xs = x_ref[...].astype(F32)
    inv = lax.rsqrt(jnp.mean(xs * xs, axis=-1, keepdims=True) + EPSILON)
    n = (xs * inv * gain_attn_ref[...]).astype(BF)
    qt = jnp.dot(n, wq_ref[...], preferred_element_type=F32).T.astype(BF)
    for head in range(4):
        for block in range(4):
            qt_ref[block % 2, head, :, (block // 2) * 128 : (block // 2) * 128 + 128] = qt[
                head * HD : head * HD + HD, block * 128 : block * 128 + 128
            ]
    loads[2].wait()
    k = jnp.dot(n, wk_ref[...], preferred_element_type=F32)
    for head in range(4):
        for half in range(2):
            kh = k[half * 256 : half * 256 + 256, head * HD : head * HD + HD]
            kp_ref[head, half] = jnp.concatenate([kh[0:128], kh[128:256]], axis=1).astype(BF)
    loads[3].wait()
    vt = jnp.dot(n, wv_ref[...], preferred_element_type=F32).T.astype(BF)
    for head in range(4):
        for half in range(2):
            for u in range(2):
                at = half * 256 + u * 128
                vt_ref[head, half, u] = vt[head * HD : head * HD + HD, at : at + 128]

    pl.semaphore_wait(barrier, 18)
    tell(known.at[0], far_chip)

    def head_copies(i):
        head, half = (z + 1 + i // 2) % 4, i % 2
        at = pl.ds(pl.multiple_of(mine * 128, 128), 128)
        parts = (
            (qt_ref.at[half, head], qg.at[half * 4 + z], half * 4 + z, ylo),
            (kp_ref.at[head, half], kg.at[0, half, at, :], mine, half),
            (vt_ref.at[head, half], vg.at[0, half, :, :, at], mine, half),
        )
        here = (core == ylo) & (head == z)
        own = [here, here & (half == core), here & (half == core)]
        away = [
            pltpu.make_async_remote_copy(
                src_ref=src,
                dst_ref=dst,
                send_sem=x_send.at[n, i],
                recv_sem=x_recv.at[n, at_sem],
                device_id=device(core, x, head, yhi, to_core),
                device_id_type=MESH,
            )
            for n, (src, dst, at_sem, to_core) in enumerate(parts)
        ]
        local = [
            pltpu.make_async_copy(src, dst, x_recv.at[n, at_sem])
            for n, (src, dst, at_sem, to_core) in enumerate(parts)
        ]
        return own, away, local

    def send_heads(i, carry):
        for own, away, local in zip(*head_copies(i)):

            @pl.when(own)
            def _(local=local):
                local.start()

            @pl.when(jnp.logical_not(own))
            def _(away=away):
                away.start()

        return carry

    lax.fori_loop(0, 8, send_heads, 0)

    pl.semaphore_wait(known.at[0], 1)
    tell(known.at[1], left, right)

    rows = at_ref.shape[2]
    experts, cap = rows_out.shape[0], rows_out.shape[1]
    places = experts * cap
    ids = lax.broadcasted_iota(jnp.int32, (experts, rows), 0)
    picks = (routes_ref[0:1, :] == ids) | (routes_ref[1:2, :] == ids)
    marks = jnp.where(picks, 1.0, 0.0).astype(BF)
    before = lax.broadcasted_iota(jnp.int32, (rows, rows), 0) < lax.broadcasted_iota(
        jnp.int32, (rows, rows), 1
    )
    slots = jnp.dot(
        marks, jnp.where(before, 1.0, 0.0).astype(BF), preferred_element_type=F32
    ).astype(BF)
    spread = jnp.where(
        lax.broadcasted_iota(jnp.int32, (places, experts), 0) // cap
        == lax.broadcasted_iota(jnp.int32, (places, experts), 1),
        1.0,
        0.0,
    ).astype(BF)
    wide = lambda v: jnp.dot(spread, v, preferred_element_type=F32)
    order = (lax.broadcasted_iota(jnp.int32, (places, rows), 0) % cap).astype(F32)
    here = (wide(marks) > 0.5) & (wide(slots) == order)
    table_ref[...] = jnp.where(here, 1.0, 0.0).astype(BF)
    pl.semaphore_wait(known.at[1], 2)
    tell(known.at[2], left, right)

    def await_heads(j, carry):
        pltpu.make_async_copy(qg.at[j], qg.at[j], x_recv.at[0, j]).wait()
        at = pl.ds(pl.multiple_of(j * 128, 128), 128)
        kd = kg.at[0, core, at, :]
        pltpu.make_async_copy(kd, kd, x_recv.at[1, j]).wait()
        vd = vg.at[0, core, :, :, at]
        pltpu.make_async_copy(vd, vd, x_recv.at[2, j]).wait()
        return carry

    lax.fori_loop(0, 8, await_heads, 0)
    pl.semaphore_wait(known.at[2], 2)

    def remote(src, dst, send, recv, to):
        return pltpu.make_async_remote_copy(
            src_ref=src,
            dst_ref=dst,
            send_sem=send,
            recv_sem=recv,
            device_id=to,
            device_id_type=MESH,
        )

    def to_sibling(slot):
        return [
            remote(g.at[slot, core], g.at[slot, core], sib_send.at[n, slot], sib_recv.at[n, slot], sibling)
            for n, g in enumerate((kg, vg))
        ]

    def from_sibling(slot):
        return [
            remote(g.at[slot, 1 - core], g.at[slot, 1 - core], sib_send.at[n, slot], sib_recv.at[n, slot], sibling)
            for n, g in enumerate((kg, vg))
        ]

    k_right = remote(kg.at[0, core], kg.at[1, core], ring_send.at[0, 0], ring_recv.at[0, 0], right)
    v_right = remote(vg.at[0, core], vg.at[1, core], ring_send.at[1, 0], ring_recv.at[1, 0], right)
    k_left = remote(kg.at[0, core], kg.at[2, core], ring_send.at[0, 1], ring_recv.at[0, 1], left)
    v_left = remote(vg.at[0, core], vg.at[2, core], ring_send.at[1, 1], ring_recv.at[1, 1], left)
    k_on = remote(kg.at[1, core], kg.at[3, core], ring_send.at[0, 2], ring_recv.at[0, 2], right)
    v_on = remote(vg.at[2, core], vg.at[3, core], ring_send.at[1, 2], ring_recv.at[1, 2], left)
    for copy in (k_right, k_left, v_right, v_left):
        copy.start()
    for copy in to_sibling(0):
        copy.start()

    far_exp = (exp + 2) % 4
    w_local = pltpu.make_async_copy(wo_ref, wo_all.at[exp], w_own)
    w_across = remote(wo_ref, wo_all.at[exp], w_send.at[0], w_recv.at[0], far_chip)
    w_beside = remote(wo_ref, wo_all.at[exp], w_send.at[1], w_recv.at[1], sibling)
    w_on = remote(
        wo_all.at[far_exp], wo_all.at[far_exp], w_send.at[2], w_recv.at[2], sibling
    )
    w_across.start()
    w_beside.start()
    w_local.start()
    e_beside = [
        remote(src, dst, e_send.at[n], e_recv.at[n], sibling)
        for n, (src, dst) in enumerate(
            ((gate_ref, wg.at[1]), (up_ref, wu.at[1]), (down_ref, wd.at[1]))
        )
    ]
    weight_loads = [
        pltpu.make_async_copy(src, dst.at[0], w_sem.at[n])
        for n, (src, dst) in enumerate(((gate_ref, wg), (up_ref, wu), (down_ref, wd)))
    ]
    for copy in weight_loads:
        copy.start()
    for copy in e_beside:
        copy.start()

    zero = jnp.zeros((HD, 256), BF)
    for j in range(8):
        q2[j, 0, 0:HD] = qg[j]
        q2[j, 0, HD : 2 * HD] = zero
        q2[j, 1, 0:HD] = zero
        q2[j, 1, HD : 2 * HD] = qg[j]
    acc[...] = jnp.zeros_like(acc)
    mx[...] = jnp.full_like(mx, LOWEST)
    ls[...] = jnp.zeros_like(ls)

    def score(phase, tile, p):
        j = (tile // 4) * 4 + (tile + z) % 4
        keys = kg[phase // 2, (phase + core) % 2]
        for u in range(2):
            s_ref[p, u] = lax.dot_general(
                keys, q2[j, u], (((1,), (0,)), ((), ())), preferred_element_type=F32
            )

    def absorb(phase, tile, p):
        j = (tile // 4) * 4 + (tile + z) % 4
        s0 = s_ref[p, 0]
        s1 = s_ref[p, 1]
        old = mx[j]
        new = jnp.maximum(
            old,
            jnp.maximum(jnp.max(s0, axis=0, keepdims=True), jnp.max(s1, axis=0, keepdims=True)),
        )
        fade = jnp.exp2((old - new) * ALPHA)
        e0 = jnp.exp2((s0 - new) * ALPHA)
        e1 = jnp.exp2((s1 - new) * ALPHA)
        slot, half = phase // 2, (phase + core) % 2
        ls[j] = ls[j] * fade + (
            jnp.sum(e0, axis=0, keepdims=True) + jnp.sum(e1, axis=0, keepdims=True)
        )
        acc[j] = acc[j] * fade + (
            jnp.dot(vg[slot, half, 0], e0.astype(BF), preferred_element_type=F32)
            + jnp.dot(vg[slot, half, 1], e1.astype(BF), preferred_element_type=F32)
        )
        mx[j] = new

    head = yhi * 8 + mine

    def out_copy(i):
        j, to_yhi = i % 8, i // 8
        to = device(core, x, j % 4, to_yhi, j // 4)
        own = (core == ylo) & (j % 4 == z) & (to_yhi == yhi) & (j // 4 == core)
        return (
            own,
            remote(ost.at[j, to_yhi], at_ref.at[head], o_send.at[i], o_recv.at[head], to),
            pltpu.make_async_copy(ost.at[j, to_yhi], at_ref.at[head], o_recv.at[head]),
        )

    def send_out(tile):
        j = (tile // 4) * 4 + (tile + z) % 4
        o = (acc[j] / ls[j]).astype(BF)
        ost[j, 0] = o[:, 0:128]
        ost[j, 1] = o[:, 128:256]
        for to_yhi in range(2):
            i = to_yhi * 8 + j
            own, away, local = out_copy(i)

            @pl.when(own)
            def _(local=local):
                local.start()

            @pl.when(jnp.logical_not(own))
            def _(away=away):
                away.start()

    score(0, 0, 0)

    def pair(n):
        return pl.ds(pl.multiple_of(2 * n, 2), 2)

    def row_copy(i):
        to = shifted(i, 1, ctx, exp)
        return pltpu.make_async_remote_copy(
            src_ref=rows_out.at[pair(to[0])],
            dst_ref=got.at[i],
            send_sem=send.at[i],
            recv_sem=recv.at[i],
            device_id=to,
            device_id_type=MESH,
        )

    def back_copy(i):
        return pltpu.make_async_remote_copy(
            src_ref=stage.at[i],
            dst_ref=back.at[yhi, pair(ctx)],
            send_sem=b_send.at[i],
            recv_sem=b_recv.at[i],
            device_id=shifted(i, -1, ctx, exp),
            device_id_type=MESH,
        )

    def route_rows():
        def await_out(i, carry):
            pltpu.make_async_copy(at_ref.at[i], at_ref.at[i], o_recv.at[i]).wait()
            return carry

        lax.fori_loop(0, 16, await_out, 0)
        w_local.wait()
        w_beside.wait_recv()
        w_on.wait_recv()
        mixed = lax.dot_general(
            at_ref[...].reshape(D, rows),
            wo_all[...].reshape(D, D),
            (((0,), (0,)), ((), ())),
            preferred_element_type=F32,
        )
        own_rows = x_ref[pl.ds(pl.multiple_of(exp * rows, rows), rows), :]
        residual = own_rows.astype(F32) + mixed
        inv = lax.rsqrt(jnp.mean(residual * residual, axis=-1, keepdims=True) + EPSILON)
        res_ref[...] = residual
        normed = (residual * inv * gain_ref[...]).astype(BF)
        normed_ref[...] = normed
        picked = jnp.dot(table_ref[...], normed, preferred_element_type=F32)
        rows_out[...] = picked.reshape(rows_out.shape).astype(BF)
        pltpu.make_async_copy(rows_out.at[pair(ctx)], got.at[0], recv.at[0]).start()

        def send_rows(i, carry):
            row_copy(i).start()
            return carry

        lax.fori_loop(1, 64, send_rows, 0)

    def step_of(g):
        late = jnp.minimum(g // 8, 1)
        k = jnp.maximum(g - 8, 0)
        phase = (1 - late) * (g // 4) + late * (2 + (k % 12) // 2)
        pair = (1 - late) * (g % 4) + late * ((k // 12) * 2 + k % 2)
        return phase, pair

    def turn(g, carry):
        phase, pair = step_of(g)

        for slot, at in ((0, 3), (1, 9), (2, 13), (3, 17)):

            @pl.when(g == at)
            def _(slot=slot):
                for copy in from_sibling(slot):
                    copy.wait_recv()

        @pl.when(g == 7)
        def _():
            for copy in (k_right, k_left, v_right, v_left):
                copy.wait_recv()
            k_on.start()
            v_on.start()
            for slot in (1, 2):
                for copy in to_sibling(slot):
                    copy.start()

        @pl.when(g == 15)
        def _():
            k_on.wait_recv()
            v_on.wait_recv()
            for copy in to_sibling(3):
                copy.start()
            w_across.wait_recv()
            w_on.start()

        @pl.when((g == 23) & (core == 0))
        def _():
            route_rows()

        score(phase, 2 * pair + 1, 1)
        absorb(phase, 2 * pair, 0)
        later = jnp.minimum(g + 1, 31)
        next_phase, next_pair = step_of(later)
        score(next_phase, 2 * next_pair, 0)
        absorb(phase, 2 * pair + 1, 1)

        @pl.when(phase == 7)
        def _():
            send_out(2 * pair)
            send_out(2 * pair + 1)

        return carry

    lax.fori_loop(0, 32, turn, 0)

    @pl.when(core == 1)
    def _():
        route_rows()


    normed = normed_ref[...]
    here = table_ref[...].astype(F32) > 0.5
    logits = lax.dot_general(
        wr_ref[...], normed, (((1,), (1,)), ((), ())), preferred_element_type=F32
    )
    top = jnp.max(jnp.where(picks, logits, -jnp.inf), axis=0, keepdims=True)
    weights = jnp.where(picks, jnp.exp(jnp.where(picks, logits - top, 0.0)), 0.0)
    gates = weights / jnp.sum(weights, axis=0, keepdims=True)
    gate_hi = gates.astype(BF)
    gate_lo = (gates - gate_hi.astype(F32)).astype(BF)
    hi = jnp.where(here, wide(gate_hi), 0.0).astype(BF)
    lo = jnp.where(here, wide(gate_lo), 0.0).astype(BF)
    for copy in weight_loads:
        copy.wait()
    for copy in e_beside:
        copy.wait_recv()

    group = 32

    def serve(g, carry):
        first = g * group

        def await_rows(i, carry):
            pltpu.make_async_copy(got.at[first + i], got.at[first + i], recv.at[first + i]).wait()
            return carry

        lax.fori_loop(0, group, await_rows, 0)
        at = pl.ds(pl.multiple_of(first, group), group)

        def expert(j, carry):
            mine = got[at, j].astype(F32).reshape(group * cap, D).astype(BF)
            total = None
            for q in range(2):
                gate = jnp.dot(mine, wg[q, j], preferred_element_type=F32)
                up = jnp.dot(mine, wu[q, j], preferred_element_type=F32)
                hidden = (gate / (1.0 + jnp.exp(-gate)) * up).astype(BF)
                part = jnp.dot(hidden, wd[q, j], preferred_element_type=F32)
                total = part if total is None else total + part
            stage[at, j] = total.reshape(group, cap, D).astype(BF)
            return carry

        lax.fori_loop(0, 2, expert, 0)

        @pl.when(first == 0)
        def _():
            pltpu.make_async_copy(stage.at[0], back.at[yhi, pair(ctx)], b_recv.at[0]).start()

        def send_back(i, carry):
            @pl.when(first + i > 0)
            def _():
                back_copy(first + i).start()

            return carry

        lax.fori_loop(0, group, send_back, 0)
        return carry

    lax.fori_loop(0, 2, serve, 0)

    def await_back(i, carry):
        from_ctx, from_exp = shifted(i, 1, ctx, exp)
        block = back.at[from_exp // 2, pair(from_ctx)]
        pltpu.make_async_copy(block, block, b_recv.at[i]).wait()
        return carry

    lax.fori_loop(0, 64, await_back, 0)
    total = res_ref[...]
    for n in range(2):
        served = back[n].astype(F32).reshape(places, D).astype(BF)
        for gate in (hi, lo):
            total = total + lax.dot_general(
                gate, served, (((0,), (0,)), ((), ())), preferred_element_type=F32
            )
    out_ref[...] = total.astype(BF)

    def sent(i, carry):
        row_copy(i).wait_send()
        back_copy(i).wait_send()
        return carry

    lax.fori_loop(1, 64, sent, 0)

    def sent_heads(i, carry):
        for own, away, _ in zip(*head_copies(i)):

            @pl.when(jnp.logical_not(own))
            def _(away=away):
                away.wait_send()

        return carry

    lax.fori_loop(0, 8, sent_heads, 0)

    def sent_out(i, carry):
        own, away, local = out_copy(i)

        @pl.when(jnp.logical_not(own))
        def _():
            away.wait_send()

        return carry

    lax.fori_loop(0, 16, sent_out, 0)
    for copy in (k_right, k_left, v_right, v_left, k_on, v_on):
        copy.wait_send()
    for slot in range(4):
        for copy in to_sibling(slot):
            copy.wait_send()
    for copy in (w_across, w_beside, w_on):
        copy.wait_send()
    for copy in e_beside:
        copy.wait_send()


def layer(hit, gain_attn, wq, wk, wv, wo, gain, wr, w_gate, w_up, w_down, routes):
    experts = wr.shape[1]
    rows = routes.shape[0]
    cap = 8
    dma = pltpu.SemaphoreType.DMA
    return pl.pallas_call(
        layer_kernel,
        out_shape=jax.ShapeDtypeStruct((rows, D), BF),
        in_specs=[
            anywhere(),
            whole(),
            anywhere(),
            anywhere(),
            anywhere(),
            anywhere(),
            whole(),
            whole(),
            whole(),
            anywhere(),
            anywhere(),
            anywhere(),
        ],
        out_specs=whole(),
        scratch_shapes=[
            VMEM(hit.shape, BF),
            VMEM(wq.shape, BF),
            VMEM(wk.shape, BF),
            VMEM(wv.shape, BF),
            VMEM((2, 4, HD, 256), BF),
            VMEM((4, 2, 128, 128), BF),
            VMEM((4, 2, 2, HD, 128), BF),
            VMEM((8, HD, 256), BF),
            VMEM((4, 2, 1024, 128), BF),
            VMEM((4, 2, 2, HD, 1024), BF),
            VMEM((8, 2, 128, 256), BF),
            VMEM((2, 2, 1024, 256), F32),
            VMEM((8, HD, 256), F32),
            VMEM((8, 1, 256), F32),
            VMEM((8, 1, 256), F32),
            VMEM((8, 2, HD, 128), BF),
            VMEM((16, HD, 128), BF),
            VMEM((4,) + wo.shape, BF),
            VMEM((2,) + w_gate.shape, BF),
            VMEM((2,) + w_up.shape, BF),
            VMEM((2,) + w_down.shape, BF),
            VMEM((experts, cap, D), BF),
            VMEM((64, 2, cap, D), BF),
            VMEM((64, 2, cap, D), BF),
            VMEM((2, experts, cap, D), BF),
            VMEM((experts * cap, rows), BF),
            VMEM((rows, D), F32),
            VMEM((rows, D), BF),
            dma((4,)),
            dma((3, 8)),
            dma((3, 8)),
            dma((2, 3)),
            dma((2, 3)),
            dma((2, 4)),
            dma((2, 4)),
            dma((16,)),
            dma((16,)),
            dma((3,)),
            dma((3,)),
            dma,
            dma((3,)),
            dma((3,)),
            dma((3,)),
            dma((64,)),
            dma((64,)),
            dma((64,)),
            dma((64,)),
            pltpu.SemaphoreType.REGULAR((3,)),
        ],
        compiler_params=pltpu.CompilerParams(
            collective_id=0, has_side_effects=True, vmem_limit_bytes=60 << 20
        ),
        name="layer",
    )(
        hit,
        gain_attn.reshape(1, D),
        wq,
        wk,
        wv,
        wo,
        gain.reshape(1, D),
        wr.T,
        routes.T,
        w_gate,
        w_up,
        w_down,
    )


def solution(mesh):
    return jax.shard_map(
        layer,
        mesh=mesh,
        in_specs=(
            P("ctx", None),
            P(),
            P(None, "exp"),
            P(None, "exp"),
            P(None, "exp"),
            P("exp", None),
            P(),
            P(),
            P("ctx", None, "exp"),
            P("ctx", None, "exp"),
            P("ctx", "exp", None),
            P(("ctx", "exp"), None),
        ),
        out_specs=P(("ctx", "exp"), None),
        check_vma=False,
    )
```

```python
import functools
import math

import jax
import jax.numpy as jnp
from jax import lax
from jax.experimental import pallas as pl
from jax.experimental.pallas import tpu as pltpu
from jax.sharding import PartitionSpec as P

D = 1024
HD = 64
EPSILON = 1e-05
LOWEST = -1e30
ALPHA = math.log2(math.e) / math.sqrt(HD)
BF = jnp.bfloat16
F32 = jnp.float32
MESH = pl.DeviceIdType.MESH
VMEM = pltpu.VMEM


def whole():
    return pl.BlockSpec(memory_space=pltpu.VMEM)


def anywhere():
    return pl.BlockSpec(memory_space=pl.ANY)


def shifted(i, sign, ctx, exp):
    o = (i * 11) % 64
    ylo, x, z, yhi = ctx // 16, (ctx // 4) % 4, ctx % 4, exp // 2
    to_x = (x + 4 + sign * (o % 4)) % 4
    to_y = (yhi * 2 + ylo + 4 + sign * ((o // 4) % 4)) % 4
    to_z = (z + 4 + sign * (o // 16)) % 4
    to_ctx = (to_y % 2) * 16 + to_x * 4 + to_z
    return to_ctx, (to_y // 2) * 2 + exp % 2


def layer_kernel(
    hit_hbm,
    gain_attn_ref,
    wq_hbm,
    wk_hbm,
    wv_hbm,
    wo_ref,
    gain_ref,
    wr_ref,
    routes_ref,
    gate_ref,
    up_ref,
    down_ref,
    out_ref,
    x_ref,
    wq_ref,
    wk_ref,
    wv_ref,
    qt_ref,
    kp_ref,
    vt_ref,
    qg,
    kg,
    vg,
    q2,
    s_ref,
    acc,
    mx,
    ls,
    ost,
    at_ref,
    wo_all,
    wg,
    wu,
    wd,
    rows_out,
    got,
    stage,
    back,
    table_ref,
    res_ref,
    normed_ref,
    load,
    x_send,
    x_recv,
    ring_send,
    ring_recv,
    sib_send,
    sib_recv,
    o_send,
    o_recv,
    w_send,
    w_recv,
    w_own,
    e_send,
    e_recv,
    w_sem,
    send,
    recv,
    b_send,
    b_recv,
    known,
):
    ctx = lax.axis_index("ctx")
    exp = lax.axis_index("exp")
    ylo = ctx // 16
    x = (ctx // 4) % 4
    z = ctx % 4
    yhi = exp // 2
    core = exp % 2
    mine = ylo * 4 + z

    def device(to_ylo, to_x, to_z, to_yhi, to_core):
        return (to_ylo * 16 + to_x * 4 + to_z, to_yhi * 2 + to_core)

    right = device(ylo, (x + 1) % 4, z, yhi, core)
    left = device(ylo, (x + 3) % 4, z, yhi, core)
    sibling = device(ylo, x, z, yhi, 1 - core)

    barrier = pltpu.get_barrier_semaphore()

    def greet(i, carry):
        @pl.when(i != mine * 2 + core)
        def _():
            to = device(i // 8, x, (i // 2) % 4, yhi, i % 2)
            pl.semaphore_signal(barrier, inc=1, device_id=to, device_id_type=MESH)

        return carry

    far_chip = device(ylo, x, z, 1 - yhi, core)

    def tell(sem, *others):
        for to in others:
            pl.semaphore_signal(sem, inc=1, device_id=to, device_id_type=MESH)

    loads = [
        pltpu.make_async_copy(src, dst, load.at[m])
        for m, (src, dst) in enumerate(
            ((hit_hbm, x_ref), (wq_hbm, wq_ref), (wk_hbm, wk_ref), (wv_hbm, wv_ref))
        )
    ]
    for copy in loads:
        copy.start()
    lax.fori_loop(0, 16, greet, 0)
    tell(barrier, left, right, far_chip)

    for copy in loads[:2]:
        copy.wait()
    xs = x_ref[...].astype(F32)
    inv = lax.rsqrt(jnp.mean(xs * xs, axis=-1, keepdims=True) + EPSILON)
    n = (xs * inv * gain_attn_ref[...]).astype(BF)
    qt = jnp.dot(n, wq_ref[...], preferred_element_type=F32).T.astype(BF)
    for head in range(4):
        for block in range(4):
            qt_ref[block % 2, head, :, (block // 2) * 128 : (block // 2) * 128 + 128] = qt[
                head * HD : head * HD + HD, block * 128 : block * 128 + 128
            ]
    loads[2].wait()
    k = jnp.dot(n, wk_ref[...], preferred_element_type=F32)
    for head in range(4):
        for half in range(2):
            kh = k[half * 256 : half * 256 + 256, head * HD : head * HD + HD]
            kp_ref[head, half] = jnp.concatenate([kh[0:128], kh[128:256]], axis=1).astype(BF)
    loads[3].wait()
    vt = jnp.dot(n, wv_ref[...], preferred_element_type=F32).T.astype(BF)
    for head in range(4):
        for half in range(2):
            for u in range(2):
                at = half * 256 + u * 128
                vt_ref[head, half, u] = vt[head * HD : head * HD + HD, at : at + 128]

    pl.semaphore_wait(barrier, 18)
    tell(known.at[0], far_chip)

    def head_copies(i):
        head, half = (z + 1 + i // 2) % 4, i % 2
        at = pl.ds(pl.multiple_of(mine * 128, 128), 128)
        parts = (
            (qt_ref.at[half, head], qg.at[half * 4 + z], half * 4 + z, ylo),
            (kp_ref.at[head, half], kg.at[0, half, at, :], mine, half),
            (vt_ref.at[head, half], vg.at[0, half, :, :, at], mine, half),
        )
        here = (core == ylo) & (head == z)
        own = [here, here & (half == core), here & (half == core)]
        away = [
            pltpu.make_async_remote_copy(
                src_ref=src,
                dst_ref=dst,
                send_sem=x_send.at[n, i],
                recv_sem=x_recv.at[n, at_sem],
                device_id=device(core, x, head, yhi, to_core),
                device_id_type=MESH,
            )
            for n, (src, dst, at_sem, to_core) in enumerate(parts)
        ]
        local = [
            pltpu.make_async_copy(src, dst, x_recv.at[n, at_sem])
            for n, (src, dst, at_sem, to_core) in enumerate(parts)
        ]
        return own, away, local

    def send_heads(i, carry):
        for own, away, local in zip(*head_copies(i)):

            @pl.when(own)
            def _(local=local):
                local.start()

            @pl.when(jnp.logical_not(own))
            def _(away=away):
                away.start()

        return carry

    lax.fori_loop(0, 8, send_heads, 0)

    pl.semaphore_wait(known.at[0], 1)
    tell(known.at[1], left, right)

    rows = at_ref.shape[2]
    experts, cap = rows_out.shape[0], rows_out.shape[1]
    places = experts * cap
    ids = lax.broadcasted_iota(jnp.int32, (experts, rows), 0)
    picks = (routes_ref[0:1, :] == ids) | (routes_ref[1:2, :] == ids)
    marks = jnp.where(picks, 1.0, 0.0).astype(BF)
    before = lax.broadcasted_iota(jnp.int32, (rows, rows), 0) < lax.broadcasted_iota(
        jnp.int32, (rows, rows), 1
    )
    slots = jnp.dot(
        marks, jnp.where(before, 1.0, 0.0).astype(BF), preferred_element_type=F32
    ).astype(BF)
    spread = jnp.where(
        lax.broadcasted_iota(jnp.int32, (places, experts), 0) // cap
        == lax.broadcasted_iota(jnp.int32, (places, experts), 1),
        1.0,
        0.0,
    ).astype(BF)
    wide = lambda v: jnp.dot(spread, v, preferred_element_type=F32)
    order = (lax.broadcasted_iota(jnp.int32, (places, rows), 0) % cap).astype(F32)
    here = (wide(marks) > 0.5) & (wide(slots) == order)
    table_ref[...] = jnp.where(here, 1.0, 0.0).astype(BF)
    pl.semaphore_wait(known.at[1], 2)
    tell(known.at[2], left, right)

    def await_heads(j, carry):
        pltpu.make_async_copy(qg.at[j], qg.at[j], x_recv.at[0, j]).wait()
        at = pl.ds(pl.multiple_of(j * 128, 128), 128)
        kd = kg.at[0, core, at, :]
        pltpu.make_async_copy(kd, kd, x_recv.at[1, j]).wait()
        vd = vg.at[0, core, :, :, at]
        pltpu.make_async_copy(vd, vd, x_recv.at[2, j]).wait()
        return carry

    lax.fori_loop(0, 8, await_heads, 0)
    pl.semaphore_wait(known.at[2], 2)

    def remote(src, dst, send, recv, to):
        return pltpu.make_async_remote_copy(
            src_ref=src,
            dst_ref=dst,
            send_sem=send,
            recv_sem=recv,
            device_id=to,
            device_id_type=MESH,
        )

    def to_sibling(slot):
        return [
            remote(g.at[slot, core], g.at[slot, core], sib_send.at[n, slot], sib_recv.at[n, slot], sibling)
            for n, g in enumerate((kg, vg))
        ]

    def from_sibling(slot):
        return [
            remote(g.at[slot, 1 - core], g.at[slot, 1 - core], sib_send.at[n, slot], sib_recv.at[n, slot], sibling)
            for n, g in enumerate((kg, vg))
        ]

    k_right = remote(kg.at[0, core], kg.at[1, core], ring_send.at[0, 0], ring_recv.at[0, 0], right)
    v_right = remote(vg.at[0, core], vg.at[1, core], ring_send.at[1, 0], ring_recv.at[1, 0], right)
    k_left = remote(kg.at[0, core], kg.at[2, core], ring_send.at[0, 1], ring_recv.at[0, 1], left)
    v_left = remote(vg.at[0, core], vg.at[2, core], ring_send.at[1, 1], ring_recv.at[1, 1], left)
    k_on = remote(kg.at[1, core], kg.at[3, core], ring_send.at[0, 2], ring_recv.at[0, 2], right)
    v_on = remote(vg.at[2, core], vg.at[3, core], ring_send.at[1, 2], ring_recv.at[1, 2], left)
    for copy in (k_right, k_left, v_right, v_left):
        copy.start()
    for copy in to_sibling(0):
        copy.start()

    far_exp = (exp + 2) % 4
    w_local = pltpu.make_async_copy(wo_ref, wo_all.at[exp], w_own)
    w_across = remote(wo_ref, wo_all.at[exp], w_send.at[0], w_recv.at[0], far_chip)
    w_beside = remote(wo_ref, wo_all.at[exp], w_send.at[1], w_recv.at[1], sibling)
    w_on = remote(
        wo_all.at[far_exp], wo_all.at[far_exp], w_send.at[2], w_recv.at[2], sibling
    )
    w_across.start()
    w_beside.start()
    w_local.start()
    e_beside = [
        remote(src, dst, e_send.at[n], e_recv.at[n], sibling)
        for n, (src, dst) in enumerate(
            ((gate_ref, wg.at[1]), (up_ref, wu.at[1]), (down_ref, wd.at[1]))
        )
    ]
    weight_loads = [
        pltpu.make_async_copy(src, dst.at[0], w_sem.at[n])
        for n, (src, dst) in enumerate(((gate_ref, wg), (up_ref, wu), (down_ref, wd)))
    ]
    for copy in weight_loads:
        copy.start()
    for copy in e_beside:
        copy.start()

    zero = jnp.zeros((HD, 256), BF)
    for j in range(8):
        q2[j, 0, 0:HD] = qg[j]
        q2[j, 0, HD : 2 * HD] = zero
        q2[j, 1, 0:HD] = zero
        q2[j, 1, HD : 2 * HD] = qg[j]
    acc[...] = jnp.zeros_like(acc)
    mx[...] = jnp.full_like(mx, LOWEST)
    ls[...] = jnp.zeros_like(ls)

    def score(phase, tile, p):
        j = (tile // 4) * 4 + (tile + z) % 4
        keys = kg[phase // 2, (phase + core) % 2]
        for u in range(2):
            s_ref[p, u] = lax.dot_general(
                keys, q2[j, u], (((1,), (0,)), ((), ())), preferred_element_type=F32
            )

    def absorb(phase, tile, p):
        j = (tile // 4) * 4 + (tile + z) % 4
        s0 = s_ref[p, 0]
        s1 = s_ref[p, 1]
        old = mx[j]
        new = jnp.maximum(
            old,
            jnp.maximum(jnp.max(s0, axis=0, keepdims=True), jnp.max(s1, axis=0, keepdims=True)),
        )
        fade = jnp.exp2((old - new) * ALPHA)
        e0 = jnp.exp2((s0 - new) * ALPHA)
        e1 = jnp.exp2((s1 - new) * ALPHA)
        slot, half = phase // 2, (phase + core) % 2
        ls[j] = ls[j] * fade + (
            jnp.sum(e0, axis=0, keepdims=True) + jnp.sum(e1, axis=0, keepdims=True)
        )
        acc[j] = acc[j] * fade + (
            jnp.dot(vg[slot, half, 0], e0.astype(BF), preferred_element_type=F32)
            + jnp.dot(vg[slot, half, 1], e1.astype(BF), preferred_element_type=F32)
        )
        mx[j] = new

    head = yhi * 8 + mine

    def out_copy(i):
        j, to_yhi = i % 8, i // 8
        to = device(core, x, j % 4, to_yhi, j // 4)
        own = (core == ylo) & (j % 4 == z) & (to_yhi == yhi) & (j // 4 == core)
        return (
            own,
            remote(ost.at[j, to_yhi], at_ref.at[head], o_send.at[i], o_recv.at[head], to),
            pltpu.make_async_copy(ost.at[j, to_yhi], at_ref.at[head], o_recv.at[head]),
        )

    def send_out(tile):
        j = (tile // 4) * 4 + (tile + z) % 4
        o = (acc[j] / ls[j]).astype(BF)
        ost[j, 0] = o[:, 0:128]
        ost[j, 1] = o[:, 128:256]
        for to_yhi in range(2):
            i = to_yhi * 8 + j
            own, away, local = out_copy(i)

            @pl.when(own)
            def _(local=local):
                local.start()

            @pl.when(jnp.logical_not(own))
            def _(away=away):
                away.start()

    score(0, 0, 0)

    def pair(n):
        return pl.ds(pl.multiple_of(2 * n, 2), 2)

    def row_copy(i):
        to = shifted(i, 1, ctx, exp)
        return pltpu.make_async_remote_copy(
            src_ref=rows_out.at[pair(to[0])],
            dst_ref=got.at[i],
            send_sem=send.at[i],
            recv_sem=recv.at[i],
            device_id=to,
            device_id_type=MESH,
        )

    def back_copy(i):
        return pltpu.make_async_remote_copy(
            src_ref=stage.at[i],
            dst_ref=back.at[yhi, pair(ctx)],
            send_sem=b_send.at[i],
            recv_sem=b_recv.at[i],
            device_id=shifted(i, -1, ctx, exp),
            device_id_type=MESH,
        )

    def route_rows():
        def await_out(i, carry):
            pltpu.make_async_copy(at_ref.at[i], at_ref.at[i], o_recv.at[i]).wait()
            return carry

        lax.fori_loop(0, 16, await_out, 0)
        w_local.wait()
        w_beside.wait_recv()
        w_on.wait_recv()
        mixed = lax.dot_general(
            at_ref[...].reshape(D, rows),
            wo_all[...].reshape(D, D),
            (((0,), (0,)), ((), ())),
            preferred_element_type=F32,
        )
        own_rows = x_ref[pl.ds(pl.multiple_of(exp * rows, rows), rows), :]
        residual = own_rows.astype(F32) + mixed
        inv = lax.rsqrt(jnp.mean(residual * residual, axis=-1, keepdims=True) + EPSILON)
        res_ref[...] = residual
        normed = (residual * inv * gain_ref[...]).astype(BF)
        normed_ref[...] = normed
        picked = jnp.dot(table_ref[...], normed, preferred_element_type=F32)
        rows_out[...] = picked.reshape(rows_out.shape).astype(BF)
        pltpu.make_async_copy(rows_out.at[pair(ctx)], got.at[0], recv.at[0]).start()

        def send_rows(i, carry):
            row_copy(i).start()
            return carry

        lax.fori_loop(1, 64, send_rows, 0)

    def step_of(g):
        late = jnp.minimum(g // 8, 1)
        k = jnp.maximum(g - 8, 0)
        phase = (1 - late) * (g // 4) + late * (2 + (k % 12) // 2)
        pair = (1 - late) * (g % 4) + late * ((k // 12) * 2 + k % 2)
        return phase, pair

    def turn(g, carry):
        phase, pair = step_of(g)

        for slot, at in ((0, 3), (1, 9), (2, 13), (3, 17)):

            @pl.when(g == at)
            def _(slot=slot):
                for copy in from_sibling(slot):
                    copy.wait_recv()

        @pl.when(g == 7)
        def _():
            for copy in (k_right, k_left, v_right, v_left):
                copy.wait_recv()
            k_on.start()
            v_on.start()
            for slot in (1, 2):
                for copy in to_sibling(slot):
                    copy.start()

        @pl.when(g == 15)
        def _():
            k_on.wait_recv()
            v_on.wait_recv()
            for copy in to_sibling(3):
                copy.start()
            w_across.wait_recv()
            w_on.start()

        @pl.when((g == 23) & (core == 0))
        def _():
            route_rows()

        score(phase, 2 * pair + 1, 1)
        absorb(phase, 2 * pair, 0)
        later = jnp.minimum(g + 1, 31)
        next_phase, next_pair = step_of(later)
        score(next_phase, 2 * next_pair, 0)
        absorb(phase, 2 * pair + 1, 1)

        @pl.when(phase == 7)
        def _():
            send_out(2 * pair)
            send_out(2 * pair + 1)

        return carry

    lax.fori_loop(0, 32, turn, 0)

    @pl.when(core == 1)
    def _():
        route_rows()


    for copy in weight_loads:
        copy.wait()
    for copy in e_beside:
        copy.wait_recv()

    group = 32

    def serve(g, carry):
        first = g * group

        def await_rows(i, carry):
            pltpu.make_async_copy(got.at[first + i], got.at[first + i], recv.at[first + i]).wait()
            return carry

        lax.fori_loop(0, group, await_rows, 0)
        at = pl.ds(pl.multiple_of(first, group), group)

        def expert(j, carry):
            mine = got[at, j].astype(F32).reshape(group * cap, D).astype(BF)
            total = None
            for q in range(2):
                gate = jnp.dot(mine, wg[q, j], preferred_element_type=F32)
                up = jnp.dot(mine, wu[q, j], preferred_element_type=F32)
                hidden = (gate / (1.0 + jnp.exp(-gate)) * up).astype(BF)
                part = jnp.dot(hidden, wd[q, j], preferred_element_type=F32)
                total = part if total is None else total + part
            stage[at, j] = total.reshape(group, cap, D).astype(BF)
            return carry

        lax.fori_loop(0, 2, expert, 0)

        @pl.when(first == 0)
        def _():
            pltpu.make_async_copy(stage.at[0], back.at[yhi, pair(ctx)], b_recv.at[0]).start()

        def send_back(i, carry):
            @pl.when(first + i > 0)
            def _():
                back_copy(first + i).start()

            return carry

        lax.fori_loop(0, group, send_back, 0)
        return carry

    lax.fori_loop(0, 2, serve, 0)

    normed = normed_ref[...]
    here = table_ref[...].astype(F32) > 0.5
    logits = lax.dot_general(
        wr_ref[...], normed, (((1,), (1,)), ((), ())), preferred_element_type=F32
    )
    top = jnp.max(jnp.where(picks, logits, -jnp.inf), axis=0, keepdims=True)
    weights = jnp.where(picks, jnp.exp(jnp.where(picks, logits - top, 0.0)), 0.0)
    gates = weights / jnp.sum(weights, axis=0, keepdims=True)
    gate_hi = gates.astype(BF)
    gate_lo = (gates - gate_hi.astype(F32)).astype(BF)
    hi = jnp.where(here, wide(gate_hi), 0.0).astype(BF)
    lo = jnp.where(here, wide(gate_lo), 0.0).astype(BF)

    def await_back(i, carry):
        from_ctx, from_exp = shifted(i, 1, ctx, exp)
        block = back.at[from_exp // 2, pair(from_ctx)]
        pltpu.make_async_copy(block, block, b_recv.at[i]).wait()
        return carry

    lax.fori_loop(0, 64, await_back, 0)
    total = res_ref[...]
    for n in range(2):
        served = back[n].astype(F32).reshape(places, D).astype(BF)
        for gate in (hi, lo):
            total = total + lax.dot_general(
                gate, served, (((0,), (0,)), ((), ())), preferred_element_type=F32
            )
    out_ref[...] = total.astype(BF)

    def sent(i, carry):
        row_copy(i).wait_send()
        back_copy(i).wait_send()
        return carry

    lax.fori_loop(1, 64, sent, 0)

    def sent_heads(i, carry):
        for own, away, _ in zip(*head_copies(i)):

            @pl.when(jnp.logical_not(own))
            def _(away=away):
                away.wait_send()

        return carry

    lax.fori_loop(0, 8, sent_heads, 0)

    def sent_out(i, carry):
        own, away, local = out_copy(i)

        @pl.when(jnp.logical_not(own))
        def _():
            away.wait_send()

        return carry

    lax.fori_loop(0, 16, sent_out, 0)
    for copy in (k_right, k_left, v_right, v_left, k_on, v_on):
        copy.wait_send()
    for slot in range(4):
        for copy in to_sibling(slot):
            copy.wait_send()
    for copy in (w_across, w_beside, w_on):
        copy.wait_send()
    for copy in e_beside:
        copy.wait_send()


def layer(hit, gain_attn, wq, wk, wv, wo, gain, wr, w_gate, w_up, w_down, routes):
    experts = wr.shape[1]
    rows = routes.shape[0]
    cap = 8
    dma = pltpu.SemaphoreType.DMA
    return pl.pallas_call(
        layer_kernel,
        out_shape=jax.ShapeDtypeStruct((rows, D), BF),
        in_specs=[
            anywhere(),
            whole(),
            anywhere(),
            anywhere(),
            anywhere(),
            anywhere(),
            whole(),
            whole(),
            whole(),
            anywhere(),
            anywhere(),
            anywhere(),
        ],
        out_specs=whole(),
        scratch_shapes=[
            VMEM(hit.shape, BF),
            VMEM(wq.shape, BF),
            VMEM(wk.shape, BF),
            VMEM(wv.shape, BF),
            VMEM((2, 4, HD, 256), BF),
            VMEM((4, 2, 128, 128), BF),
            VMEM((4, 2, 2, HD, 128), BF),
            VMEM((8, HD, 256), BF),
            VMEM((4, 2, 1024, 128), BF),
            VMEM((4, 2, 2, HD, 1024), BF),
            VMEM((8, 2, 128, 256), BF),
            VMEM((2, 2, 1024, 256), F32),
            VMEM((8, HD, 256), F32),
            VMEM((8, 1, 256), F32),
            VMEM((8, 1, 256), F32),
            VMEM((8, 2, HD, 128), BF),
            VMEM((16, HD, 128), BF),
            VMEM((4,) + wo.shape, BF),
            VMEM((2,) + w_gate.shape, BF),
            VMEM((2,) + w_up.shape, BF),
            VMEM((2,) + w_down.shape, BF),
            VMEM((experts, cap, D), BF),
            VMEM((64, 2, cap, D), BF),
            VMEM((64, 2, cap, D), BF),
            VMEM((2, experts, cap, D), BF),
            VMEM((experts * cap, rows), BF),
            VMEM((rows, D), F32),
            VMEM((rows, D), BF),
            dma((4,)),
            dma((3, 8)),
            dma((3, 8)),
            dma((2, 3)),
            dma((2, 3)),
            dma((2, 4)),
            dma((2, 4)),
            dma((16,)),
            dma((16,)),
            dma((3,)),
            dma((3,)),
            dma,
            dma((3,)),
            dma((3,)),
            dma((3,)),
            dma((64,)),
            dma((64,)),
            dma((64,)),
            dma((64,)),
            pltpu.SemaphoreType.REGULAR((3,)),
        ],
        compiler_params=pltpu.CompilerParams(
            collective_id=0, has_side_effects=True, vmem_limit_bytes=60 << 20
        ),
        name="layer",
    )(
        hit,
        gain_attn.reshape(1, D),
        wq,
        wk,
        wv,
        wo,
        gain.reshape(1, D),
        wr.T,
        routes.T,
        w_gate,
        w_up,
        w_down,
    )


def solution(mesh):
    return jax.shard_map(
        layer,
        mesh=mesh,
        in_specs=(
            P("ctx", None),
            P(),
            P(None, "exp"),
            P(None, "exp"),
            P(None, "exp"),
            P("exp", None),
            P(),
            P(),
            P("ctx", None, "exp"),
            P("ctx", None, "exp"),
            P("ctx", "exp", None),
            P(("ctx", "exp"), None),
        ),
        out_specs=P(("ctx", "exp"), None),
        check_vma=False,
    )
```

```python
import functools
import math

import jax
import jax.numpy as jnp
from jax import lax
from jax.experimental import pallas as pl
from jax.experimental.pallas import tpu as pltpu
from jax.sharding import PartitionSpec as P

D = 1024
HD = 64
EPSILON = 1e-05
LOWEST = -1e30
ALPHA = math.log2(math.e) / math.sqrt(HD)
BF = jnp.bfloat16
F32 = jnp.float32
MESH = pl.DeviceIdType.MESH
VMEM = pltpu.VMEM


def whole():
    return pl.BlockSpec(memory_space=pltpu.VMEM)


def anywhere():
    return pl.BlockSpec(memory_space=pl.ANY)


def shifted(i, sign, ctx, exp):
    o = (i * 27) % 64
    ylo, x, z, yhi = ctx // 16, (ctx // 4) % 4, ctx % 4, exp // 2
    to_x = (x + 4 + sign * (o % 4)) % 4
    to_y = (yhi * 2 + ylo + 4 + sign * ((o // 4) % 4)) % 4
    to_z = (z + 4 + sign * (o // 16)) % 4
    to_ctx = (to_y % 2) * 16 + to_x * 4 + to_z
    return to_ctx, (to_y // 2) * 2 + exp % 2


def layer_kernel(
    hit_hbm,
    gain_attn_ref,
    wq_hbm,
    wk_hbm,
    wv_hbm,
    wo_ref,
    gain_ref,
    wr_ref,
    routes_ref,
    gate_ref,
    up_ref,
    down_ref,
    out_ref,
    x_ref,
    wq_ref,
    wk_ref,
    wv_ref,
    qt_ref,
    kp_ref,
    vt_ref,
    qg,
    kg,
    vg,
    q2,
    s_ref,
    acc,
    mx,
    ls,
    ost,
    at_ref,
    wo_all,
    wg,
    wu,
    wd,
    rows_out,
    got,
    stage,
    back,
    table_ref,
    res_ref,
    normed_ref,
    load,
    x_send,
    x_recv,
    ring_send,
    ring_recv,
    sib_send,
    sib_recv,
    o_send,
    o_recv,
    w_send,
    w_recv,
    w_own,
    e_send,
    e_recv,
    w_sem,
    send,
    recv,
    b_send,
    b_recv,
    known,
):
    ctx = lax.axis_index("ctx")
    exp = lax.axis_index("exp")
    ylo = ctx // 16
    x = (ctx // 4) % 4
    z = ctx % 4
    yhi = exp // 2
    core = exp % 2
    mine = ylo * 4 + z

    def device(to_ylo, to_x, to_z, to_yhi, to_core):
        return (to_ylo * 16 + to_x * 4 + to_z, to_yhi * 2 + to_core)

    right = device(ylo, (x + 1) % 4, z, yhi, core)
    left = device(ylo, (x + 3) % 4, z, yhi, core)
    sibling = device(ylo, x, z, yhi, 1 - core)

    barrier = pltpu.get_barrier_semaphore()

    def greet(i, carry):
        @pl.when(i != mine * 2 + core)
        def _():
            to = device(i // 8, x, (i // 2) % 4, yhi, i % 2)
            pl.semaphore_signal(barrier, inc=1, device_id=to, device_id_type=MESH)

        return carry

    far_chip = device(ylo, x, z, 1 - yhi, core)

    def tell(sem, *others):
        for to in others:
            pl.semaphore_signal(sem, inc=1, device_id=to, device_id_type=MESH)

    loads = [
        pltpu.make_async_copy(src, dst, load.at[m])
        for m, (src, dst) in enumerate(
            ((hit_hbm, x_ref), (wq_hbm, wq_ref), (wk_hbm, wk_ref), (wv_hbm, wv_ref))
        )
    ]
    for copy in loads:
        copy.start()
    lax.fori_loop(0, 16, greet, 0)
    tell(barrier, left, right, far_chip)

    for copy in loads[:2]:
        copy.wait()
    xs = x_ref[...].astype(F32)
    inv = lax.rsqrt(jnp.mean(xs * xs, axis=-1, keepdims=True) + EPSILON)
    n = (xs * inv * gain_attn_ref[...]).astype(BF)
    qt = jnp.dot(n, wq_ref[...], preferred_element_type=F32).T.astype(BF)
    for head in range(4):
        for block in range(4):
            qt_ref[block % 2, head, :, (block // 2) * 128 : (block // 2) * 128 + 128] = qt[
                head * HD : head * HD + HD, block * 128 : block * 128 + 128
            ]
    loads[2].wait()
    k = jnp.dot(n, wk_ref[...], preferred_element_type=F32)
    for head in range(4):
        for half in range(2):
            kh = k[half * 256 : half * 256 + 256, head * HD : head * HD + HD]
            kp_ref[head, half] = jnp.concatenate([kh[0:128], kh[128:256]], axis=1).astype(BF)
    loads[3].wait()
    vt = jnp.dot(n, wv_ref[...], preferred_element_type=F32).T.astype(BF)
    for head in range(4):
        for half in range(2):
            for u in range(2):
                at = half * 256 + u * 128
                vt_ref[head, half, u] = vt[head * HD : head * HD + HD, at : at + 128]

    pl.semaphore_wait(barrier, 18)
    tell(known.at[0], far_chip)

    def head_copies(i):
        head, half = (z + 1 + i // 2) % 4, i % 2
        at = pl.ds(pl.multiple_of(mine * 128, 128), 128)
        parts = (
            (qt_ref.at[half, head], qg.at[half * 4 + z], half * 4 + z, ylo),
            (kp_ref.at[head, half], kg.at[0, half, at, :], mine, half),
            (vt_ref.at[head, half], vg.at[0, half, :, :, at], mine, half),
        )
        here = (core == ylo) & (head == z)
        own = [here, here & (half == core), here & (half == core)]
        away = [
            pltpu.make_async_remote_copy(
                src_ref=src,
                dst_ref=dst,
                send_sem=x_send.at[n, i],
                recv_sem=x_recv.at[n, at_sem],
                device_id=device(core, x, head, yhi, to_core),
                device_id_type=MESH,
            )
            for n, (src, dst, at_sem, to_core) in enumerate(parts)
        ]
        local = [
            pltpu.make_async_copy(src, dst, x_recv.at[n, at_sem])
            for n, (src, dst, at_sem, to_core) in enumerate(parts)
        ]
        return own, away, local

    def send_heads(i, carry):
        for own, away, local in zip(*head_copies(i)):

            @pl.when(own)
            def _(local=local):
                local.start()

            @pl.when(jnp.logical_not(own))
            def _(away=away):
                away.start()

        return carry

    lax.fori_loop(0, 8, send_heads, 0)

    pl.semaphore_wait(known.at[0], 1)
    tell(known.at[1], left, right)

    rows = at_ref.shape[2]
    experts, cap = rows_out.shape[0], rows_out.shape[1]
    places = experts * cap
    ids = lax.broadcasted_iota(jnp.int32, (experts, rows), 0)
    picks = (routes_ref[0:1, :] == ids) | (routes_ref[1:2, :] == ids)
    marks = jnp.where(picks, 1.0, 0.0).astype(BF)
    before = lax.broadcasted_iota(jnp.int32, (rows, rows), 0) < lax.broadcasted_iota(
        jnp.int32, (rows, rows), 1
    )
    slots = jnp.dot(
        marks, jnp.where(before, 1.0, 0.0).astype(BF), preferred_element_type=F32
    ).astype(BF)
    spread = jnp.where(
        lax.broadcasted_iota(jnp.int32, (places, experts), 0) // cap
        == lax.broadcasted_iota(jnp.int32, (places, experts), 1),
        1.0,
        0.0,
    ).astype(BF)
    wide = lambda v: jnp.dot(spread, v, preferred_element_type=F32)
    order = (lax.broadcasted_iota(jnp.int32, (places, rows), 0) % cap).astype(F32)
    here = (wide(marks) > 0.5) & (wide(slots) == order)
    table_ref[...] = jnp.where(here, 1.0, 0.0).astype(BF)
    pl.semaphore_wait(known.at[1], 2)
    tell(known.at[2], left, right)

    def await_heads(j, carry):
        pltpu.make_async_copy(qg.at[j], qg.at[j], x_recv.at[0, j]).wait()
        at = pl.ds(pl.multiple_of(j * 128, 128), 128)
        kd = kg.at[0, core, at, :]
        pltpu.make_async_copy(kd, kd, x_recv.at[1, j]).wait()
        vd = vg.at[0, core, :, :, at]
        pltpu.make_async_copy(vd, vd, x_recv.at[2, j]).wait()
        return carry

    lax.fori_loop(0, 8, await_heads, 0)
    pl.semaphore_wait(known.at[2], 2)

    def remote(src, dst, send, recv, to):
        return pltpu.make_async_remote_copy(
            src_ref=src,
            dst_ref=dst,
            send_sem=send,
            recv_sem=recv,
            device_id=to,
            device_id_type=MESH,
        )

    def to_sibling(slot):
        return [
            remote(g.at[slot, core], g.at[slot, core], sib_send.at[n, slot], sib_recv.at[n, slot], sibling)
            for n, g in enumerate((kg, vg))
        ]

    def from_sibling(slot):
        return [
            remote(g.at[slot, 1 - core], g.at[slot, 1 - core], sib_send.at[n, slot], sib_recv.at[n, slot], sibling)
            for n, g in enumerate((kg, vg))
        ]

    k_right = remote(kg.at[0, core], kg.at[1, core], ring_send.at[0, 0], ring_recv.at[0, 0], right)
    v_right = remote(vg.at[0, core], vg.at[1, core], ring_send.at[1, 0], ring_recv.at[1, 0], right)
    k_left = remote(kg.at[0, core], kg.at[2, core], ring_send.at[0, 1], ring_recv.at[0, 1], left)
    v_left = remote(vg.at[0, core], vg.at[2, core], ring_send.at[1, 1], ring_recv.at[1, 1], left)
    k_on = remote(kg.at[1, core], kg.at[3, core], ring_send.at[0, 2], ring_recv.at[0, 2], right)
    v_on = remote(vg.at[2, core], vg.at[3, core], ring_send.at[1, 2], ring_recv.at[1, 2], left)
    for copy in (k_right, k_left, v_right, v_left):
        copy.start()
    for copy in to_sibling(0):
        copy.start()

    far_exp = (exp + 2) % 4
    w_local = pltpu.make_async_copy(wo_ref, wo_all.at[exp], w_own)
    w_across = remote(wo_ref, wo_all.at[exp], w_send.at[0], w_recv.at[0], far_chip)
    w_beside = remote(wo_ref, wo_all.at[exp], w_send.at[1], w_recv.at[1], sibling)
    w_on = remote(
        wo_all.at[far_exp], wo_all.at[far_exp], w_send.at[2], w_recv.at[2], sibling
    )
    w_across.start()
    w_beside.start()
    w_local.start()
    e_beside = [
        remote(src, dst, e_send.at[n], e_recv.at[n], sibling)
        for n, (src, dst) in enumerate(
            ((gate_ref, wg.at[1]), (up_ref, wu.at[1]), (down_ref, wd.at[1]))
        )
    ]
    weight_loads = [
        pltpu.make_async_copy(src, dst.at[0], w_sem.at[n])
        for n, (src, dst) in enumerate(((gate_ref, wg), (up_ref, wu), (down_ref, wd)))
    ]
    for copy in weight_loads:
        copy.start()
    for copy in e_beside:
        copy.start()

    zero = jnp.zeros((HD, 256), BF)
    for j in range(8):
        q2[j, 0, 0:HD] = qg[j]
        q2[j, 0, HD : 2 * HD] = zero
        q2[j, 1, 0:HD] = zero
        q2[j, 1, HD : 2 * HD] = qg[j]
    acc[...] = jnp.zeros_like(acc)
    mx[...] = jnp.full_like(mx, LOWEST)
    ls[...] = jnp.zeros_like(ls)

    def score(phase, tile, p):
        j = (tile // 4) * 4 + (tile + z) % 4
        keys = kg[phase // 2, (phase + core) % 2]
        for u in range(2):
            s_ref[p, u] = lax.dot_general(
                keys, q2[j, u], (((1,), (0,)), ((), ())), preferred_element_type=F32
            )

    def absorb(phase, tile, p):
        j = (tile // 4) * 4 + (tile + z) % 4
        s0 = s_ref[p, 0]
        s1 = s_ref[p, 1]
        old = mx[j]
        new = jnp.maximum(
            old,
            jnp.maximum(jnp.max(s0, axis=0, keepdims=True), jnp.max(s1, axis=0, keepdims=True)),
        )
        fade = jnp.exp2((old - new) * ALPHA)
        e0 = jnp.exp2((s0 - new) * ALPHA)
        e1 = jnp.exp2((s1 - new) * ALPHA)
        slot, half = phase // 2, (phase + core) % 2
        ls[j] = ls[j] * fade + (
            jnp.sum(e0, axis=0, keepdims=True) + jnp.sum(e1, axis=0, keepdims=True)
        )
        acc[j] = acc[j] * fade + (
            jnp.dot(vg[slot, half, 0], e0.astype(BF), preferred_element_type=F32)
            + jnp.dot(vg[slot, half, 1], e1.astype(BF), preferred_element_type=F32)
        )
        mx[j] = new

    head = yhi * 8 + mine

    def out_copy(i):
        j, to_yhi = i % 8, i // 8
        to = device(core, x, j % 4, to_yhi, j // 4)
        own = (core == ylo) & (j % 4 == z) & (to_yhi == yhi) & (j // 4 == core)
        return (
            own,
            remote(ost.at[j, to_yhi], at_ref.at[head], o_send.at[i], o_recv.at[head], to),
            pltpu.make_async_copy(ost.at[j, to_yhi], at_ref.at[head], o_recv.at[head]),
        )

    def send_out(tile):
        j = (tile // 4) * 4 + (tile + z) % 4
        o = (acc[j] / ls[j]).astype(BF)
        ost[j, 0] = o[:, 0:128]
        ost[j, 1] = o[:, 128:256]
        for to_yhi in range(2):
            i = to_yhi * 8 + j
            own, away, local = out_copy(i)

            @pl.when(own)
            def _(local=local):
                local.start()

            @pl.when(jnp.logical_not(own))
            def _(away=away):
                away.start()

    score(0, 0, 0)

    def pair(n):
        return pl.ds(pl.multiple_of(2 * n, 2), 2)

    def row_copy(i):
        to = shifted(i, 1, ctx, exp)
        return pltpu.make_async_remote_copy(
            src_ref=rows_out.at[pair(to[0])],
            dst_ref=got.at[i],
            send_sem=send.at[i],
            recv_sem=recv.at[i],
            device_id=to,
            device_id_type=MESH,
        )

    def back_copy(i):
        return pltpu.make_async_remote_copy(
            src_ref=stage.at[i],
            dst_ref=back.at[yhi, pair(ctx)],
            send_sem=b_send.at[i],
            recv_sem=b_recv.at[i],
            device_id=shifted(i, -1, ctx, exp),
            device_id_type=MESH,
        )

    def route_rows():
        def await_out(i, carry):
            pltpu.make_async_copy(at_ref.at[i], at_ref.at[i], o_recv.at[i]).wait()
            return carry

        lax.fori_loop(0, 16, await_out, 0)
        w_local.wait()
        w_beside.wait_recv()
        w_on.wait_recv()
        mixed = lax.dot_general(
            at_ref[...].reshape(D, rows),
            wo_all[...].reshape(D, D),
            (((0,), (0,)), ((), ())),
            preferred_element_type=F32,
        )
        own_rows = x_ref[pl.ds(pl.multiple_of(exp * rows, rows), rows), :]
        residual = own_rows.astype(F32) + mixed
        inv = lax.rsqrt(jnp.mean(residual * residual, axis=-1, keepdims=True) + EPSILON)
        res_ref[...] = residual
        normed = (residual * inv * gain_ref[...]).astype(BF)
        normed_ref[...] = normed
        picked = jnp.dot(table_ref[...], normed, preferred_element_type=F32)
        rows_out[...] = picked.reshape(rows_out.shape).astype(BF)
        pltpu.make_async_copy(rows_out.at[pair(ctx)], got.at[0], recv.at[0]).start()

        def send_rows(i, carry):
            row_copy(i).start()
            return carry

        lax.fori_loop(1, 64, send_rows, 0)

    def step_of(g):
        late = jnp.minimum(g // 8, 1)
        k = jnp.maximum(g - 8, 0)
        phase = (1 - late) * (g // 4) + late * (2 + (k % 12) // 2)
        pair = (1 - late) * (g % 4) + late * ((k // 12) * 2 + k % 2)
        return phase, pair

    def turn(g, carry):
        phase, pair = step_of(g)

        for slot, at in ((0, 3), (1, 9), (2, 13), (3, 17)):

            @pl.when(g == at)
            def _(slot=slot):
                for copy in from_sibling(slot):
                    copy.wait_recv()

        @pl.when(g == 7)
        def _():
            for copy in (k_right, k_left, v_right, v_left):
                copy.wait_recv()
            k_on.start()
            v_on.start()
            for slot in (1, 2):
                for copy in to_sibling(slot):
                    copy.start()

        @pl.when(g == 15)
        def _():
            k_on.wait_recv()
            v_on.wait_recv()
            for copy in to_sibling(3):
                copy.start()
            w_across.wait_recv()
            w_on.start()

        @pl.when((g == 23) & (core == 0))
        def _():
            route_rows()

        score(phase, 2 * pair + 1, 1)
        absorb(phase, 2 * pair, 0)
        later = jnp.minimum(g + 1, 31)
        next_phase, next_pair = step_of(later)
        score(next_phase, 2 * next_pair, 0)
        absorb(phase, 2 * pair + 1, 1)

        @pl.when(phase == 7)
        def _():
            send_out(2 * pair)
            send_out(2 * pair + 1)

        return carry

    lax.fori_loop(0, 32, turn, 0)

    @pl.when(core == 1)
    def _():
        route_rows()


    normed = normed_ref[...]
    here = table_ref[...].astype(F32) > 0.5
    logits = lax.dot_general(
        wr_ref[...], normed, (((1,), (1,)), ((), ())), preferred_element_type=F32
    )
    top = jnp.max(jnp.where(picks, logits, -jnp.inf), axis=0, keepdims=True)
    weights = jnp.where(picks, jnp.exp(jnp.where(picks, logits - top, 0.0)), 0.0)
    gates = weights / jnp.sum(weights, axis=0, keepdims=True)
    gate_hi = gates.astype(BF)
    gate_lo = (gates - gate_hi.astype(F32)).astype(BF)
    hi = jnp.where(here, wide(gate_hi), 0.0).T.astype(BF)
    lo = jnp.where(here, wide(gate_lo), 0.0).T.astype(BF)
    hi_lo = jnp.concatenate([hi, lo], axis=0)
    for copy in weight_loads:
        copy.wait()
    for copy in e_beside:
        copy.wait_recv()

    group = 32

    def serve(g, carry):
        first = g * group

        def await_rows(i, carry):
            pltpu.make_async_copy(got.at[first + i], got.at[first + i], recv.at[first + i]).wait()
            return carry

        lax.fori_loop(0, group, await_rows, 0)
        at = pl.ds(pl.multiple_of(first, group), group)

        def expert(j, carry):
            mine = got[at, j].astype(F32).reshape(group * cap, D).astype(BF)
            total = None
            for q in range(2):
                gate = jnp.dot(mine, wg[q, j], preferred_element_type=F32)
                up = jnp.dot(mine, wu[q, j], preferred_element_type=F32)
                hidden = (gate / (1.0 + jnp.exp(-gate)) * up).astype(BF)
                part = jnp.dot(hidden, wd[q, j], preferred_element_type=F32)
                total = part if total is None else total + part
            stage[at, j] = total.reshape(group, cap, D).astype(BF)
            return carry

        lax.fori_loop(0, 2, expert, 0)

        @pl.when(first == 0)
        def _():
            pltpu.make_async_copy(stage.at[0], back.at[yhi, pair(ctx)], b_recv.at[0]).start()

        def send_back(i, carry):
            @pl.when(first + i > 0)
            def _():
                back_copy(first + i).start()

            return carry

        lax.fori_loop(0, group, send_back, 0)
        return carry

    lax.fori_loop(0, 2, serve, 0)

    def await_back(i, carry):
        from_ctx, from_exp = shifted(i, 1, ctx, exp)
        block = back.at[from_exp // 2, pair(from_ctx)]
        pltpu.make_async_copy(block, block, b_recv.at[i]).wait()
        return carry

    lax.fori_loop(0, 64, await_back, 0)
    total = res_ref[...]
    for n in range(2):
        served = back[n].astype(F32).reshape(places, D).astype(BF)
        both = jnp.dot(hi_lo, served, preferred_element_type=F32)
        total = total + (both[:rows] + both[rows:])
    out_ref[...] = total.astype(BF)

    def sent(i, carry):
        row_copy(i).wait_send()
        back_copy(i).wait_send()
        return carry

    lax.fori_loop(1, 64, sent, 0)

    def sent_heads(i, carry):
        for own, away, _ in zip(*head_copies(i)):

            @pl.when(jnp.logical_not(own))
            def _(away=away):
                away.wait_send()

        return carry

    lax.fori_loop(0, 8, sent_heads, 0)

    def sent_out(i, carry):
        own, away, local = out_copy(i)

        @pl.when(jnp.logical_not(own))
        def _():
            away.wait_send()

        return carry

    lax.fori_loop(0, 16, sent_out, 0)
    for copy in (k_right, k_left, v_right, v_left, k_on, v_on):
        copy.wait_send()
    for slot in range(4):
        for copy in to_sibling(slot):
            copy.wait_send()
    for copy in (w_across, w_beside, w_on):
        copy.wait_send()
    for copy in e_beside:
        copy.wait_send()


def layer(hit, gain_attn, wq, wk, wv, wo, gain, wr, w_gate, w_up, w_down, routes):
    experts = wr.shape[1]
    rows = routes.shape[0]
    cap = 8
    dma = pltpu.SemaphoreType.DMA
    return pl.pallas_call(
        layer_kernel,
        out_shape=jax.ShapeDtypeStruct((rows, D), BF),
        in_specs=[
            anywhere(),
            whole(),
            anywhere(),
            anywhere(),
            anywhere(),
            anywhere(),
            whole(),
            whole(),
            whole(),
            anywhere(),
            anywhere(),
            anywhere(),
        ],
        out_specs=whole(),
        scratch_shapes=[
            VMEM(hit.shape, BF),
            VMEM(wq.shape, BF),
            VMEM(wk.shape, BF),
            VMEM(wv.shape, BF),
            VMEM((2, 4, HD, 256), BF),
            VMEM((4, 2, 128, 128), BF),
            VMEM((4, 2, 2, HD, 128), BF),
            VMEM((8, HD, 256), BF),
            VMEM((4, 2, 1024, 128), BF),
            VMEM((4, 2, 2, HD, 1024), BF),
            VMEM((8, 2, 128, 256), BF),
            VMEM((2, 2, 1024, 256), F32),
            VMEM((8, HD, 256), F32),
            VMEM((8, 1, 256), F32),
            VMEM((8, 1, 256), F32),
            VMEM((8, 2, HD, 128), BF),
            VMEM((16, HD, 128), BF),
            VMEM((4,) + wo.shape, BF),
            VMEM((2,) + w_gate.shape, BF),
            VMEM((2,) + w_up.shape, BF),
            VMEM((2,) + w_down.shape, BF),
            VMEM((experts, cap, D), BF),
            VMEM((64, 2, cap, D), BF),
            VMEM((64, 2, cap, D), BF),
            VMEM((2, experts, cap, D), BF),
            VMEM((experts * cap, rows), BF),
            VMEM((rows, D), F32),
            VMEM((rows, D), BF),
            dma((4,)),
            dma((3, 8)),
            dma((3, 8)),
            dma((2, 3)),
            dma((2, 3)),
            dma((2, 4)),
            dma((2, 4)),
            dma((16,)),
            dma((16,)),
            dma((3,)),
            dma((3,)),
            dma,
            dma((3,)),
            dma((3,)),
            dma((3,)),
            dma((64,)),
            dma((64,)),
            dma((64,)),
            dma((64,)),
            pltpu.SemaphoreType.REGULAR((3,)),
        ],
        compiler_params=pltpu.CompilerParams(
            collective_id=0, has_side_effects=True, vmem_limit_bytes=60 << 20
        ),
        name="layer",
    )(
        hit,
        gain_attn.reshape(1, D),
        wq,
        wk,
        wv,
        wo,
        gain.reshape(1, D),
        wr.T,
        routes.T,
        w_gate,
        w_up,
        w_down,
    )


def solution(mesh):
    return jax.shard_map(
        layer,
        mesh=mesh,
        in_specs=(
            P("ctx", None),
            P(),
            P(None, "exp"),
            P(None, "exp"),
            P(None, "exp"),
            P("exp", None),
            P(),
            P(),
            P("ctx", None, "exp"),
            P("ctx", None, "exp"),
            P("ctx", "exp", None),
            P(("ctx", "exp"), None),
        ),
        out_specs=P(("ctx", "exp"), None),
        check_vma=False,
    )
```
